512 devices in a mesh: dom: 128 (over y, z, core), sub: 4 (over x).
Axes of the slice: x: 4, y: 4, z: 16, core: 2. Of those that a mesh axis runs over, the one named last changes fastest.
Arguments:
- segments: float32 [1024, 9, 128], P(('dom', 'sub')), may hold values from -6 to 6
- stress: float32 [3, 3], replicated, may hold values from -3 to 3
- drag_coef: float32 [1024, 128], P(('dom', 'sub')), may hold values from 0.5 to 4
- send_ids: int32 [512, 128, 1], P(('dom', 'sub')), may hold values from -1 to 1, as said below
- partner_ids: int32 [512, 128, 1], P(('dom', 'sub')), may hold values from 0 to 1
Outputs:
- positions: float32 [1024, 3, 128], P(('dom', 'sub'))
- velocity: float32 [1024, 3, 128], P(('dom', 'sub'))
The draws below stay inside these ranges and needn't reach their ends.
Inputs may be any that keep to these rules, and one draw needn't show every extreme that they name: `send_ids`: entry [d, p, s] names a block of device d, which goes in slot s to the device with dom index p and d's sub index; -1 marks an empty slot. Some device receives a block in every slot from every sender.
All inputs are finite; a program needn't handle non-finite values.
Results may differ from the reference program's by a relative error of at most 0.0003.
Values sent between devices are 32-bit elements; how exact they have to be, the bound alone decides.
No kernel may reach another device: no remote copies, remote signals or barrier semaphores. Data moves between devices by JAX's collectives and lax.ppermute only.
A program may use at most 64 MiB of HBM per device.

```python
import math
import jax
import jax.numpy as jnp
from jax import lax

BLK = 128
NB_DEV = 2
SLOTS = 1
STEPS = 2
NBLOCKS = 1024
N_DOM = 128
N_SUB = 4


def draw_send_ids(key, part):
    subkeys = jax.random.split(key, 4)
    device_count = N_DOM * N_SUB
    levels = jax.random.randint(subkeys[0], (device_count,), 1, 5)
    hottest = jax.random.randint(subkeys[1], (), 0, device_count)
    levels = jnp.where(jnp.arange(device_count, dtype=jnp.int32) == hottest, 8, levels)
    sender = jnp.arange(device_count, dtype=jnp.int32)[:, None, None]
    peer_index = jnp.arange(N_DOM, dtype=jnp.int32)[None, :, None]
    receiver = peer_index * N_SUB + sender % N_SUB
    receiver = jnp.broadcast_to(receiver, (device_count, N_DOM, SLOTS))
    rolled = jax.random.randint(subkeys[2], (device_count, N_DOM, SLOTS), 0, 8)
    filled = rolled < levels[receiver]
    block_ids = jax.random.randint(subkeys[3], (device_count, N_DOM, SLOTS), 0, NB_DEV)
    return jnp.where(filled, block_ids, -1).astype(jnp.int32)


def place_ends(entries, stream_key, smallest, largest):
    place = [jax.random.randint(jax.random.fold_in(stream_key, axis), (), 0, length) for axis, length in enumerate(entries.shape)]
    longest = entries.shape.index(max(entries.shape))
    next_to = place[:longest] + [(place[longest] + 1) % entries.shape[longest]] + place[longest + 1:]
    return entries.at[tuple(place)].set(smallest).at[tuple(next_to)].set(largest)


def block_scale(stream_key, extent, cuts, low, largest):
    def one(dim, blocks):
        draws = jax.random.uniform(jax.random.fold_in(jax.random.fold_in(stream_key, 6), dim), (blocks,), jnp.float32, low / len(cuts), largest / len(cuts))
        return jnp.repeat(jnp.exp(draws), extent[dim] // blocks).reshape((-1,) + (1,) * (len(extent) - dim - 1))

    gain = one(*cuts[0])
    for cut in cuts[1:]:
        gain = gain * one(*cut)
    return gain


def bell_draw(stream_key, shape, spread, limit, cuts=(), kind=jnp.bfloat16):
    result = spread * jax.random.normal(stream_key, shape, jnp.float32)
    if cuts:
        result = result * block_scale(stream_key, shape, cuts, -0.22, 0.18)
    return jnp.clip(result, -limit, limit).astype(kind)


def setup_inputs(seed: int = 0) -> dict:
    key_of = jax.random.split(jax.random.key(seed), 6)
    return {
        "segments": bell_draw(key_of[0], (NBLOCKS, 9, BLK), 1.0, 6.0, ((0, 512),), jnp.float32),
        "stress": bell_draw(key_of[1], (3, 3), 0.5, 3.0, (), jnp.float32),
        "drag_coef": jnp.clip(jnp.exp(math.log(4.0) - 2.0794415 * jax.random.uniform(key_of[2], (NBLOCKS, BLK), jnp.float32) ** block_scale(key_of[2], (NBLOCKS, BLK), ((0, 512),), -0.2, 0.2)), 0.5, 4.0),
        "send_ids": draw_send_ids(jax.random.fold_in(key_of[5], 71), 0),
        "partner_ids": place_ends(jax.random.randint(key_of[4], (N_DOM * N_SUB, N_DOM, SLOTS), 0, NB_DEV), jax.random.fold_in(key_of[4], 1), 0, NB_DEV - 1).astype(jnp.int32),
    }


COUPLE = 0.0625
CORE_SQUARE = 0.5
TENSION = 0.25
STEP_LENGTH = 1.0
EPSILON = 1e-06

def pair_terms(target, source):
    offsets = [target[..., component, :][..., :, None] - source[..., component, :][..., None, :] for component in range(3)]
    distance_sq = CORE_SQUARE + offsets[0] * offsets[0] + offsets[1] * offsets[1] + offsets[2] * offsets[2]
    inverse = lax.rsqrt(distance_sq)
    burgers_dot = target[..., 6, :][..., :, None] * source[..., 6, :][..., None, :]
    burgers_dot = burgers_dot + target[..., 7, :][..., :, None] * source[..., 7, :][..., None, :]
    burgers_dot = burgers_dot + target[..., 8, :][..., :, None] * source[..., 8, :][..., None, :]
    lines_dot = target[..., 3, :][..., :, None] * source[..., 3, :][..., None, :]
    lines_dot = lines_dot + target[..., 4, :][..., :, None] * source[..., 4, :][..., None, :]
    lines_dot = lines_dot + target[..., 5, :][..., :, None] * source[..., 5, :][..., None, :]
    weights = burgers_dot * lines_dot * inverse * inverse * inverse
    return (weights, offsets)

def force_on_target(weights, offsets):
    return jnp.stack([lax.optimization_barrier(jnp.sum(weights * offset_c, axis=-1)) for offset_c in offsets], axis=-2)

def force_on_source(weights, offsets):
    return jnp.stack([-lax.optimization_barrier(jnp.sum(weights * offset_c, axis=-2)) for offset_c in offsets], axis=-2)

def external_force(stress, line_vec, burgers):
    pulled = [stress[component, 0] * burgers[:, 0] + stress[component, 1] * burgers[:, 1] + stress[component, 2] * burgers[:, 2] for component in range(3)]
    first = pulled[1] * line_vec[:, 2] - pulled[2] * line_vec[:, 1]
    second = pulled[2] * line_vec[:, 0] - pulled[0] * line_vec[:, 2]
    third = pulled[0] * line_vec[:, 1] - pulled[1] * line_vec[:, 0]
    return jnp.stack([first, second, third], axis=1)

def chain_term(position):
    left_side = jnp.concatenate([position[..., :1], position[..., :-1]], axis=-1)
    right_side = jnp.concatenate([position[..., 1:], position[..., -1:]], axis=-1)
    return left_side + right_side - 2.0 * position

def group_forces(seg_state):
    group_blocks = N_SUB * NB_DEV
    grouped = seg_state.reshape(N_DOM, group_blocks, 9, BLK)

    def one_group(blocks):
        target = blocks.transpose(1, 0, 2).reshape(9, group_blocks * BLK)

        def add_block(running, source):
            weights, offsets = pair_terms(target, source)
            return (running + force_on_target(weights, offsets), None)
        running = lax.scan(add_block, jnp.zeros((3, group_blocks * BLK), jnp.float32), blocks)[0]
        return running.reshape(3, group_blocks, BLK).transpose(1, 0, 2)
    return lax.map(one_group, grouped).reshape(N_DOM * group_blocks, 3, BLK)

def cross_forces(seg_state, is_valid, source_block, target_block):
    pair_count = is_valid.shape[0]
    batch_size = math.gcd(pair_count, 64)
    source_ids = source_block.reshape(-1, batch_size)
    target_ids = target_block.reshape(-1, batch_size)
    keep_flags = is_valid.reshape(-1, batch_size)

    def one_batch(accum_force, pieces):
        src_rows, tgt_rows, keep_rows = pieces
        source = jnp.where(keep_rows[:, None, None], seg_state[src_rows], 0.0)
        target = seg_state[tgt_rows]
        weights, offsets = pair_terms(target, source)
        accum_force = accum_force.at[tgt_rows].add(force_on_target(weights, offsets))
        accum_force = accum_force.at[src_rows].add(force_on_source(weights, offsets))
        return (accum_force, None)
    start_force = jnp.zeros((seg_state.shape[0], 3, BLK), jnp.float32)
    return lax.scan(one_batch, start_force, (source_ids, target_ids, keep_flags))[0]

def reference(segments, stress, drag_coef, send_ids, partner_ids):
    position = segments[:, 0:3]
    line_vec = segments[:, 3:6]
    burgers = segments[:, 6:9]
    applied = external_force(stress, line_vec, burgers)
    device_count = N_DOM * N_SUB
    sender = jnp.arange(device_count, dtype=jnp.int32)[:, None, None]
    peer_index = jnp.arange(N_DOM, dtype=jnp.int32)[None, :, None]
    receiver = peer_index * N_SUB + sender % N_SUB
    is_valid = (send_ids >= 0).reshape(-1)
    source_block = (sender * NB_DEV + jnp.maximum(send_ids, 0)).astype(jnp.int32).reshape(-1)
    target_block = (receiver * NB_DEV + partner_ids).astype(jnp.int32).reshape(-1)
    velocity = jnp.zeros_like(position)
    for step_index in range(STEPS):
        seg_state = jnp.concatenate([position, line_vec, burgers], axis=1)
        grouped = group_forces(seg_state)
        crossed = cross_forces(seg_state, is_valid, source_block, target_block)
        force = COUPLE * (grouped + crossed) + applied + TENSION * chain_term(position)
        velocity = force / drag_coef[:, None, :]
        speed_sq = lax.optimization_barrier(jnp.sum(velocity * velocity, axis=1))
        time_step = STEP_LENGTH / (jnp.sqrt(jnp.max(speed_sq)) + EPSILON)
        position = position + time_step * velocity
    return (position, velocity)
```

```python
import functools

import jax
import jax.numpy as jnp
from jax import lax
from jax.experimental import pallas as pl
from jax.experimental.pallas import tpu as pltpu
from jax.sharding import Mesh
from jax.sharding import PartitionSpec as P

NY, NZ, NC = 4, 16, 2
DOM = ("y", "z", "c")
DOM_SUB = ("y", "z", "c", "x")

COUPLE = 0.0625
CORE_SQUARE = 0.5
TENSION = 0.25
STEP_LENGTH = 1.0
EPSILON = 1e-06

SEG = 128
NDEV = NY * NZ
BATCH = 8
LIST = 192
F32 = jnp.float32
BF16 = jnp.bfloat16


def sublane(shape=(8, SEG)):
    return lax.broadcasted_iota(jnp.int32, shape, len(shape) - 2)


def up(value, count):
    return jnp.concatenate([value[count:], value[:count]], axis=0)


def split2(value):
    high = value.astype(BF16).astype(F32)
    return high, value - high


def split3(value):
    high, rest = split2(value)
    mid, low = split2(rest)
    return high, mid, low


def source_operands(x_tile, l_tile, b_tile):
    row = sublane()
    x_tile = jnp.where(row < 6, x_tile, 0.0)
    square = x_tile * x_tile
    norm0 = square[0:1] + square[1:2] + square[2:3] + CORE_SQUARE
    norm1 = square[3:4] + square[4:5] + square[5:6] + CORE_SQUARE
    full = jnp.where(row == 6, norm0, jnp.where(row == 7, norm1, x_tile))
    high, mid, low = split3(full)
    one = jnp.ones_like(high)
    zero = jnp.zeros_like(high)
    dist = [high, mid, high, mid, low, high, one, zero]
    prod = [jnp.where(row < 3, b_tile[a : a + 1], b_tile[3 + a : 4 + a]) * l_tile for a in range(3)]
    parts = [split2(p) for p in prod]
    highs = [p[0] for p in parts]
    mids = [p[1] for p in parts]
    weight = highs + highs + mids + [zero]
    flag = jnp.where(row == 6, 1.0, 0.0)
    first = jnp.where(row < 6, high, flag)
    second = jnp.where(row < 6, mid, 0.0)
    first_up = jnp.where(row < 3, up(high, 3), flag)
    second_up = jnp.where(row < 3, up(mid, 3), 0.0)
    return dist, weight, (first, second), (first_up, second_up)


def store_rows(ref, index, tiles):
    for at in range(0, len(tiles), 2):
        pair = jnp.concatenate([tiles[at], tiles[at + 1]], axis=0).astype(BF16)
        ref[index, 8 * at : 8 * at + 16, :] = pair


def target_rows(x_tile, l_tile, b_tile, block):
    row = sublane()

    def both(tile):
        if block == 0:
            return jnp.where(row < 3, tile, jnp.where(row < 6, up(tile, 5), 0.0))
        return jnp.where(row < 3, up(tile, 3), jnp.where(row < 6, tile, 0.0))

    x_both = both(x_tile)
    high, mid, low = split3(x_both)
    square = x_both * x_both
    norm = square[0:1] + square[1:2] + square[2:3]
    norm_h, norm_m, norm_l = split3(norm)
    unit = jnp.where(row >= 6, 1.0, 0.0)
    norms = jnp.where(
        row == 0, norm_h, jnp.where(row == 1, norm_m, jnp.where(row == 2, norm_l, 0.0))
    )
    zero = jnp.zeros_like(high)
    dist = [
        -2.0 * high + unit,
        -2.0 * high + unit,
        -2.0 * mid,
        -2.0 * mid,
        -2.0 * high + unit,
        -2.0 * low,
        norms,
    ]
    l_both = both(l_tile)
    base = 3 * block
    prod = [b_tile[base + a : base + a + 1] * l_both for a in range(3)]
    parts = [split2(p) for p in prod]
    highs = [p[0] for p in parts]
    mids = [p[1] for p in parts]
    weight = highs + mids + highs
    dist = dist + [zero] * (16 - len(dist))
    weight = weight + [zero] * (16 - len(weight))
    return jnp.concatenate(dist, axis=0), jnp.concatenate(weight, axis=0)


def build_lists(ints_ref, list_ref, count_ref):
    core = ints_ref[6, 0]
    dummy = 2 * (NDEV + 4)
    for side in range(NC):

        def add(k, counts, side=side):
            c0, c1 = counts
            sent = ints_ref[side, 2 * k]
            part = ints_ref[side, 2 * k + 1]
            source = 2 * k + sent
            list_ref[2 * side, c0] = source
            list_ref[2 * side + 1, c1] = source
            valid = (sent >= 0).astype(jnp.int32)
            to1 = valid * part
            c1 = c1 + to1
            c0 = c0 + valid - to1
            mine = ints_ref[2 + 2 * side, 2 * k + core]
            other = ints_ref[3 + 2 * side, 2 * k + core]
            source = 2 * k + other
            list_ref[2 * side, c0] = source
            list_ref[2 * side + 1, c1] = source
            c0 = c0 + (mine == 0).astype(jnp.int32)
            c1 = c1 + (mine == 1).astype(jnp.int32)
            return c0, c1

        c0, c1 = lax.fori_loop(0, NDEV, add, (jnp.int32(0), jnp.int32(0)), unroll=8)
        own = (core == side).astype(jnp.int32)
        for place, count in ((2 * side, c0), (2 * side + 1, c1)):
            for j in range(8):
                list_ref[place, count + j] = 2 * NDEV + j
            count = count + 8 * own
            for j in range(BATCH):
                list_ref[place, count + j] = dummy
            count_ref[0, place] = lax.div(count + (BATCH - 1), BATCH)


def pair_body(
    list_ref, count_ref, get_source, get_target, force_ref, dist_s, prod_s, mom_s, dist_t, prod_t
):
    def prepare(k):
        x_tile, l_tile, b_tile = get_source(k)
        dist, weight, first, second = source_operands(x_tile, l_tile, b_tile)
        store_rows(dist_s, k, dist)
        store_rows(prod_s, k, weight)
        mom_s[2 * k] = jnp.concatenate(first, axis=0).astype(BF16)
        mom_s[2 * k + 1] = jnp.concatenate(second, axis=0).astype(BF16)

    tail = jnp.zeros((64, SEG), BF16)
    tail_p = jnp.zeros((48, SEG), BF16)

    def clear(k, carry):
        dist_s[k, 64:128, :] = tail
        prod_s[k, 80:128, :] = tail_p
        return carry

    lax.fori_loop(0, NDEV + 5, clear, 0, unroll=3)

    def prepare_loop(k, carry):
        prepare(k)
        return carry

    lax.fori_loop(0, NDEV, prepare_loop, 0, unroll=4)
    for k in range(NDEV, NDEV + 5):
        prepare(k)

    lane = lax.broadcasted_iota(jnp.int32, (SEG, SEG), 1)
    group = lax.shift_right_logical(lane, 3)
    place = lax.bitwise_and(lane, 7)
    for side in range(NC):
        x_tile, l_tile, b_tile = get_target(side)
        for block in range(2):
            dist, weight = target_rows(x_tile, l_tile, b_tile, block)
            dist = dist.T
            weight = weight.T
            for j in range(2):
                mine = (place >= 3 * j) & (place < 3 * j + 3)
                keep = mine | (place == 6 + j) | (group == 6)
                at = 2 * (2 * side + block) + j
                dist_t[at] = jnp.where(keep, dist, 0.0).astype(BF16)
                prod_t[at] = jnp.where(mine, weight, 0.0).astype(BF16)

    for side in range(NC):
        x_tile = get_target(side)[0]
        rows = []
        for block in range(2):
            n = 2 * side + block

            def items(step, total, n=n):
                lows, highs, moments = [], [], []
                for b in range(BATCH):
                    m = list_ref[n, step * BATCH + b]
                    k = lax.shift_right_logical(m, 1)
                    at = 2 * n + lax.bitwise_and(m, 1)
                    sq = jnp.dot(dist_t[at], dist_s[k], preferred_element_type=F32)
                    pr = jnp.dot(prod_t[at], prod_s[k], preferred_element_type=F32)
                    inverse = lax.rsqrt(sq)
                    w = pr * (inverse * inverse * inverse)
                    high = w.astype(BF16)
                    low = (w - high.astype(F32)).astype(BF16)
                    highs.append(high)
                    lows.append(low)
                    moments.append(mom_s[m])
                lhs = jnp.concatenate(highs + lows, axis=1)
                rhs = jnp.concatenate(moments + moments, axis=1)
                return total + lax.dot_general(
                    lhs, rhs, (((1,), (1,)), ((), ())), preferred_element_type=F32
                )

            total = lax.fori_loop(0, count_ref[0, n], items, jnp.zeros((SEG, 16), F32))
            total = jnp.concatenate([total, jnp.zeros((SEG, SEG - 16), F32)], axis=1).T
            x_block = x_tile[3 * block : 3 * block + 3]
            rows.append(x_block * total[6:7] - (total[0:3] + total[8:11]))
        rows.append(jnp.zeros((2, SEG), F32))
        force_ref[side] = jnp.concatenate(rows, axis=0)


SCRATCH = [
    pltpu.VMEM((NDEV + 5, SEG, SEG), BF16),
    pltpu.VMEM((NDEV + 5, SEG, SEG), BF16),
    pltpu.VMEM((2 * (NDEV + 5), 16, SEG), BF16),
    pltpu.VMEM((8, SEG, SEG), BF16),
    pltpu.VMEM((8, SEG, SEG), BF16),
]


def first_kernel(
    ints_ref, all_ref, group_ref, chip_ref, force_ref, list_ref, count_ref, *scratch
):
    build_lists(ints_ref, list_ref, count_ref)

    def get_source(k):
        if isinstance(k, int) and k == NDEV + 4:
            zero = jnp.zeros((8, SEG), F32)
            return zero, zero, zero
        if isinstance(k, int):
            tile = group_ref[k - NDEV]
        else:
            tile = all_ref[k]
        return tile[0:8], tile[8:16], tile[16:24]

    def get_target(side):
        return chip_ref[side, 0:8], chip_ref[side, 8:16], chip_ref[side, 16:24]

    pair_body(list_ref, count_ref, get_source, get_target, force_ref, *scratch)


def second_kernel(
    ints_ref,
    list_ref,
    count_ref,
    all_ref,
    group_ref,
    chip_ref,
    vel_ref,
    top_ref,
    chip_vel_ref,
    force_ref,
    chip_x_ref,
    *scratch,
):
    y_index = ints_ref[6, 1]
    top = jnp.max(jnp.max(top_ref[...], axis=0)[6:7], axis=1, keepdims=True)
    step = STEP_LENGTH / (jnp.sqrt(top) + EPSILON)
    row = sublane()

    def get_source(k):
        if isinstance(k, int) and k == NDEV + 4:
            zero = jnp.zeros((8, SEG), F32)
            return zero, zero, zero
        if isinstance(k, int):
            tile = group_ref[k - NDEV]
            moved = top_ref[4 * y_index + (k - NDEV)]
        else:
            tile = all_ref[k]
            moved = vel_ref[k]
        return tile[0:8] + step * moved, tile[8:16], tile[16:24]

    for side in range(NC):
        moved = jnp.where(row < 6, chip_vel_ref[side], 0.0)
        chip_x_ref[side] = chip_ref[side, 0:8] + step * moved

    def get_target(side):
        return chip_x_ref[side], chip_ref[side, 8:16], chip_ref[side, 16:24]

    pair_body(list_ref, count_ref, get_source, get_target, force_ref, *scratch)


def finish_kernel(ints_ref, stress_ref, parts_ref, chip_ref, x_ref, vel_ref, mine_ref):
    core = ints_ref[6, 0]
    row = sublane()
    lane = lax.broadcasted_iota(jnp.int32, (8, SEG), 1)
    tops = []
    tiles = []
    for side in range(NC):
        x_tile = x_ref[side, 0:8]
        l_tile = chip_ref[side, 8:16]
        b_tile = chip_ref[side, 16:24]
        rows = []
        for block in range(2):
            b = [b_tile[3 * block + a : 3 * block + a + 1] for a in range(3)]
            line = [l_tile[3 * block + a : 3 * block + a + 1] for a in range(3)]
            pulled = [
                stress_ref[a, 0] * b[0] + stress_ref[a, 1] * b[1] + stress_ref[a, 2] * b[2]
                for a in range(3)
            ]
            rows.append(pulled[1] * line[2] - pulled[2] * line[1])
            rows.append(pulled[2] * line[0] - pulled[0] * line[2])
            rows.append(pulled[0] * line[1] - pulled[1] * line[0])
        rows.append(jnp.zeros((2, SEG), F32))
        applied = jnp.concatenate(rows, axis=0)
        left = jnp.where(lane == 0, x_tile, pltpu.roll(x_tile, 1, 1))
        right = jnp.where(lane == SEG - 1, x_tile, pltpu.roll(x_tile, SEG - 1, 1))
        chain = left + right - 2.0 * x_tile
        pair = parts_ref[0, side] + parts_ref[1, side]
        drag = jnp.where(row < 3, b_tile[6:7], b_tile[7:8])
        velocity = (COUPLE * pair + applied + TENSION * chain) / drag
        speed = velocity * velocity
        tops.append(
            jnp.maximum(
                speed[0:1] + speed[1:2] + speed[2:3], speed[3:4] + speed[4:5] + speed[5:6]
            )
        )
        tiles.append(velocity)
    top = jnp.maximum(tops[0], tops[1])
    for side in range(NC):
        vel_ref[side] = jnp.where(row < 6, tiles[side], jnp.where(row == 6, top, 0.0))
    mine_ref[...] = vel_ref[core]


def last_kernel(ints_ref, top_ref, x_ref, vel_ref, pos_out, vel_out):
    core = ints_ref[6, 0]
    top = jnp.max(jnp.max(top_ref[...], axis=0)[6:7], axis=1, keepdims=True)
    step = STEP_LENGTH / (jnp.sqrt(top) + EPSILON)
    velocity = vel_ref[core]
    moved = x_ref[core] + step * velocity
    for block in range(2):
        pos_out[block] = moved[3 * block : 3 * block + 3]
        vel_out[block] = velocity[3 * block : 3 * block + 3]


SMEM = pl.BlockSpec(memory_space=pltpu.SMEM)
VMEM = pl.BlockSpec(memory_space=pltpu.VMEM)


def shape(*dims, dtype=F32):
    return jax.ShapeDtypeStruct(dims, dtype)


def spread(value, axes, count):
    return lax.all_to_all(
        jnp.broadcast_to(value[None], (count,) + value.shape), axes, 0, 0, tiled=True
    )


def local(segments, stress, drag_coef, send_ids, partner_ids):
    core = lax.axis_index("c")
    y_index = lax.axis_index("y")
    chip_index = y_index * NZ + lax.axis_index("z")
    send = send_ids.reshape(1, SEG).astype(F32)
    part = partner_ids.reshape(1, SEG).astype(F32)
    raw = jnp.concatenate(
        [
            segments[:, 0:3].reshape(6, SEG),
            jnp.zeros((2, SEG), F32),
            segments[:, 3:6].reshape(6, SEG),
            send,
            part,
            segments[:, 6:9].reshape(6, SEG),
            drag_coef,
        ],
        axis=0,
    )
    chip = lax.all_gather(raw, "c", axis=0)
    along_z = spread(raw, "z", NZ)
    group = spread(raw, "x", 4)
    everyone = spread(along_z.reshape(NZ * 24, SEG), "y", NY).reshape(NDEV, 24, SEG)

    lists = everyone[:, 14:16].reshape(2 * NDEV, SEG)
    lane = lax.broadcasted_iota(jnp.int32, (NC, SEG), 1)
    wanted = 2 * chip_index + lax.broadcasted_iota(jnp.int32, (NC, SEG), 0)
    pick = (lane == wanted).astype(F32)
    incoming = lax.dot_general(
        pick, lists, (((1,), (1,)), ((), ())), precision=lax.Precision.HIGHEST
    )
    where = jnp.where(lane[0:1] == 0, core, y_index)
    ints = jnp.concatenate(
        [
            incoming.astype(jnp.int32),
            chip[:, 14:16].reshape(4, SEG).astype(jnp.int32),
            where,
            jnp.zeros((1, SEG), jnp.int32),
        ],
        axis=0,
    )

    force, lists, counts = pl.pallas_call(
        first_kernel,
        name="first_pairs",
        in_specs=[SMEM, VMEM, VMEM, VMEM],
        out_specs=[VMEM, SMEM, SMEM],
        out_shape=[
            shape(NC, 8, SEG),
            shape(4, LIST, dtype=jnp.int32),
            shape(1, 4, dtype=jnp.int32),
        ],
        scratch_shapes=SCRATCH,
    )(ints, everyone, group, chip)

    def finish(parts, position):
        return pl.pallas_call(
            finish_kernel,
            name="finish",
            in_specs=[SMEM, SMEM, VMEM, VMEM, VMEM],
            out_specs=[VMEM, VMEM],
            out_shape=[shape(NC, 8, SEG), shape(8, SEG)],
        )(ints, stress, parts, chip, position)

    chip_vel, mine = finish(lax.all_gather(force, "c", axis=0), chip[:, 0:8])
    vel_z = spread(mine, "z", NZ)
    vel_all = spread(vel_z.reshape(NZ * 8, SEG), "y", NY).reshape(NDEV, 8, SEG)
    row = lax.broadcasted_iota(jnp.int32, (8, SEG), 0)
    with_top = jnp.where(row == 6, jnp.max(vel_z[:, 6:7], axis=0), mine)
    tops = spread(with_top, ("y", "x"), 16)

    force, position = pl.pallas_call(
        second_kernel,
        name="second_pairs",
        in_specs=[SMEM, SMEM, SMEM] + [VMEM] * 6,
        out_specs=[VMEM, VMEM],
        out_shape=[shape(NC, 8, SEG), shape(NC, 8, SEG)],
        scratch_shapes=SCRATCH,
    )(ints, lists, counts, everyone, group, chip, vel_all, tops, chip_vel)

    chip_vel, mine = finish(lax.all_gather(force, "c", axis=0), position)
    top_z = jnp.max(spread(mine, "z", NZ), axis=0)
    tops = spread(top_z, ("y", "x"), 16)
    return pl.pallas_call(
        last_kernel,
        name="last",
        in_specs=[SMEM, VMEM, VMEM, VMEM],
        out_specs=[VMEM, VMEM],
        out_shape=[shape(2, 3, SEG), shape(2, 3, SEG)],
    )(ints, tops, position, chip_vel)


def solution(mesh):
    split = Mesh(
        mesh.devices.reshape(NY, NZ, NC, mesh.shape["sub"]), ("y", "z", "c", "x")
    )
    return jax.shard_map(
        local,
        mesh=split,
        in_specs=(
            P(DOM_SUB, None, None),
            P(),
            P(DOM_SUB, None),
            P(DOM_SUB, None, None),
            P(DOM_SUB, None, None),
        ),
        out_specs=(P(DOM_SUB, None, None), P(DOM_SUB, None, None)),
        check_vma=False,
    )
```

```python
import functools

import jax
import jax.numpy as jnp
from jax import lax
from jax.experimental import pallas as pl
from jax.experimental.pallas import tpu as pltpu
from jax.sharding import Mesh
from jax.sharding import PartitionSpec as P

NY, NZ, NC = 4, 16, 2
DOM = ("y", "z", "c")
DOM_SUB = ("y", "z", "c", "x")

COUPLE = 0.0625
CORE_SQUARE = 0.5
TENSION = 0.25
STEP_LENGTH = 1.0
EPSILON = 1e-06

SEG = 128
NDEV = NY * NZ
NX = 4
BATCH = 16
LIST = 320
DUMMY = 2 * (NDEV + NX)
F32 = jnp.float32
BF16 = jnp.bfloat16


def sublane(shape=(8, SEG)):
    return lax.broadcasted_iota(jnp.int32, shape, len(shape) - 2)


def up(value, count):
    return jnp.concatenate([value[count:], value[:count]], axis=0)


def split2(value):
    high = value.astype(BF16).astype(F32)
    return high, value - high


def split3(value):
    high, rest = split2(value)
    mid, low = split2(rest)
    return high, mid, low


def source_operands(x_tile, l_tile, b_tile):
    row = sublane()
    x_tile = jnp.where(row < 6, x_tile, 0.0)
    square = x_tile * x_tile
    norm0 = square[0:1] + square[1:2] + square[2:3] + CORE_SQUARE
    norm1 = square[3:4] + square[4:5] + square[5:6] + CORE_SQUARE
    full = jnp.where(row == 6, norm0, jnp.where(row == 7, norm1, x_tile))
    high, mid, low = split3(full)
    dist = [high, mid, high, mid, low, high, jnp.ones_like(high)]
    prod = [jnp.where(row < 3, b_tile[a : a + 1], b_tile[3 + a : 4 + a]) * l_tile for a in range(3)]
    parts = [split2(p) for p in prod]
    highs = [p[0] for p in parts]
    mids = [p[1] for p in parts]
    weight = highs + highs + mids
    flag = jnp.where(row == 6, 1.0, 0.0)
    first = (jnp.where(row < 6, high, flag), jnp.where(row < 6, mid, 0.0))
    second = (jnp.where(row < 3, up(high, 3), flag), jnp.where(row < 3, up(mid, 3), 0.0))
    return dist + weight, first, second


def store_rows(ref, index, tiles):
    for at in range(0, len(tiles), 2):
        pair = jnp.concatenate([tiles[at], tiles[at + 1]], axis=0).astype(BF16)
        ref[index, 8 * at : 8 * at + 16, :] = pair


def target_rows(x_tile, l_tile, b_tile, block):
    row = sublane()

    def both(tile):
        if block == 0:
            return jnp.where(row < 3, tile, jnp.where(row < 6, up(tile, 5), 0.0))
        return jnp.where(row < 3, up(tile, 3), jnp.where(row < 6, tile, 0.0))

    x_both = both(x_tile)
    high, mid, low = split3(x_both)
    square = x_both * x_both
    norm = square[0:1] + square[1:2] + square[2:3]
    norm_h, norm_m, norm_l = split3(norm)
    unit = jnp.where(row >= 6, 1.0, 0.0)
    norms = jnp.where(
        row == 0, norm_h, jnp.where(row == 1, norm_m, jnp.where(row == 2, norm_l, 0.0))
    )
    zero = jnp.zeros_like(high)
    dist = [
        -2.0 * high + unit,
        -2.0 * high + unit,
        -2.0 * mid,
        -2.0 * mid,
        -2.0 * high + unit,
        -2.0 * low,
        norms,
    ]
    l_both = both(l_tile)
    base = 3 * block
    prod = [b_tile[base + a : base + a + 1] * l_both for a in range(3)]
    parts = [split2(p) for p in prod]
    highs = [p[0] for p in parts]
    mids = [p[1] for p in parts]
    weight = highs + mids + highs
    return jnp.concatenate(dist + [zero] * 9, axis=0), jnp.concatenate([zero] * 7 + weight, axis=0)


def build_list(codes_ref, list_ref, count_ref):
    core = codes_ref[6, 0]

    def add(k, count):
        for line in range(2 * NC):
            code = codes_ref[line, 2 * k + core if line >= NC else 2 * k]
            list_ref[0, count] = code
            count = count + (code >= 0).astype(jnp.int32)
        return count

    count = lax.fori_loop(0, NDEV, add, jnp.int32(0), unroll=8)
    for block in range(2):
        for j in range(2 * NX):
            list_ref[0, count + 2 * NX * block + j] = 256 * (2 * core + block) + 2 * NDEV + j
    count = count + 4 * NX
    for j in range(BATCH):
        list_ref[0, count + j] = DUMMY
    count_ref[0, 0] = lax.div(count + (BATCH - 1), BATCH)


def pair_body(list_ref, count_ref, get_source, get_target, force_ref, source_s, moment_s, target_s):
    def prepare(k):
        tiles, first, second = source_operands(*get_source(k))
        store_rows(source_s, k, tiles)
        moment_s[2 * k] = jnp.concatenate(first, axis=0).astype(BF16)
        moment_s[2 * k + 1] = jnp.concatenate(second, axis=0).astype(BF16)

    def prepare_loop(k, carry):
        prepare(k)
        return carry

    lax.fori_loop(0, NDEV, prepare_loop, 0, unroll=4)
    for k in range(NDEV, NDEV + NX + 1):
        prepare(k)

    lane = lax.broadcasted_iota(jnp.int32, (SEG, SEG), 1)
    place = lax.bitwise_and(lane, 7)
    for side in range(NC):
        x_tile, l_tile, b_tile = get_target(side)
        for block in range(2):
            dist, weight = target_rows(x_tile, l_tile, b_tile, block)
            dist = dist.T
            weight = weight.T
            for j in range(2):
                mine = (place >= 3 * j) & (place < 3 * j + 3)
                keep = mine | (place == 6 + j) | (lane >= 48)
                at = 2 * (2 * side + block) + j
                target_s[at, 0:SEG] = jnp.where(keep, dist, 0.0).astype(BF16)
                target_s[at, SEG : 2 * SEG] = jnp.where(mine, weight, 0.0).astype(BF16)

    def items(step, total):
        lows, highs, moments = [], [], []
        for b in range(BATCH):
            code = list_ref[0, step * BATCH + b]
            n = lax.shift_right_logical(code, 8)
            m = lax.bitwise_and(code, 255)
            at = 2 * n + lax.bitwise_and(m, 1)
            both = jnp.dot(
                target_s[at], source_s[lax.shift_right_logical(m, 1)], preferred_element_type=F32
            )
            inverse = lax.rsqrt(both[0:SEG])
            w = both[SEG : 2 * SEG] * (inverse * inverse * inverse)
            high = w.astype(BF16)
            highs.append(high)
            lows.append((w - high.astype(F32)).astype(BF16))
            moment = moment_s[m]
            zero = jnp.zeros_like(moment)
            moments.append(
                jnp.concatenate([jnp.where(n == t, moment, zero) for t in range(4)], axis=0)
            )
        lhs = jnp.concatenate(moments + moments, axis=1)
        rhs = jnp.concatenate(highs + lows, axis=1)
        return total + lax.dot_general(
            lhs, rhs, (((1,), (1,)), ((), ())), preferred_element_type=F32
        )

    total = lax.fori_loop(0, count_ref[0, 0], items, jnp.zeros((64, SEG), F32))
    for side in range(NC):
        x_tile = get_target(side)[0]
        rows = []
        for block in range(2):
            at = 16 * (2 * side + block)
            x_block = x_tile[3 * block : 3 * block + 3]
            rows.append(
                x_block * total[at + 6 : at + 7] - (total[at : at + 3] + total[at + 8 : at + 11])
            )
        rows.append(jnp.zeros((2, SEG), F32))
        force_ref[side] = jnp.concatenate(rows, axis=0)


SCRATCH = [
    pltpu.VMEM((NDEV + NX + 1, SEG, SEG), BF16),
    pltpu.VMEM((2 * (NDEV + NX + 1), 16, SEG), BF16),
    pltpu.VMEM((8, 2 * SEG, SEG), BF16),
]


def tiles_of(tile):
    return tile[0:8], tile[8:16], tile[16:24]


def no_source():
    zero = jnp.zeros((8, SEG), F32)
    return zero, zero, zero


def first_kernel(codes_ref, all_ref, g0, g1, g2, g3, chip_ref, force_ref, list_ref, count_ref, *scratch):
    build_list(codes_ref, list_ref, count_ref)
    group = (g0, g1, g2, g3)

    def get_source(k):
        if isinstance(k, int):
            return no_source() if k == NDEV + NX else tiles_of(group[k - NDEV])
        return tiles_of(all_ref.at[k])

    def get_target(side):
        return tiles_of(chip_ref.at[side])

    pair_body(list_ref, count_ref, get_source, get_target, force_ref, *scratch)


def second_kernel(
    codes_ref,
    list_ref,
    count_ref,
    all_ref,
    g0,
    g1,
    g2,
    g3,
    chip_ref,
    vel_ref,
    near_ref,
    chip_vel_ref,
    force_ref,
    chip_x_ref,
    *scratch,
):
    y_index = codes_ref[6, 1]
    x_index = codes_ref[6, 2]
    top = vel_ref[0, 0]
    for z in range(1, NZ):
        top = jnp.maximum(top, vel_ref[z, 0])
    top = jnp.max(top[6:7], axis=1, keepdims=True)
    step = STEP_LENGTH / (jnp.sqrt(top) + EPSILON)
    row = sublane()
    group = (g0, g1, g2, g3)

    def get_source(k):
        if isinstance(k, int):
            if k == NDEV + NX:
                return no_source()
            shift = k - NDEV
            x_tile, l_tile, b_tile = tiles_of(group[shift])
            moved = near_ref[y_index, lax.bitwise_and(x_index - shift, NX - 1)]
        else:
            x_tile, l_tile, b_tile = tiles_of(all_ref.at[k])
            moved = vel_ref[lax.bitwise_and(k, NZ - 1), lax.shift_right_logical(k, 4)]
        return x_tile + step * moved, l_tile, b_tile

    for side in range(NC):
        moved = jnp.where(row < 6, chip_vel_ref[side], 0.0)
        chip_x_ref[side] = chip_ref[side, 0:8] + step * moved

    def get_target(side):
        return chip_x_ref[side], chip_ref[side, 8:16], chip_ref[side, 16:24]

    pair_body(list_ref, count_ref, get_source, get_target, force_ref, *scratch)


def finish_kernel(last, codes_ref, stress_ref, parts_ref, chip_ref, x_ref, vel_ref, out_ref):
    core = codes_ref[6, 0]
    row = sublane()
    lane = lax.broadcasted_iota(jnp.int32, (8, SEG), 1)
    tops = []
    tiles = []
    for side in range(NC):
        x_tile = x_ref[side, 0:8]
        l_tile = chip_ref[side, 8:16]
        b_tile = chip_ref[side, 16:24]
        rows = []
        for block in range(2):
            b = [b_tile[3 * block + a : 3 * block + a + 1] for a in range(3)]
            line = [l_tile[3 * block + a : 3 * block + a + 1] for a in range(3)]
            pulled = [
                stress_ref[a, 0] * b[0] + stress_ref[a, 1] * b[1] + stress_ref[a, 2] * b[2]
                for a in range(3)
            ]
            rows.append(pulled[1] * line[2] - pulled[2] * line[1])
            rows.append(pulled[2] * line[0] - pulled[0] * line[2])
            rows.append(pulled[0] * line[1] - pulled[1] * line[0])
        rows.append(jnp.zeros((2, SEG), F32))
        applied = jnp.concatenate(rows, axis=0)
        left = jnp.where(lane == 0, x_tile, pltpu.roll(x_tile, 1, 1))
        right = jnp.where(lane == SEG - 1, x_tile, pltpu.roll(x_tile, SEG - 1, 1))
        chain = left + right - 2.0 * x_tile
        pair = parts_ref[0, side] + parts_ref[1, side]
        drag = jnp.where(row < 3, b_tile[6:7], b_tile[7:8])
        velocity = (COUPLE * pair + applied + TENSION * chain) / drag
        speed = velocity * velocity
        tops.append(
            jnp.maximum(
                speed[0:1] + speed[1:2] + speed[2:3], speed[3:4] + speed[4:5] + speed[5:6]
            )
        )
        tiles.append(velocity)
    top = jnp.maximum(tops[0], tops[1])
    for side in range(NC):
        vel_ref[side] = jnp.where(row < 6, tiles[side], jnp.where(row == 6, top, 0.0))
    if last:
        for peer in range(NZ):
            out_ref[peer] = top
    else:
        mine = vel_ref[core]
        for peer in range(NY * NX):
            out_ref[peer] = mine


def pack_kernel(seg_ref, drag_ref, send_ref, part_ref, raw_ref, out_ref):
    raw_ref[...] = jnp.zeros((24, SEG), F32)
    for block in range(2):
        for comp in range(3):
            for tile in range(3):
                raw_ref[8 * tile + 3 * block + comp, :] = seg_ref[3 * tile + comp, block, :]
        raw_ref[22 + block, :] = drag_ref[block, :]
    raw_ref[14, :] = send_ref[0, :].astype(F32)
    raw_ref[15, :] = part_ref[0, :].astype(F32)
    raw = raw_ref[...]
    for peer in range(NZ):
        out_ref[peer] = raw


def relay_kernel(codes_ref, near_ref, out_ref):
    x_index = codes_ref[6, 2]
    top = near_ref[0, 0]
    for at in range(1, NY * NX):
        top = jnp.maximum(top, near_ref[at // NX, at % NX])
    row = sublane()
    for y in range(NY):
        tile = jnp.where(row == 6, top, near_ref[y, x_index])
        for peer in range(NZ):
            out_ref[peer, y] = tile


def last_kernel(codes_ref, top_ref, x_ref, vel_ref, pos_out, vel_out):
    core = codes_ref[6, 0]
    top = jnp.max(jnp.max(top_ref[...], axis=0), axis=1, keepdims=True)
    step = STEP_LENGTH / (jnp.sqrt(top) + EPSILON)
    velocity = vel_ref[core]
    moved = x_ref[core] + step * velocity
    for block in range(2):
        for comp in range(3):
            pos_out[comp, block, :] = moved[3 * block + comp]
            vel_out[comp, block, :] = velocity[3 * block + comp]


SMEM = pl.BlockSpec(memory_space=pltpu.SMEM)
VMEM = pl.BlockSpec(memory_space=pltpu.VMEM)


def shape(*dims, dtype=F32):
    return jax.ShapeDtypeStruct(dims, dtype)


def call(kernel, name, operands, outs, smem_in=0, smem_out=0, scratch=(), mib=4):
    return pl.pallas_call(
        kernel,
        name=name,
        in_specs=[SMEM] * smem_in + [VMEM] * (len(operands) - smem_in),
        out_specs=[VMEM] * (len(outs) - smem_out) + [SMEM] * smem_out,
        out_shape=outs,
        scratch_shapes=scratch,
        compiler_params=pltpu.CompilerParams(vmem_limit_bytes=mib << 20),
    )(*operands)


def exchange(value, axes):
    return lax.all_to_all(value, axes, 0, 0, tiled=True)


def local(segments, stress, drag_coef, send_ids, partner_ids):
    core = lax.axis_index("c")
    y_index = lax.axis_index("y")
    x_index = lax.axis_index("x")
    chip_index = y_index * NZ + lax.axis_index("z")
    raw, to_z = call(
        pack_kernel,
        "pack",
        (
            segments.transpose(1, 0, 2),
            drag_coef,
            send_ids.reshape(1, SEG),
            partner_ids.reshape(1, SEG),
        ),
        [shape(24, SEG), shape(NZ, 24, SEG)],
    )
    along_z = exchange(to_z, "z")
    group = [raw] + [
        lax.ppermute(raw, "x", [(i, (i + shift) % NX) for i in range(NX)])
        for shift in range(1, NX)
    ]
    chip = lax.all_gather(raw, "c", axis=0)
    everyone = exchange(
        jnp.broadcast_to(along_z.reshape(1, NZ * 24, SEG), (NY, NZ * 24, SEG)), "y"
    ).reshape(NDEV, 24, SEG)

    lists = everyone[:, 14:16].reshape(2 * NDEV, SEG)
    lane = lax.broadcasted_iota(jnp.int32, (NC, SEG), 1)
    side = lax.broadcasted_iota(jnp.int32, (NC, SEG), 0)
    even = lax.bitwise_and(lane, SEG - 2)
    pick = (lane == 2 * chip_index + side).astype(F32)
    incoming = lax.dot_general(
        pick, lists, (((1,), (1,)), ((), ())), precision=lax.Precision.HIGHEST
    ).astype(jnp.int32)
    partner = jnp.concatenate([incoming[:, 1:], incoming[:, :1]], axis=1)
    into = jnp.where(incoming >= 0, even + incoming + 256 * (2 * side + partner), -1)
    sent = chip[:, 14].astype(jnp.int32)
    other = chip[:, 15].astype(jnp.int32)
    out = jnp.where(sent >= 0, even + other + 256 * (2 * side + sent), -1)
    first = lane[0:1]
    where = jnp.where(first == 0, core, jnp.where(first == 1, y_index, x_index))
    zero = jnp.zeros((1, SEG), jnp.int32)
    codes = jnp.concatenate([into, out, zero, zero, where, zero], axis=0)

    force, items, count = call(
        first_kernel,
        "first_pairs",
        (codes, everyone, *group, chip),
        [
            shape(NC, 8, SEG),
            shape(1, LIST, dtype=jnp.int32),
            shape(1, 1, dtype=jnp.int32),
        ],
        smem_in=1,
        smem_out=2,
        scratch=SCRATCH,
        mib=16,
    )
    chip_vel, to_near = call(
        functools.partial(finish_kernel, False),
        "finish",
        (codes, stress, lax.all_gather(force, "c", axis=0), chip, chip),
        [shape(NC, 8, SEG), shape(NY * NX, 8, SEG)],
        smem_in=2,
    )
    near = exchange(to_near, ("y", "x")).reshape(NY, NX, 8, SEG)
    (to_z,) = call(relay_kernel, "relay", (codes, near), [shape(NZ, NY, 8, SEG)], smem_in=1)
    vel_all = exchange(to_z.reshape(NZ, NY * 8, SEG), "z").reshape(NZ, NY, 8, SEG)

    force, position = call(
        second_kernel,
        "second_pairs",
        (codes, items, count, everyone, *group, chip, vel_all, near, chip_vel),
        [shape(NC, 8, SEG), shape(NC, 8, SEG)],
        smem_in=3,
        scratch=SCRATCH,
        mib=16,
    )
    chip_vel, to_z = call(
        functools.partial(finish_kernel, True),
        "finish_last",
        (codes, stress, lax.all_gather(force, "c", axis=0), chip, position),
        [shape(NC, 8, SEG), shape(NZ, 1, SEG)],
        smem_in=2,
    )
    top_z = jnp.max(exchange(to_z, "z"), axis=0)
    tops = exchange(jnp.broadcast_to(top_z[None], (NY * NX, 1, SEG)), ("y", "x"))
    positions, velocity = call(
        last_kernel,
        "last",
        (codes, tops, position, chip_vel),
        [shape(3, 2, SEG), shape(3, 2, SEG)],
        smem_in=1,
    )
    return positions.transpose(1, 0, 2), velocity.transpose(1, 0, 2)


def solution(mesh):
    split = Mesh(
        mesh.devices.reshape(NY, NZ, NC, mesh.shape["sub"]), ("y", "z", "c", "x")
    )
    return jax.shard_map(
        local,
        mesh=split,
        in_specs=(
            P(DOM_SUB, None, None),
            P(),
            P(DOM_SUB, None),
            P(DOM_SUB, None, None),
            P(DOM_SUB, None, None),
        ),
        out_specs=(P(DOM_SUB, None, None), P(DOM_SUB, None, None)),
        check_vma=False,
    )
```

```python
import functools

import jax
import jax.numpy as jnp
from jax import lax
from jax.experimental import pallas as pl
from jax.experimental.pallas import tpu as pltpu
from jax.sharding import Mesh
from jax.sharding import PartitionSpec as P

NY, NZ, NC = 4, 16, 2
DOM = ("y", "z", "c")
DOM_SUB = ("y", "z", "c", "x")

COUPLE = 0.0625
CORE_SQUARE = 0.5
TENSION = 0.25
STEP_LENGTH = 1.0
EPSILON = 1e-06

SEG = 128
NDEV = NY * NZ
NX = 4
BATCH = 16
LIST = 320
DUMMY = 2 * (NDEV + NX)
F32 = jnp.float32
BF16 = jnp.bfloat16


def sublane(shape=(8, SEG)):
    return lax.broadcasted_iota(jnp.int32, shape, len(shape) - 2)


def up(value, count):
    return jnp.concatenate([value[count:], value[:count]], axis=0)


def split2(value):
    high = value.astype(BF16).astype(F32)
    return high, value - high


def split3(value):
    high, rest = split2(value)
    mid, low = split2(rest)
    return high, mid, low


def source_operands(x_tile, l_tile, b_tile):
    row = sublane()
    x_tile = jnp.where(row < 6, x_tile, 0.0)
    square = x_tile * x_tile
    norm0 = square[0:1] + square[1:2] + square[2:3] + CORE_SQUARE
    norm1 = square[3:4] + square[4:5] + square[5:6] + CORE_SQUARE
    full = jnp.where(row == 6, norm0, jnp.where(row == 7, norm1, x_tile))
    high, mid, low = split3(full)
    dist = [high, mid, high, mid, low, high, jnp.ones_like(high)]
    prod = [jnp.where(row < 3, b_tile[a : a + 1], b_tile[3 + a : 4 + a]) * l_tile for a in range(3)]
    parts = [split2(p) for p in prod]
    highs = [p[0] for p in parts]
    mids = [p[1] for p in parts]
    weight = highs + highs + mids
    flag = jnp.where(row == 6, 1.0, 0.0)
    first = (jnp.where(row < 6, high, flag), jnp.where(row < 6, mid, 0.0))
    second = (jnp.where(row < 3, up(high, 3), flag), jnp.where(row < 3, up(mid, 3), 0.0))
    return dist + weight, first, second


def store_rows(ref, index, tiles):
    for at in range(0, len(tiles), 2):
        pair = jnp.concatenate([tiles[at], tiles[at + 1]], axis=0).astype(BF16)
        ref[index, 8 * at : 8 * at + 16, :] = pair


def target_rows(x_tile, l_tile, b_tile, block):
    row = sublane()

    def both(tile):
        if block == 0:
            return jnp.where(row < 3, tile, jnp.where(row < 6, up(tile, 5), 0.0))
        return jnp.where(row < 3, up(tile, 3), jnp.where(row < 6, tile, 0.0))

    x_both = both(x_tile)
    high, mid, low = split3(x_both)
    square = x_both * x_both
    norm = square[0:1] + square[1:2] + square[2:3]
    norm_h, norm_m, norm_l = split3(norm)
    unit = jnp.where(row >= 6, 1.0, 0.0)
    norms = jnp.where(
        row == 0, norm_h, jnp.where(row == 1, norm_m, jnp.where(row == 2, norm_l, 0.0))
    )
    zero = jnp.zeros_like(high)
    dist = [
        -2.0 * high + unit,
        -2.0 * high + unit,
        -2.0 * mid,
        -2.0 * mid,
        -2.0 * high + unit,
        -2.0 * low,
        norms,
    ]
    l_both = both(l_tile)
    base = 3 * block
    prod = [b_tile[base + a : base + a + 1] * l_both for a in range(3)]
    parts = [split2(p) for p in prod]
    highs = [p[0] for p in parts]
    mids = [p[1] for p in parts]
    weight = highs + mids + highs
    return jnp.concatenate(dist + [zero] * 9, axis=0), jnp.concatenate([zero] * 7 + weight, axis=0)


def build_list(codes_ref, list_ref, count_ref):
    core = codes_ref[6, 0]

    def add(k, count):
        for line in range(2 * NC):
            code = codes_ref[line, 2 * k + core if line >= NC else 2 * k]
            list_ref[0, count] = code
            count = count + (code >= 0).astype(jnp.int32)
        return count

    count = lax.fori_loop(0, NDEV, add, jnp.int32(0), unroll=8)
    for block in range(2):
        for j in range(2 * NX):
            list_ref[0, count + 2 * NX * block + j] = 256 * (2 * core + block) + 2 * NDEV + j
    count = count + 4 * NX
    for j in range(BATCH):
        list_ref[0, count + j] = DUMMY
    count_ref[0, 0] = lax.div(count + (BATCH - 1), BATCH)


def pair_body(list_ref, count_ref, get_source, get_target, force_ref, source_s, moment_s, target_s):
    def prepare(k):
        tiles, first, second = source_operands(*get_source(k))
        store_rows(source_s, k, tiles)
        moment_s[2 * k] = jnp.concatenate(first, axis=0).astype(BF16)
        moment_s[2 * k + 1] = jnp.concatenate(second, axis=0).astype(BF16)

    def prepare_loop(k, carry):
        prepare(k)
        return carry

    lax.fori_loop(0, NDEV, prepare_loop, 0, unroll=4)
    for k in range(NDEV, NDEV + NX + 1):
        prepare(k)

    lane = lax.broadcasted_iota(jnp.int32, (SEG, SEG), 1)
    place = lax.bitwise_and(lane, 7)
    for side in range(NC):
        x_tile, l_tile, b_tile = get_target(side)
        for block in range(2):
            dist, weight = target_rows(x_tile, l_tile, b_tile, block)
            dist = dist.T
            weight = weight.T
            for j in range(2):
                mine = (place >= 3 * j) & (place < 3 * j + 3)
                keep = mine | (place == 6 + j) | (lane >= 48)
                at = 2 * (2 * side + block) + j
                target_s[at, 0:SEG] = jnp.where(keep, dist, 0.0).astype(BF16)
                target_s[at, SEG : 2 * SEG] = jnp.where(mine, weight, 0.0).astype(BF16)

    def items(step, total):
        lows, highs, moments = [], [], []
        for b in range(BATCH):
            code = list_ref[0, step * BATCH + b]
            n = lax.shift_right_logical(code, 8)
            m = lax.bitwise_and(code, 255)
            at = 2 * n + lax.bitwise_and(m, 1)
            both = jnp.dot(
                target_s[at], source_s[lax.shift_right_logical(m, 1)], preferred_element_type=F32
            )
            inverse = lax.rsqrt(both[0:SEG])
            w = both[SEG : 2 * SEG] * (inverse * inverse * inverse)
            high = w.astype(BF16)
            highs.append(high)
            lows.append((w - high.astype(F32)).astype(BF16))
            moment = moment_s[m]
            zero = jnp.zeros_like(moment)
            moments.append(
                jnp.concatenate([jnp.where(n == t, moment, zero) for t in range(4)], axis=0)
            )
        lhs = jnp.concatenate(moments + moments, axis=1)
        rhs = jnp.concatenate(highs + lows, axis=1)
        return total + lax.dot_general(
            lhs, rhs, (((1,), (1,)), ((), ())), preferred_element_type=F32
        )

    total = lax.fori_loop(0, count_ref[0, 0], items, jnp.zeros((64, SEG), F32))
    for side in range(NC):
        x_tile = get_target(side)[0]
        rows = []
        for block in range(2):
            at = 16 * (2 * side + block)
            x_block = x_tile[3 * block : 3 * block + 3]
            rows.append(
                x_block * total[at + 6 : at + 7] - (total[at : at + 3] + total[at + 8 : at + 11])
            )
        rows.append(jnp.zeros((2, SEG), F32))
        force_ref[side] = jnp.concatenate(rows, axis=0)


SCRATCH = [
    pltpu.VMEM((NDEV + NX + 1, SEG, SEG), BF16),
    pltpu.VMEM((2 * (NDEV + NX + 1), 16, SEG), BF16),
    pltpu.VMEM((8, 2 * SEG, SEG), BF16),
]


def tiles_of(tile):
    return tile[0:8], tile[8:16], tile[16:24]


def no_source():
    zero = jnp.zeros((8, SEG), F32)
    return zero, zero, zero


def first_kernel(codes_ref, all_ref, g0, g1, g2, g3, chip_ref, force_ref, list_ref, count_ref, *scratch):
    build_list(codes_ref, list_ref, count_ref)
    group = (g0, g1, g2, g3)

    def get_source(k):
        if isinstance(k, int):
            return no_source() if k == NDEV + NX else tiles_of(group[k - NDEV])
        return tiles_of(all_ref.at[k])

    def get_target(side):
        return tiles_of(chip_ref.at[side])

    pair_body(list_ref, count_ref, get_source, get_target, force_ref, *scratch)


def second_kernel(
    codes_ref,
    list_ref,
    count_ref,
    all_ref,
    g0,
    g1,
    g2,
    g3,
    chip_ref,
    vel_ref,
    near_ref,
    chip_vel_ref,
    force_ref,
    chip_x_ref,
    *scratch,
):
    x_index = codes_ref[6, 2]
    top = vel_ref[0]
    for k in range(1, NDEV):
        top = jnp.maximum(top, vel_ref[k])
    top = jnp.max(top[6:7], axis=1, keepdims=True)
    step = STEP_LENGTH / (jnp.sqrt(top) + EPSILON)
    row = sublane()
    group = (g0, g1, g2, g3)

    def get_source(k):
        if isinstance(k, int):
            if k == NDEV + NX:
                return no_source()
            shift = k - NDEV
            x_tile, l_tile, b_tile = tiles_of(group[shift])
            moved = near_ref[lax.bitwise_and(x_index - shift, NX - 1)]
        else:
            x_tile, l_tile, b_tile = tiles_of(all_ref.at[k])
            moved = vel_ref[k]
        return x_tile + step * moved, l_tile, b_tile

    for side in range(NC):
        moved = jnp.where(row < 6, chip_vel_ref[side], 0.0)
        chip_x_ref[side] = chip_ref[side, 0:8] + step * moved

    def get_target(side):
        return chip_x_ref[side], chip_ref[side, 8:16], chip_ref[side, 16:24]

    pair_body(list_ref, count_ref, get_source, get_target, force_ref, *scratch)


def finish_kernel(last, codes_ref, stress_ref, parts_ref, chip_ref, x_ref, vel_ref, out_ref):
    core = codes_ref[6, 0]
    row = sublane()
    lane = lax.broadcasted_iota(jnp.int32, (8, SEG), 1)
    tops = []
    tiles = []
    for side in range(NC):
        x_tile = x_ref[side, 0:8]
        l_tile = chip_ref[side, 8:16]
        b_tile = chip_ref[side, 16:24]
        rows = []
        for block in range(2):
            b = [b_tile[3 * block + a : 3 * block + a + 1] for a in range(3)]
            line = [l_tile[3 * block + a : 3 * block + a + 1] for a in range(3)]
            pulled = [
                stress_ref[a, 0] * b[0] + stress_ref[a, 1] * b[1] + stress_ref[a, 2] * b[2]
                for a in range(3)
            ]
            rows.append(pulled[1] * line[2] - pulled[2] * line[1])
            rows.append(pulled[2] * line[0] - pulled[0] * line[2])
            rows.append(pulled[0] * line[1] - pulled[1] * line[0])
        rows.append(jnp.zeros((2, SEG), F32))
        applied = jnp.concatenate(rows, axis=0)
        left = jnp.where(lane == 0, x_tile, pltpu.roll(x_tile, 1, 1))
        right = jnp.where(lane == SEG - 1, x_tile, pltpu.roll(x_tile, SEG - 1, 1))
        chain = left + right - 2.0 * x_tile
        pair = parts_ref[0, side] + parts_ref[1, side]
        drag = jnp.where(row < 3, b_tile[6:7], b_tile[7:8])
        velocity = (COUPLE * pair + applied + TENSION * chain) / drag
        speed = velocity * velocity
        tops.append(
            jnp.maximum(
                speed[0:1] + speed[1:2] + speed[2:3], speed[3:4] + speed[4:5] + speed[5:6]
            )
        )
        tiles.append(velocity)
    top = jnp.maximum(tops[0], tops[1])
    for side in range(NC):
        vel_ref[side] = jnp.where(row < 6, tiles[side], jnp.where(row == 6, top, 0.0))
    if last:
        out_ref[...] = jnp.broadcast_to(top[None], out_ref.shape)
    else:
        mine = vel_ref[core]
        for peer in range(NX):
            out_ref[peer] = mine


def pack_kernel(seg_ref, drag_ref, send_ref, part_ref, raw_ref, out_ref):
    raw_ref[...] = jnp.zeros((24, SEG), F32)
    for block in range(2):
        for comp in range(3):
            for tile in range(3):
                raw_ref[8 * tile + 3 * block + comp, :] = seg_ref[3 * tile + comp, block, :]
        raw_ref[22 + block, :] = drag_ref[block, :]
    raw_ref[14, :] = send_ref[0, :].astype(F32)
    raw_ref[15, :] = part_ref[0, :].astype(F32)
    raw = raw_ref[...]
    for peer in range(NZ):
        out_ref[peer] = raw


def relay_kernel(codes_ref, near_ref, out_ref):
    x_index = codes_ref[6, 2]
    top = near_ref[0]
    for x in range(1, NX):
        top = jnp.maximum(top, near_ref[x])
    tile = jnp.where(sublane() == 6, top, near_ref[x_index])
    for peer in range(NZ):
        out_ref[peer] = tile


def last_kernel(codes_ref, top_ref, x_ref, vel_ref, pos_out, vel_out):
    core = codes_ref[6, 0]
    top = jnp.max(jnp.max(top_ref[...], axis=0), axis=1, keepdims=True)
    step = STEP_LENGTH / (jnp.sqrt(top) + EPSILON)
    velocity = vel_ref[core]
    moved = x_ref[core] + step * velocity
    for block in range(2):
        for comp in range(3):
            pos_out[comp, block, :] = moved[3 * block + comp]
            vel_out[comp, block, :] = velocity[3 * block + comp]


SMEM = pl.BlockSpec(memory_space=pltpu.SMEM)
VMEM = pl.BlockSpec(memory_space=pltpu.VMEM)


def shape(*dims, dtype=F32):
    return jax.ShapeDtypeStruct(dims, dtype)


def call(kernel, name, operands, outs, smem_in=0, smem_out=0, scratch=(), mib=4):
    return pl.pallas_call(
        kernel,
        name=name,
        in_specs=[SMEM] * smem_in + [VMEM] * (len(operands) - smem_in),
        out_specs=[VMEM] * (len(outs) - smem_out) + [SMEM] * smem_out,
        out_shape=outs,
        scratch_shapes=scratch,
        compiler_params=pltpu.CompilerParams(vmem_limit_bytes=mib << 20),
    )(*operands)


def pass_x(value, shift):
    return lax.ppermute(value, "x", [(i, (i + shift) % NX) for i in range(NX)])


def exchange(value, axes):
    return lax.all_to_all(value, axes, 0, 0, tiled=True)


def local(segments, stress, drag_coef, send_ids, partner_ids):
    core = lax.axis_index("c")
    y_index = lax.axis_index("y")
    x_index = lax.axis_index("x")
    chip_index = y_index * NZ + lax.axis_index("z")
    raw, to_z = call(
        pack_kernel,
        "pack",
        (
            segments.transpose(1, 0, 2),
            drag_coef,
            send_ids.reshape(1, SEG),
            partner_ids.reshape(1, SEG),
        ),
        [shape(24, SEG), shape(NZ, 24, SEG)],
        mib=56,
    )
    along_z = exchange(to_z, "z")
    chip = lax.all_gather(raw, "c", axis=0)
    near1 = pass_x(raw, 1)
    along_z, chip, near1, raw = lax.optimization_barrier((along_z, chip, near1, raw))
    group = [raw, near1, pass_x(raw, 2), pass_x(raw, 3)]
    everyone = exchange(
        jnp.broadcast_to(along_z.reshape(1, NZ * 24, SEG), (NY, NZ * 24, SEG)), "y"
    ).reshape(NDEV, 24, SEG)

    lists = everyone[:, 14:16].reshape(2 * NDEV, SEG)
    lane = lax.broadcasted_iota(jnp.int32, (NC, SEG), 1)
    side = lax.broadcasted_iota(jnp.int32, (NC, SEG), 0)
    even = lax.bitwise_and(lane, SEG - 2)
    pick = (lane == 2 * chip_index + side).astype(F32)
    incoming = lax.dot_general(
        pick, lists, (((1,), (1,)), ((), ())), precision=lax.Precision.HIGHEST
    ).astype(jnp.int32)
    partner = jnp.concatenate([incoming[:, 1:], incoming[:, :1]], axis=1)
    into = jnp.where(incoming >= 0, even + incoming + 256 * (2 * side + partner), -1)
    sent = chip[:, 14].astype(jnp.int32)
    other = chip[:, 15].astype(jnp.int32)
    out = jnp.where(sent >= 0, even + other + 256 * (2 * side + sent), -1)
    first = lane[0:1]
    where = jnp.where(first == 0, core, jnp.where(first == 1, y_index, x_index))
    zero = jnp.zeros((1, SEG), jnp.int32)
    codes = jnp.concatenate([into, out, zero, zero, where, zero], axis=0)

    force, items, count = call(
        first_kernel,
        "first_pairs",
        (codes, everyone, *group, chip),
        [
            shape(NC, 8, SEG),
            shape(1, LIST, dtype=jnp.int32),
            shape(1, 1, dtype=jnp.int32),
        ],
        smem_in=1,
        smem_out=2,
        scratch=SCRATCH,
        mib=16,
    )
    chip_vel, to_near = call(
        functools.partial(finish_kernel, False),
        "finish",
        (codes, stress, lax.all_gather(force, "c", axis=0), chip, chip),
        [shape(NC, 8, SEG), shape(NX, 8, SEG)],
        smem_in=2,
    )
    near = exchange(to_near, "x")
    (to_z,) = call(relay_kernel, "relay", (codes, near), [shape(NZ, 8, SEG)], smem_in=1)
    along_z = exchange(to_z, "z").reshape(1, NZ * 8, SEG)
    vel_all = exchange(jnp.broadcast_to(along_z, (NY, NZ * 8, SEG)), "y").reshape(NDEV, 8, SEG)

    force, position = call(
        second_kernel,
        "second_pairs",
        (codes, items, count, everyone, *group, chip, vel_all, near, chip_vel),
        [shape(NC, 8, SEG), shape(NC, 8, SEG)],
        smem_in=3,
        scratch=SCRATCH,
        mib=16,
    )
    chip_vel, to_all = call(
        functools.partial(finish_kernel, True),
        "finish_last",
        (codes, stress, lax.all_gather(force, "c", axis=0), chip, position),
        [shape(NC, 8, SEG), shape(NDEV * NX, 1, SEG)],
        smem_in=2,
    )
    tops = exchange(to_all, ("y", "z", "x"))
    positions, velocity = call(
        last_kernel,
        "last",
        (codes, tops, position, chip_vel),
        [shape(3, 2, SEG), shape(3, 2, SEG)],
        smem_in=1,
    )
    return positions.transpose(1, 0, 2), velocity.transpose(1, 0, 2)


def solution(mesh):
    split = Mesh(
        mesh.devices.reshape(NY, NZ, NC, mesh.shape["sub"]), ("y", "z", "c", "x")
    )
    return jax.shard_map(
        local,
        mesh=split,
        in_specs=(
            P(DOM_SUB, None, None),
            P(),
            P(DOM_SUB, None),
            P(DOM_SUB, None, None),
            P(DOM_SUB, None, None),
        ),
        out_specs=(P(DOM_SUB, None, None), P(DOM_SUB, None, None)),
        check_vma=False,
    )
```

```python
import functools

import jax
import jax.numpy as jnp
from jax import lax
from jax.experimental import pallas as pl
from jax.experimental.pallas import tpu as pltpu
from jax.sharding import Mesh
from jax.sharding import PartitionSpec as P

NY, NZ, NC = 4, 16, 2
DOM = ("y", "z", "c")
DOM_SUB = ("y", "z", "c", "x")

COUPLE = 0.0625
CORE_SQUARE = 0.5
TENSION = 0.25
STEP_LENGTH = 1.0
EPSILON = 1e-06

SEG = 128
NT = NY * NC
NX = 4
BATCH = 16
LIST = 320
NONE = NZ + NX
F32 = jnp.float32
BF16 = jnp.bfloat16


def sublane(shape=(8, SEG)):
    return lax.broadcasted_iota(jnp.int32, shape, len(shape) - 2)


def up(value, count):
    return jnp.concatenate([value[count:], value[:count]], axis=0)


def split2(value):
    high = value.astype(BF16).astype(F32)
    return high, value - high


def split3(value):
    high, rest = split2(value)
    mid, low = split2(rest)
    return high, mid, low


def source_operands(x_tile, l_tile, b_tile):
    row = sublane()
    x_tile = jnp.where(row < 6, x_tile, 0.0)
    square = x_tile * x_tile
    norm0 = square[0:1] + square[1:2] + square[2:3] + CORE_SQUARE
    norm1 = square[3:4] + square[4:5] + square[5:6] + CORE_SQUARE
    full = jnp.where(row == 6, norm0, jnp.where(row == 7, norm1, x_tile))
    high, mid, low = split3(full)
    dist = [high, mid, high, mid, low, high, jnp.ones_like(high)]
    prod = [jnp.where(row < 3, b_tile[a : a + 1], b_tile[3 + a : 4 + a]) * l_tile for a in range(3)]
    parts = [split2(p) for p in prod]
    highs = [p[0] for p in parts]
    mids = [p[1] for p in parts]
    weight = highs + highs + mids
    flag = jnp.where(row == 6, 1.0, 0.0)
    first = (jnp.where(row < 6, high, flag), jnp.where(row < 6, mid, 0.0))
    second = (jnp.where(row < 3, up(high, 3), flag), jnp.where(row < 3, up(mid, 3), 0.0))
    return dist + weight, first, second


def store_rows(ref, index, tiles):
    for at in range(0, len(tiles), 2):
        pair = jnp.concatenate([tiles[at], tiles[at + 1]], axis=0).astype(BF16)
        ref[index, 8 * at : 8 * at + 16, :] = pair


def target_rows(x_tile, l_tile, b_tile, block):
    row = sublane()

    def both(tile):
        if block == 0:
            return jnp.where(row < 3, tile, jnp.where(row < 6, up(tile, 5), 0.0))
        return jnp.where(row < 3, up(tile, 3), jnp.where(row < 6, tile, 0.0))

    x_both = both(x_tile)
    high, mid, low = split3(x_both)
    square = x_both * x_both
    norm = square[0:1] + square[1:2] + square[2:3]
    norm_h, norm_m, norm_l = split3(norm)
    unit = jnp.where(row >= 6, 1.0, 0.0)
    norms = jnp.where(
        row == 0, norm_h, jnp.where(row == 1, norm_m, jnp.where(row == 2, norm_l, 0.0))
    )
    zero = jnp.zeros_like(high)
    dist = [
        -2.0 * high + unit,
        -2.0 * high + unit,
        -2.0 * mid,
        -2.0 * mid,
        -2.0 * high + unit,
        -2.0 * low,
        norms,
    ]
    l_both = both(l_tile)
    base = 3 * block
    prod = [b_tile[base + a : base + a + 1] * l_both for a in range(3)]
    parts = [split2(p) for p in prod]
    highs = [p[0] for p in parts]
    mids = [p[1] for p in parts]
    weight = highs + mids + highs
    return jnp.concatenate(dist + [zero] * 9, axis=0), jnp.concatenate([zero] * 7 + weight, axis=0)


def build_list(codes_ref, info_ref, list_ref, count_ref):
    core, y_index, z_index = info_ref[8, 0], info_ref[8, 1], info_ref[8, 2]
    from_here = 32 * y_index + core

    def add(z, count):
        for t in range(NT):
            for code in (
                codes_ref[z, 2 * z_index + (32 * (t // NC) + t % NC)],
                info_ref[t, 2 * z + from_here],
            ):
                list_ref[0, count] = code
                count = count + (code >= 0).astype(jnp.int32)
        return count

    count = lax.fori_loop(0, NZ, add, jnp.int32(0))
    mine = 2 * (NC * y_index + core)
    for block in range(2):
        for j in range(2 * NX):
            list_ref[0, count + 2 * NX * block + j] = 256 * (mine + block) + 2 * NZ + j
    count = count + 4 * NX
    for j in range(BATCH):
        list_ref[0, count + j] = 2 * NONE
    count_ref[0, 0] = lax.div(count + (BATCH - 1), BATCH)


def pair_body(
    list_ref, count_ref, get_source, get_target, force_ref, source_s, moment_s, target_s, total_s
):
    def prepare(k):
        tiles, first, second = source_operands(*get_source(k))
        store_rows(source_s, k, tiles)
        moment_s[2 * k] = jnp.concatenate(first, axis=0).astype(BF16)
        moment_s[2 * k + 1] = jnp.concatenate(second, axis=0).astype(BF16)

    def prepare_loop(k, carry):
        prepare(k)
        return carry

    lax.fori_loop(0, NZ, prepare_loop, 0, unroll=4)
    for k in range(NZ, NONE + 1):
        prepare(k)

    lane = lax.broadcasted_iota(jnp.int32, (SEG, SEG), 1)
    place = lax.bitwise_and(lane, 7)

    def target_loop(t, carry):
        x_tile, l_tile, b_tile = get_target(t)
        for block in range(2):
            dist, weight = target_rows(x_tile, l_tile, b_tile, block)
            dist = dist.T
            weight = weight.T
            for j in range(2):
                mine = (place >= 3 * j) & (place < 3 * j + 3)
                keep = mine | (place == 6 + j) | (lane >= 48)
                at = 4 * t + 2 * block + j
                target_s[at, 0:SEG] = jnp.where(keep, dist, 0.0).astype(BF16)
                target_s[at, SEG : 2 * SEG] = jnp.where(mine, weight, 0.0).astype(BF16)
        return carry

    lax.fori_loop(0, NT, target_loop, 0, unroll=2)
    total_s[...] = jnp.zeros_like(total_s)

    def items(step, carry):
        sums = []
        for b in range(BATCH):
            code = list_ref[0, step * BATCH + b]
            n = lax.shift_right_logical(code, 8)
            m = lax.bitwise_and(code, 255)
            at = 2 * n + lax.bitwise_and(m, 1)
            both = jnp.dot(
                target_s[at], source_s[lax.shift_right_logical(m, 1)], preferred_element_type=F32
            )
            inverse = lax.rsqrt(both[0:SEG])
            w = both[SEG : 2 * SEG] * (inverse * inverse * inverse)
            high = w.astype(BF16)
            low = (w - high.astype(F32)).astype(BF16)
            moment = moment_s[m]
            total = lax.dot_general(
                jnp.concatenate([moment, moment], axis=1),
                jnp.concatenate([high, low], axis=1),
                (((1,), (1,)), ((), ())),
                preferred_element_type=F32,
            )
            sums.append((n, total))
        for n, total in sums:
            total_s[n] += total
        return carry

    lax.fori_loop(0, count_ref[0, 0], items, 0)
    for t in range(NT):
        x_tile = get_target(t)[0]
        rows = []
        for block in range(2):
            total = total_s[2 * t + block]
            x_block = x_tile[3 * block : 3 * block + 3]
            rows.append(x_block * total[6:7] - (total[0:3] + total[8:11]))
        rows.append(jnp.zeros((2, SEG), F32))
        force = jnp.concatenate(rows, axis=0)
        for core in range(NC):
            force_ref[NC * (t // NC) + core, t % NC] = force


SCRATCH = [
    pltpu.VMEM((NONE + 1, SEG, SEG), BF16),
    pltpu.VMEM((2 * (NONE + 1), 16, SEG), BF16),
    pltpu.VMEM((4 * NT, 2 * SEG, SEG), BF16),
    pltpu.VMEM((2 * NT, 16, SEG), F32),
]


def tiles_of(tile):
    return tile[0:8], tile[8:16], tile[16:24]


def no_source():
    zero = jnp.zeros((8, SEG), F32)
    return zero, zero, zero


def first_kernel(
    codes_ref, info_ref, line_ref, group_ref, near_ref, force_ref, list_ref, count_ref, *scratch
):
    build_list(codes_ref, info_ref, list_ref, count_ref)

    def get_source(k):
        if isinstance(k, int):
            return no_source() if k == NONE else tiles_of(group_ref.at[k - NZ])
        return tiles_of(line_ref.at[k])

    def get_target(t):
        return tiles_of(near_ref.at[t])

    pair_body(list_ref, count_ref, get_source, get_target, force_ref, *scratch)


def second_kernel(
    info_ref,
    list_ref,
    count_ref,
    line_ref,
    group_ref,
    near_ref,
    vel_ref,
    near_vel_ref,
    force_ref,
    position_ref,
    *scratch,
):
    mine = NC * info_ref[8, 1] + info_ref[8, 0]
    x_index = info_ref[8, 3]
    top = vel_ref[0]
    for z in range(1, NZ):
        top = jnp.maximum(top, vel_ref[z])
    top = jnp.max(top[6:7], axis=1, keepdims=True)
    step = STEP_LENGTH / (jnp.sqrt(top) + EPSILON)

    def get_source(k):
        if isinstance(k, int):
            if k == NONE:
                return no_source()
            x_tile, l_tile, b_tile = tiles_of(group_ref.at[k - NZ])
            moved = near_vel_ref[mine, k - NZ]
        else:
            x_tile, l_tile, b_tile = tiles_of(line_ref.at[k])
            moved = vel_ref[k]
        return x_tile + step * moved, l_tile, b_tile

    def get_target(t):
        x_tile, l_tile, b_tile = tiles_of(near_ref.at[t])
        return x_tile + step * near_vel_ref[t, x_index], l_tile, b_tile

    for side in range(NC):
        at = NC * info_ref[8, 1] + side
        moved = jnp.where(sublane() < 6, near_vel_ref[at, x_index], 0.0)
        position_ref[side] = near_ref[at, 0:8] + step * moved
    pair_body(list_ref, count_ref, get_source, get_target, force_ref, *scratch)


def finish_kernel(info_ref, stress_ref, parts_ref, near_ref, x_ref, vel_ref, out_ref):
    core, y_index = info_ref[8, 0], info_ref[8, 1]
    row = sublane()
    lane = lax.broadcasted_iota(jnp.int32, (8, SEG), 1)
    tops = []
    for side in range(NC):
        at = NC * y_index + side
        x_tile = x_ref[at, 0:8] if x_ref.shape[0] == NT else x_ref[side]
        l_tile = near_ref[at, 8:16]
        b_tile = near_ref[at, 16:24]
        rows = []
        for block in range(2):
            b = [b_tile[3 * block + a : 3 * block + a + 1] for a in range(3)]
            line = [l_tile[3 * block + a : 3 * block + a + 1] for a in range(3)]
            pulled = [
                stress_ref[a, 0] * b[0] + stress_ref[a, 1] * b[1] + stress_ref[a, 2] * b[2]
                for a in range(3)
            ]
            rows.append(pulled[1] * line[2] - pulled[2] * line[1])
            rows.append(pulled[2] * line[0] - pulled[0] * line[2])
            rows.append(pulled[0] * line[1] - pulled[1] * line[0])
        rows.append(jnp.zeros((2, SEG), F32))
        applied = jnp.concatenate(rows, axis=0)
        left = jnp.where(lane == 0, x_tile, pltpu.roll(x_tile, 1, 1))
        right = jnp.where(lane == SEG - 1, x_tile, pltpu.roll(x_tile, SEG - 1, 1))
        chain = left + right - 2.0 * x_tile
        pair = parts_ref[0, side]
        for part in range(1, NT):
            pair = pair + parts_ref[part, side]
        drag = jnp.where(row < 3, b_tile[6:7], b_tile[7:8])
        velocity = (COUPLE * pair + applied + TENSION * chain) / drag
        speed = velocity * velocity
        tops.append(
            jnp.maximum(
                speed[0:1] + speed[1:2] + speed[2:3], speed[3:4] + speed[4:5] + speed[5:6]
            )
        )

        @pl.when(core == side)
        def _(velocity=velocity):
            vel_ref[...] = velocity

    top = jnp.maximum(tops[0], tops[1])
    tile = jnp.where(row < 6, vel_ref[...], jnp.where(row == 6, top, 0.0))
    vel_ref[...] = tile
    send = top if out_ref.shape[1] == 1 else tile
    out_ref[...] = jnp.broadcast_to(send[None], out_ref.shape)


def pack_kernel(seg_ref, drag_ref, send_ref, part_ref, raw_ref, out_ref):
    raw_ref[...] = jnp.zeros((24, SEG), F32)
    for block in range(2):
        for comp in range(3):
            for tile in range(3):
                raw_ref[8 * tile + 3 * block + comp, :] = seg_ref[3 * tile + comp, block, :]
        raw_ref[22 + block, :] = drag_ref[block, :]
    raw_ref[14, :] = send_ref[0, :].astype(F32)
    raw_ref[15, :] = part_ref[0, :].astype(F32)
    raw = raw_ref[...]
    for peer in range(NZ):
        out_ref[peer] = raw


def relay_kernel(near_ref, vel_ref, out_ref):
    top = near_ref[0]
    for at in range(1, NT * NX):
        top = jnp.maximum(top, near_ref[at])
    tile = jnp.where(sublane() == 6, top, vel_ref[...])
    out_ref[...] = jnp.broadcast_to(tile[None], out_ref.shape)


def last_kernel(info_ref, top_ref, x_ref, vel_ref, pos_out, vel_out):
    top = jnp.max(jnp.max(top_ref[...], axis=0), axis=1, keepdims=True)
    step = STEP_LENGTH / (jnp.sqrt(top) + EPSILON)
    velocity = vel_ref[...]
    moved = x_ref[info_ref[8, 0]] + step * velocity
    for block in range(2):
        for comp in range(3):
            pos_out[comp, block, :] = moved[3 * block + comp]
            vel_out[comp, block, :] = velocity[3 * block + comp]


SMEM = pl.BlockSpec(memory_space=pltpu.SMEM)
VMEM = pl.BlockSpec(memory_space=pltpu.VMEM)


def shape(*dims, dtype=F32):
    return jax.ShapeDtypeStruct(dims, dtype)


def call(kernel, name, operands, outs, smem_in=0, smem_out=0, scratch=(), mib=4):
    return pl.pallas_call(
        kernel,
        name=name,
        in_specs=[SMEM] * smem_in + [VMEM] * (len(operands) - smem_in),
        out_specs=[VMEM] * (len(outs) - smem_out) + [SMEM] * smem_out,
        out_shape=outs,
        scratch_shapes=scratch,
        compiler_params=pltpu.CompilerParams(vmem_limit_bytes=mib << 20),
    )(*operands)


def exchange(value, axes):
    return lax.all_to_all(value, axes, 0, 0, tiled=True)


def local(segments, stress, drag_coef, send_ids, partner_ids):
    raw, to_z = call(
        pack_kernel,
        "pack",
        (
            segments.transpose(1, 0, 2),
            drag_coef,
            send_ids.reshape(1, SEG),
            partner_ids.reshape(1, SEG),
        ),
        [shape(24, SEG), shape(NZ, 24, SEG)],
        mib=56,
    )
    line = exchange(to_z, "z")
    near = lax.all_gather(raw, ("y", "c"), axis=0)
    group = lax.all_gather(raw, "x", axis=0)
    line, near, group = lax.optimization_barrier((line, near, group))

    sent = line[:, 14].astype(jnp.int32)
    part = line[:, 15].astype(jnp.int32)
    z_row = lax.broadcasted_iota(jnp.int32, (NZ, SEG), 0)
    peer = lax.broadcasted_iota(jnp.int32, (NZ, SEG), 1)
    target = 2 * lax.shift_right_logical(peer, 5) + lax.bitwise_and(peer, 1)
    codes = jnp.where(sent >= 0, 2 * z_row + sent + 256 * (2 * target + part), -1)
    mine = near[:, 14].astype(jnp.int32)
    other = near[:, 15].astype(jnp.int32)
    row = lax.broadcasted_iota(jnp.int32, (NT, SEG), 0)
    lane = lax.broadcasted_iota(jnp.int32, (NT, SEG), 1)
    z_lane = lax.bitwise_and(lax.shift_right_logical(lane, 1), NZ - 1)
    out = jnp.where(mine >= 0, 2 * z_lane + other + 256 * (2 * row + mine), -1)
    place = jnp.zeros((NT, SEG), jnp.int32)
    for at, axis in enumerate(("c", "y", "z", "x")):
        place = jnp.where(lane == at, lax.axis_index(axis), place)
    info = jnp.concatenate([out, place], axis=0)

    force, items, count = call(
        first_kernel,
        "first_pairs",
        (codes, info, line, group, near),
        [
            shape(NT, NC, 8, SEG),
            shape(1, LIST, dtype=jnp.int32),
            shape(1, 1, dtype=jnp.int32),
        ],
        smem_in=2,
        smem_out=2,
        scratch=SCRATCH,
        mib=16,
    )

    def finish(force, position, peers, name):
        return call(
            finish_kernel,
            name,
            (info, stress, exchange(force, ("y", "c")), near, position),
            [shape(8, SEG), shape(*peers, SEG)],
            smem_in=2,
        )

    velocity, to_near = finish(force, near, (NT * NX, 8), "finish")
    near_vel = exchange(to_near, ("y", "c", "x"))
    (to_z,) = call(relay_kernel, "relay", (near_vel, velocity), [shape(NZ, 8, SEG)])
    line_vel = exchange(to_z, "z")

    force, position = call(
        second_kernel,
        "second_pairs",
        (info, items, count, line, group, near, line_vel, near_vel.reshape(NT, NX, 8, SEG)),
        [shape(NT, NC, 8, SEG), shape(NC, 8, SEG)],
        smem_in=3,
        scratch=SCRATCH,
        mib=16,
    )
    velocity, to_all = finish(force, position, (NY * NZ * NX, 1), "finish_last")
    tops = exchange(to_all, ("y", "z", "x"))
    positions, velocity = call(
        last_kernel,
        "last",
        (info, tops, position, velocity),
        [shape(3, 2, SEG), shape(3, 2, SEG)],
        smem_in=1,
    )
    return positions.transpose(1, 0, 2), velocity.transpose(1, 0, 2)


def solution(mesh):
    split = Mesh(
        mesh.devices.reshape(NY, NZ, NC, mesh.shape["sub"]), ("y", "z", "c", "x")
    )
    return jax.shard_map(
        local,
        mesh=split,
        in_specs=(
            P(DOM_SUB, None, None),
            P(),
            P(DOM_SUB, None),
            P(DOM_SUB, None, None),
            P(DOM_SUB, None, None),
        ),
        out_specs=(P(DOM_SUB, None, None), P(DOM_SUB, None, None)),
        check_vma=False,
    )
```

```python
import functools

import jax
import jax.numpy as jnp
from jax import lax
from jax.experimental import pallas as pl
from jax.experimental.pallas import tpu as pltpu
from jax.sharding import Mesh
from jax.sharding import PartitionSpec as P

NY, NZ, NC = 4, 16, 2
DOM = ("y", "z", "c")
DOM_SUB = ("y", "z", "c", "x")

COUPLE = 0.0625
CORE_SQUARE = 0.5
TENSION = 0.25
STEP_LENGTH = 1.0
EPSILON = 1e-06

SEG = 128
NDEV = NY * NZ
NX = 4
BATCH = 32
LIST = 320
DUMMY = 2 * (NDEV + NX)
F32 = jnp.float32
BF16 = jnp.bfloat16


def sublane(shape=(8, SEG)):
    return lax.broadcasted_iota(jnp.int32, shape, len(shape) - 2)


def up(value, count):
    return jnp.concatenate([value[count:], value[:count]], axis=0)


def split2(value):
    high = value.astype(BF16).astype(F32)
    return high, value - high


def split3(value):
    high, rest = split2(value)
    mid, low = split2(rest)
    return high, mid, low


def source_operands(x_tile, l_tile, b_tile):
    row = sublane()
    x_tile = jnp.where(lax.bitwise_and(row, 3) < 3, x_tile, 0.0)
    square = x_tile * x_tile
    norm0 = square[0:1] + square[1:2] + square[2:3] + CORE_SQUARE
    norm1 = square[4:5] + square[5:6] + square[6:7] + CORE_SQUARE
    full = jnp.where(row == 3, norm0, jnp.where(row == 7, norm1, x_tile))
    high, mid, low = split3(full)
    dist = [high, mid, high, mid, low, high, jnp.ones_like(high)]
    burgers = [burgers_rows(l_tile, b_tile, block) for block in range(2)]
    prod = [jnp.where(row < 4, burgers[0][a], burgers[1][a]) * l_tile for a in range(3)]
    parts = [split2(p) for p in prod]
    highs = [p[0] for p in parts]
    mids = [p[1] for p in parts]
    weight = highs + highs + mids
    first = (jnp.where(row == 3, 1.0, high), jnp.where(row == 3, 0.0, mid))
    second = (jnp.where(row == 3, 1.0, up(high, 4)), jnp.where(row == 3, 0.0, up(mid, 4)))
    return dist + weight, first, second


def burgers_rows(l_tile, b_tile, block):
    return [
        l_tile[4 * block + 3 : 4 * block + 4],
        b_tile[2 * block : 2 * block + 1],
        b_tile[2 * block + 1 : 2 * block + 2],
    ]


def store_rows(ref, index, tiles):
    for at in range(0, len(tiles), 2):
        pair = jnp.concatenate([tiles[at], tiles[at + 1]], axis=0).astype(BF16)
        ref[index, 8 * at : 8 * at + 16, :] = pair


def target_rows(x_tile, l_tile, b_tile, block):
    row = sublane()

    def both(tile):
        other = up(tile, 4)
        own, far = (tile, other) if block == 0 else (other, tile)
        return jnp.where(lax.bitwise_and(row, 3) == 3, 0.0, jnp.where(row < 4, own, far))

    x_both = both(x_tile)
    high, mid, low = split3(x_both)
    square = x_both * x_both
    norm = square[0:1] + square[1:2] + square[2:3]
    norm_h, norm_m, norm_l = split3(norm)
    unit = jnp.where(lax.bitwise_and(row, 3) == 3, 1.0, 0.0)
    norms = jnp.where(
        row == 0, norm_h, jnp.where(row == 1, norm_m, jnp.where(row == 2, norm_l, 0.0))
    )
    zero = jnp.zeros_like(high)
    dist = [
        -2.0 * high + unit,
        -2.0 * high + unit,
        -2.0 * mid,
        -2.0 * mid,
        -2.0 * high + unit,
        -2.0 * low,
        norms,
    ]
    l_both = both(l_tile)
    prod = [b * l_both for b in burgers_rows(l_tile, b_tile, block)]
    parts = [split2(p) for p in prod]
    highs = [p[0] for p in parts]
    mids = [p[1] for p in parts]
    weight = highs + mids + highs
    return jnp.concatenate(dist + [zero] * 9, axis=0), jnp.concatenate([zero] * 7 + weight, axis=0)


def build_list(codes_ref, list_ref, count_ref):
    core = codes_ref[6, 0]

    def add(k, count):
        for line in range(2 * NC):
            code = codes_ref[line, 2 * k + core if line >= NC else 2 * k]
            list_ref[0, count] = code
            count = count + (code >= 0).astype(jnp.int32)
        return count

    count = lax.fori_loop(0, NDEV, add, jnp.int32(0), unroll=8)
    for block in range(2):
        for j in range(2 * NX):
            list_ref[0, count + 2 * NX * block + j] = 256 * (2 * core + block) + 2 * NDEV + j
    count = count + 4 * NX
    for j in range(BATCH):
        list_ref[0, count + j] = DUMMY
    count_ref[0, 0] = lax.div(count + (BATCH - 1), BATCH)


def pair_body(list_ref, count_ref, get_source, get_target, force_ref, source_s, moment_s, target_s):
    def prepare(k):
        tiles, first, second = source_operands(*get_source(k))
        store_rows(source_s, k, tiles)
        moment_s[2 * k] = jnp.concatenate(first, axis=0).astype(BF16)
        moment_s[2 * k + 1] = jnp.concatenate(second, axis=0).astype(BF16)

    def prepare_loop(k, carry):
        prepare(k)
        return carry

    lax.fori_loop(0, NDEV, prepare_loop, 0, unroll=4)
    for k in range(NDEV, NDEV + NX + 1):
        prepare(k)

    lane = lax.broadcasted_iota(jnp.int32, (SEG, SEG), 1)
    place = lax.bitwise_and(lane, 7)
    for side in range(NC):
        x_tile, l_tile, b_tile = get_target(side)
        for block in range(2):
            dist, weight = target_rows(x_tile, l_tile, b_tile, block)
            dist = dist.T
            weight = weight.T
            for j in range(2):
                mine = (place >= 4 * j) & (place < 4 * j + 3)
                keep = mine | (place == 4 * j + 3) | (lane >= 48)
                at = 2 * (2 * side + block) + j
                target_s[at, 0:SEG] = jnp.where(keep, dist, 0.0).astype(BF16)
                target_s[at, SEG : 2 * SEG] = jnp.where(mine, weight, 0.0).astype(BF16)

    def items(step, total):
        lows, highs, moments = [], [], []
        for b in range(BATCH):
            code = list_ref[0, step * BATCH + b]
            n = lax.shift_right_logical(code, 8)
            m = lax.bitwise_and(code, 255)
            at = 2 * n + lax.bitwise_and(m, 1)
            both = jnp.dot(
                target_s[at], source_s[lax.shift_right_logical(m, 1)], preferred_element_type=F32
            )
            inverse = lax.rsqrt(both[0:SEG])
            w = both[SEG : 2 * SEG] * (inverse * inverse * inverse)
            high = w.astype(BF16)
            highs.append(high)
            lows.append((w - high.astype(F32)).astype(BF16))
            moment = moment_s[m]
            zero = jnp.zeros_like(moment)
            moments.append(
                jnp.concatenate([jnp.where(n == t, moment, zero) for t in range(4)], axis=0)
            )
        lhs = jnp.concatenate(moments + moments, axis=1)
        rhs = jnp.concatenate(highs + lows, axis=1)
        return total + lax.dot_general(
            rhs, lhs, (((1,), (1,)), ((), ())), preferred_element_type=F32
        )

    total = lax.fori_loop(0, count_ref[0, 0], items, jnp.zeros((SEG, 64), F32))
    total = jnp.concatenate([total, jnp.zeros((SEG, SEG - 64), F32)], axis=1).T
    for side in range(NC):
        x_tile = get_target(side)[0]
        rows = []
        for block in range(2):
            at = 16 * (2 * side + block)
            x_block = x_tile[4 * block : 4 * block + 3]
            rows.append(
                x_block * total[at + 3 : at + 4] - (total[at : at + 3] + total[at + 8 : at + 11])
            )
            rows.append(jnp.zeros((1, SEG), F32))
        force_ref[side] = jnp.concatenate(rows, axis=0)


SCRATCH = [
    pltpu.VMEM((NDEV + NX + 1, SEG, SEG), BF16),
    pltpu.VMEM((2 * (NDEV + NX + 1), 16, SEG), BF16),
    pltpu.VMEM((8, 2 * SEG, SEG), BF16),
]


def tiles_of(tile):
    return tile[0:8], tile[8:16], tile[16:24]


def tiles_of_rows(rows):
    return (
        jnp.concatenate([rows[0], rows[1]], axis=0),
        jnp.concatenate([rows[2], rows[3]], axis=0),
        rows[4],
    )


def no_source():
    zero = jnp.zeros((8, SEG), F32)
    return zero, zero, zero


def first_kernel(codes_ref, all_ref, g0, g1, g2, g3, chip_ref, force_ref, list_ref, count_ref, *scratch):
    build_list(codes_ref, list_ref, count_ref)
    group = (g0, g1, g2, g3)

    def get_source(k):
        if isinstance(k, int):
            return no_source() if k == NDEV + NX else tiles_of(group[k - NDEV])
        return tiles_of_rows(all_ref.at[k])

    def get_target(side):
        return tiles_of(chip_ref.at[side])

    pair_body(list_ref, count_ref, get_source, get_target, force_ref, *scratch)


def second_kernel(
    codes_ref,
    list_ref,
    count_ref,
    all_ref,
    g0,
    g1,
    g2,
    g3,
    chip_ref,
    vel_ref,
    near_ref,
    chip_vel_ref,
    force_ref,
    chip_x_ref,
    *scratch,
):
    x_index = codes_ref[6, 2]
    top = vel_ref[0]
    for k in range(1, NDEV):
        top = jnp.maximum(top, vel_ref[k])
    top = jnp.max(top[3:4], axis=1, keepdims=True)
    step = STEP_LENGTH / (jnp.sqrt(top) + EPSILON)
    row = sublane()
    group = (g0, g1, g2, g3)

    def get_source(k):
        if isinstance(k, int):
            if k == NDEV + NX:
                return no_source()
            shift = k - NDEV
            x_tile, l_tile, b_tile = tiles_of(group[shift])
            moved = near_ref[lax.bitwise_and(x_index - shift, NX - 1)]
        else:
            x_tile, l_tile, b_tile = tiles_of_rows(all_ref.at[k])
            moved = vel_ref[k]
        return x_tile + step * moved, l_tile, b_tile

    for side in range(NC):
        moved = jnp.where(row == 3, 0.0, chip_vel_ref[side])
        chip_x_ref[side] = chip_ref[side, 0:8] + step * moved

    def get_target(side):
        return chip_x_ref[side], chip_ref[side, 8:16], chip_ref[side, 16:24]

    pair_body(list_ref, count_ref, get_source, get_target, force_ref, *scratch)


def finish_kernel(last, codes_ref, stress_ref, parts_ref, chip_ref, x_ref, vel_ref, out_ref):
    core = codes_ref[6, 0]
    row = sublane()
    lane = lax.broadcasted_iota(jnp.int32, (8, SEG), 1)
    tops = []
    tiles = []
    for side in range(NC):
        x_tile = x_ref[side, 0:8]
        l_tile = chip_ref[side, 8:16]
        b_tile = chip_ref[side, 16:24]
        rows = []
        for block in range(2):
            b = burgers_rows(l_tile, b_tile, block)
            line = [l_tile[4 * block + a : 4 * block + a + 1] for a in range(3)]
            pulled = [
                stress_ref[a, 0] * b[0] + stress_ref[a, 1] * b[1] + stress_ref[a, 2] * b[2]
                for a in range(3)
            ]
            rows.append(pulled[1] * line[2] - pulled[2] * line[1])
            rows.append(pulled[2] * line[0] - pulled[0] * line[2])
            rows.append(pulled[0] * line[1] - pulled[1] * line[0])
            rows.append(jnp.zeros((1, SEG), F32))
        applied = jnp.concatenate(rows, axis=0)
        left = jnp.where(lane == 0, x_tile, pltpu.roll(x_tile, 1, 1))
        right = jnp.where(lane == SEG - 1, x_tile, pltpu.roll(x_tile, SEG - 1, 1))
        chain = left + right - 2.0 * x_tile
        pair = parts_ref[0, side] + parts_ref[1, side]
        drag = jnp.where(row < 4, b_tile[4:5], b_tile[5:6])
        velocity = (COUPLE * pair + applied + TENSION * chain) / drag
        speed = velocity * velocity
        tops.append(
            jnp.maximum(
                speed[0:1] + speed[1:2] + speed[2:3], speed[4:5] + speed[5:6] + speed[6:7]
            )
        )
        tiles.append(velocity)
    top = jnp.maximum(tops[0], tops[1])
    for side in range(NC):
        vel_ref[side] = jnp.where(row == 3, top, jnp.where(row == 7, 0.0, tiles[side]))
    if last:
        out_ref[...] = jnp.broadcast_to(top[None], out_ref.shape)
    else:
        mine = vel_ref[core]
        for peer in range(NX):
            out_ref[peer] = mine


def pack_kernel(seg_ref, drag_ref, send_ref, part_ref, raw_ref, out_ref):
    raw_ref[...] = jnp.zeros((24, SEG), F32)
    for block in range(2):
        for comp in range(3):
            raw_ref[4 * block + comp, :] = seg_ref[comp, block, :]
            raw_ref[8 + 4 * block + comp, :] = seg_ref[3 + comp, block, :]
        raw_ref[11 + 4 * block, :] = seg_ref[6, block, :]
        raw_ref[16 + 2 * block, :] = seg_ref[7, block, :]
        raw_ref[17 + 2 * block, :] = seg_ref[8, block, :]
        raw_ref[20 + block, :] = drag_ref[block, :]
    raw_ref[3, :] = send_ref[0, :].astype(F32)
    raw_ref[7, :] = part_ref[0, :].astype(F32)
    for at in range(5):
        rows = raw_ref[4 * at : 4 * at + 4, :]
        for peer in range(NZ):
            out_ref[peer, at] = rows


def relay_kernel(codes_ref, near_ref, out_ref):
    x_index = codes_ref[6, 2]
    top = near_ref[0]
    for x in range(1, NX):
        top = jnp.maximum(top, near_ref[x])
    tile = jnp.where(sublane() == 3, top, near_ref[x_index])
    for peer in range(NZ):
        out_ref[peer] = tile


def last_kernel(codes_ref, top_ref, x_ref, vel_ref, pos_out, vel_out):
    core = codes_ref[6, 0]
    top = jnp.max(jnp.max(top_ref[...], axis=0), axis=1, keepdims=True)
    step = STEP_LENGTH / (jnp.sqrt(top) + EPSILON)
    velocity = vel_ref[core]
    moved = x_ref[core] + step * velocity
    for block in range(2):
        for comp in range(3):
            pos_out[comp, block, :] = moved[4 * block + comp]
            vel_out[comp, block, :] = velocity[4 * block + comp]


SMEM = pl.BlockSpec(memory_space=pltpu.SMEM)
VMEM = pl.BlockSpec(memory_space=pltpu.VMEM)


def shape(*dims, dtype=F32):
    return jax.ShapeDtypeStruct(dims, dtype)


def call(kernel, name, operands, outs, smem_in=0, smem_out=0, scratch=(), mib=4):
    return pl.pallas_call(
        kernel,
        name=name,
        in_specs=[SMEM] * smem_in + [VMEM] * (len(operands) - smem_in),
        out_specs=[VMEM] * (len(outs) - smem_out) + [SMEM] * smem_out,
        out_shape=outs,
        scratch_shapes=scratch,
        compiler_params=pltpu.CompilerParams(vmem_limit_bytes=mib << 20),
    )(*operands)


def pass_x(value, shift):
    return lax.ppermute(value, "x", [(i, (i + shift) % NX) for i in range(NX)])


def exchange(value, axes):
    return lax.all_to_all(value, axes, 0, 0, tiled=True)


def local(segments, stress, drag_coef, send_ids, partner_ids):
    core = lax.axis_index("c")
    y_index = lax.axis_index("y")
    x_index = lax.axis_index("x")
    chip_index = y_index * NZ + lax.axis_index("z")
    raw, to_z = call(
        pack_kernel,
        "pack",
        (
            segments.transpose(1, 0, 2),
            drag_coef,
            send_ids.reshape(1, SEG),
            partner_ids.reshape(1, SEG),
        ),
        [shape(24, SEG), shape(NZ, 5, 4, SEG)],
        mib=56,
    )
    along_z = exchange(to_z, "z")
    chip = lax.all_gather(raw, "c", axis=0)
    group = [raw] + [pass_x(raw, shift) for shift in range(1, NX)]

    lane = lax.broadcasted_iota(jnp.int32, (NC, SEG), 1)
    side = lax.broadcasted_iota(jnp.int32, (NC, SEG), 0)
    even = lax.bitwise_and(lane, SEG - 2)
    sent = chip[:, 3].astype(jnp.int32)
    other = chip[:, 7].astype(jnp.int32)
    out = jnp.where(sent >= 0, even + other + 256 * (2 * side + sent), -1)
    first = lane[0:1]
    where = jnp.where(first == 0, core, jnp.where(first == 1, y_index, x_index))
    zero = jnp.zeros((1, SEG), jnp.int32)
    known = jnp.concatenate([out, zero, zero, where, zero], axis=0)
    pick = (lane == 2 * chip_index + side).astype(F32)

    everyone = exchange(
        jnp.broadcast_to(along_z.reshape(1, NZ * 5, 4, SEG), (NY, NZ * 5, 4, SEG)), "y"
    ).reshape(NDEV, 5, 4, SEG)
    lists = everyone[:, 0:2, 3].reshape(2 * NDEV, SEG)
    incoming = lax.dot_general(
        pick, lists, (((1,), (1,)), ((), ())), precision=lax.Precision.HIGHEST
    ).astype(jnp.int32)
    partner = jnp.concatenate([incoming[:, 1:], incoming[:, :1]], axis=1)
    into = jnp.where(incoming >= 0, even + incoming + 256 * (2 * side + partner), -1)
    codes = jnp.concatenate([into, known], axis=0)

    force, items, count = call(
        first_kernel,
        "first_pairs",
        (codes, everyone, *group, chip),
        [
            shape(NC, 8, SEG),
            shape(1, LIST, dtype=jnp.int32),
            shape(1, 1, dtype=jnp.int32),
        ],
        smem_in=1,
        smem_out=2,
        scratch=SCRATCH,
        mib=16,
    )
    chip_vel, to_near = call(
        functools.partial(finish_kernel, False),
        "finish",
        (codes, stress, lax.all_gather(force, "c", axis=0), chip, chip),
        [shape(NC, 8, SEG), shape(NX, 8, SEG)],
        smem_in=2,
    )
    near = exchange(to_near, "x")
    (to_z,) = call(relay_kernel, "relay", (codes, near), [shape(NZ, 8, SEG)], smem_in=1)
    along_z = exchange(to_z, "z").reshape(1, NZ * 8, SEG)
    vel_all = exchange(jnp.broadcast_to(along_z, (NY, NZ * 8, SEG)), "y").reshape(NDEV, 8, SEG)

    force, position = call(
        second_kernel,
        "second_pairs",
        (codes, items, count, everyone, *group, chip, vel_all, near, chip_vel),
        [shape(NC, 8, SEG), shape(NC, 8, SEG)],
        smem_in=3,
        scratch=SCRATCH,
        mib=16,
    )
    chip_vel, to_all = call(
        functools.partial(finish_kernel, True),
        "finish_last",
        (codes, stress, lax.all_gather(force, "c", axis=0), chip, position),
        [shape(NC, 8, SEG), shape(NDEV * NX, 1, SEG)],
        smem_in=2,
    )
    tops = exchange(to_all, ("y", "z", "x"))
    positions, velocity = call(
        last_kernel,
        "last",
        (codes, tops, position, chip_vel),
        [shape(3, 2, SEG), shape(3, 2, SEG)],
        smem_in=1,
    )
    return positions.transpose(1, 0, 2), velocity.transpose(1, 0, 2)


def solution(mesh):
    split = Mesh(
        mesh.devices.reshape(NY, NZ, NC, mesh.shape["sub"]), ("y", "z", "c", "x")
    )
    return jax.shard_map(
        local,
        mesh=split,
        in_specs=(
            P(DOM_SUB, None, None),
            P(),
            P(DOM_SUB, None),
            P(DOM_SUB, None, None),
            P(DOM_SUB, None, None),
        ),
        out_specs=(P(DOM_SUB, None, None), P(DOM_SUB, None, None)),
        check_vma=False,
    )
```

```python
import functools

import jax
import jax.numpy as jnp
from jax import lax
from jax.experimental import pallas as pl
from jax.experimental.pallas import tpu as pltpu
from jax.sharding import Mesh
from jax.sharding import PartitionSpec as P

NY, NZ, NC = 4, 16, 2
DOM = ("y", "z", "c")
DOM_SUB = ("y", "z", "c", "x")

COUPLE = 0.0625
CORE_SQUARE = 0.5
TENSION = 0.25
STEP_LENGTH = 1.0
EPSILON = 1e-06

SEG = 128
NDEV = NY * NZ
NX = 4
BATCH = 32
LIST = 320
DUMMY = 2 * (NDEV + NX)
F32 = jnp.float32
BF16 = jnp.bfloat16


def sublane(shape=(8, SEG)):
    return lax.broadcasted_iota(jnp.int32, shape, len(shape) - 2)


def up(value, count):
    return jnp.concatenate([value[count:], value[:count]], axis=0)


def split2(value):
    high = value.astype(BF16).astype(F32)
    return high, value - high


def split3(value):
    high, rest = split2(value)
    mid, low = split2(rest)
    return high, mid, low


def source_operands(x_tile, l_tile, b_tile):
    row = sublane()
    x_tile = jnp.where(lax.bitwise_and(row, 3) < 3, x_tile, 0.0)
    square = x_tile * x_tile
    norm0 = square[0:1] + square[1:2] + square[2:3] + CORE_SQUARE
    norm1 = square[4:5] + square[5:6] + square[6:7] + CORE_SQUARE
    full = jnp.where(row == 3, norm0, jnp.where(row == 7, norm1, x_tile))
    high, mid, low = split3(full)
    dist = [high, mid, high, mid, low, high, jnp.ones_like(high)]
    burgers = [burgers_rows(l_tile, b_tile, block) for block in range(2)]
    prod = [jnp.where(row < 4, burgers[0][a], burgers[1][a]) * l_tile for a in range(3)]
    parts = [split2(p) for p in prod]
    highs = [p[0] for p in parts]
    mids = [p[1] for p in parts]
    weight = highs + highs + mids
    first = (jnp.where(row == 3, 1.0, high), jnp.where(row == 3, 0.0, mid))
    second = (jnp.where(row == 3, 1.0, up(high, 4)), jnp.where(row == 3, 0.0, up(mid, 4)))
    return dist + weight, first, second


def burgers_rows(l_tile, b_tile, block):
    return [
        l_tile[4 * block + 3 : 4 * block + 4],
        b_tile[2 * block : 2 * block + 1],
        b_tile[2 * block + 1 : 2 * block + 2],
    ]


def store_rows(ref, index, tiles):
    for at in range(0, len(tiles), 2):
        pair = jnp.concatenate([tiles[at], tiles[at + 1]], axis=0).astype(BF16)
        ref[index, 8 * at : 8 * at + 16, :] = pair


def target_rows(x_tile, l_tile, b_tile, block):
    row = sublane()

    def both(tile):
        other = up(tile, 4)
        own, far = (tile, other) if block == 0 else (other, tile)
        return jnp.where(lax.bitwise_and(row, 3) == 3, 0.0, jnp.where(row < 4, own, far))

    x_both = both(x_tile)
    high, mid, low = split3(x_both)
    square = x_both * x_both
    norm = square[0:1] + square[1:2] + square[2:3]
    norm_h, norm_m, norm_l = split3(norm)
    unit = jnp.where(lax.bitwise_and(row, 3) == 3, 1.0, 0.0)
    norms = jnp.where(
        row == 0, norm_h, jnp.where(row == 1, norm_m, jnp.where(row == 2, norm_l, 0.0))
    )
    zero = jnp.zeros_like(high)
    dist = [
        -2.0 * high + unit,
        -2.0 * high + unit,
        -2.0 * mid,
        -2.0 * mid,
        -2.0 * high + unit,
        -2.0 * low,
        norms,
    ]
    l_both = both(l_tile)
    prod = [b * l_both for b in burgers_rows(l_tile, b_tile, block)]
    parts = [split2(p) for p in prod]
    highs = [p[0] for p in parts]
    mids = [p[1] for p in parts]
    weight = highs + mids + highs
    return jnp.concatenate(dist + [zero] * 9, axis=0), jnp.concatenate([zero] * 7 + weight, axis=0)


def build_list(codes_ref, list_ref, count_ref):
    core = codes_ref[6, 0]

    def add(k, count):
        for line in range(2 * NC):
            code = codes_ref[line, 2 * k + core if line >= NC else 2 * k]
            list_ref[0, count] = code
            count = count + (code >= 0).astype(jnp.int32)
        return count

    count = lax.fori_loop(0, NDEV, add, jnp.int32(0), unroll=8)
    for block in range(2):
        for j in range(2 * NX):
            list_ref[0, count + 2 * NX * block + j] = 256 * (2 * core + block) + 2 * NDEV + j
    count = count + 4 * NX
    for j in range(BATCH):
        list_ref[0, count + j] = DUMMY
    count_ref[0, 0] = lax.div(count + (BATCH - 1), BATCH)


def pair_body(list_ref, count_ref, get_source, get_target, force_ref, source_s, moment_s, target_s):
    def prepare(k):
        tiles, first, second = source_operands(*get_source(k))
        store_rows(source_s, k, tiles)
        moment_s[2 * k] = jnp.concatenate(first, axis=0).astype(BF16)
        moment_s[2 * k + 1] = jnp.concatenate(second, axis=0).astype(BF16)

    def prepare_loop(k, carry):
        prepare(k)
        return carry

    lax.fori_loop(0, NDEV, prepare_loop, 0, unroll=4)
    for k in range(NDEV, NDEV + NX + 1):
        prepare(k)

    lane = lax.broadcasted_iota(jnp.int32, (SEG, SEG), 1)
    place = lax.bitwise_and(lane, 7)
    for side in range(NC):
        x_tile, l_tile, b_tile = get_target(side)
        for block in range(2):
            dist, weight = target_rows(x_tile, l_tile, b_tile, block)
            dist = dist.T
            weight = weight.T
            for j in range(2):
                mine = (place >= 4 * j) & (place < 4 * j + 3)
                keep = mine | (place == 4 * j + 3) | (lane >= 48)
                at = 2 * (2 * side + block) + j
                target_s[at, 0:SEG] = jnp.where(keep, dist, 0.0).astype(BF16)
                target_s[at, SEG : 2 * SEG] = jnp.where(mine, weight, 0.0).astype(BF16)

    def items(step, total):
        lows, highs, moments = [], [], []
        for b in range(BATCH):
            code = list_ref[0, step * BATCH + b]
            n = lax.shift_right_logical(code, 8)
            m = lax.bitwise_and(code, 255)
            at = 2 * n + lax.bitwise_and(m, 1)
            both = jnp.dot(
                target_s[at], source_s[lax.shift_right_logical(m, 1)], preferred_element_type=F32
            )
            inverse = lax.rsqrt(both[0:SEG])
            w = both[SEG : 2 * SEG] * (inverse * inverse * inverse)
            high = w.astype(BF16)
            highs.append(high)
            lows.append((w - high.astype(F32)).astype(BF16))
            moment = moment_s[m]
            zero = jnp.zeros_like(moment)
            moments.append(
                jnp.concatenate([jnp.where(n == t, moment, zero) for t in range(4)], axis=0)
            )
        lhs = jnp.concatenate(moments + moments, axis=1)
        rhs = jnp.concatenate(highs + lows, axis=1)
        return total + lax.dot_general(
            rhs, lhs, (((1,), (1,)), ((), ())), preferred_element_type=F32
        )

    total = lax.fori_loop(0, count_ref[0, 0], items, jnp.zeros((SEG, 64), F32))
    total = jnp.concatenate([total, jnp.zeros((SEG, SEG - 64), F32)], axis=1).T
    for side in range(NC):
        x_tile = get_target(side)[0]
        rows = []
        for block in range(2):
            at = 16 * (2 * side + block)
            x_block = x_tile[4 * block : 4 * block + 3]
            rows.append(
                x_block * total[at + 3 : at + 4] - (total[at : at + 3] + total[at + 8 : at + 11])
            )
            rows.append(jnp.zeros((1, SEG), F32))
        force_ref[side] = jnp.concatenate(rows, axis=0)


SCRATCH = [
    pltpu.VMEM((NDEV + NX + 1, SEG, SEG), BF16),
    pltpu.VMEM((2 * (NDEV + NX + 1), 16, SEG), BF16),
    pltpu.VMEM((8, 2 * SEG, SEG), BF16),
]


def tiles_of(tile):
    return tile[0:8], tile[8:16], tile[16:24]


def tiles_of_rows(rows):
    return (
        jnp.concatenate([rows[0], rows[1]], axis=0),
        jnp.concatenate([rows[2], rows[3]], axis=0),
        rows[4],
    )


def no_source():
    zero = jnp.zeros((8, SEG), F32)
    return zero, zero, zero


def first_kernel(codes_ref, all_ref, near_ref, force_ref, list_ref, count_ref, *scratch):
    build_list(codes_ref, list_ref, count_ref)
    core = codes_ref[6, 0]

    def get_source(k):
        if isinstance(k, int):
            return no_source() if k == NDEV + NX else tiles_of(near_ref.at[core, k - NDEV])
        return tiles_of_rows(all_ref.at[k])

    def get_target(side):
        return tiles_of(near_ref.at[side, 0])

    pair_body(list_ref, count_ref, get_source, get_target, force_ref, *scratch)


def second_kernel(
    codes_ref,
    list_ref,
    count_ref,
    all_ref,
    near_ref,
    vel_ref,
    near_vel_ref,
    force_ref,
    position_ref,
    *scratch,
):
    core = codes_ref[6, 0]
    top = vel_ref[0]
    for k in range(1, NDEV):
        top = jnp.maximum(top, vel_ref[k])
    top = jnp.max(top[3:4], axis=1, keepdims=True)
    step = STEP_LENGTH / (jnp.sqrt(top) + EPSILON)
    for side in range(NC):
        for s in range(NX):
            position_ref[side, s] = near_ref[side, s, 0:8] + step * near_vel_ref[side, s]

    def get_source(k):
        if isinstance(k, int):
            if k == NDEV + NX:
                return no_source()
            tile = near_ref.at[core, k - NDEV]
            return position_ref[core, k - NDEV], tile[8:16], tile[16:24]
        x_tile, l_tile, b_tile = tiles_of_rows(all_ref.at[k])
        return x_tile + step * vel_ref[k], l_tile, b_tile

    def get_target(side):
        return position_ref[side, 0], near_ref[side, 0, 8:16], near_ref[side, 0, 16:24]

    pair_body(list_ref, count_ref, get_source, get_target, force_ref, *scratch)


def finish_kernel(codes_ref, stress_ref, parts_ref, near_ref, x_ref, vel_ref, out_ref):
    core, x_index = codes_ref[6, 0], codes_ref[6, 2]
    row = sublane()
    lane = lax.broadcasted_iota(jnp.int32, (8, SEG), 1)
    spare = lax.bitwise_and(row, 3) == 3
    top = jnp.zeros((1, SEG), F32)
    for side, s in [(side, s) for side in range(NC) for s in range(NX)]:
        x_tile = x_ref[side, s, 0:8]
        l_tile = near_ref[side, s, 8:16]
        b_tile = near_ref[side, s, 16:24]
        rows = []
        for block in range(2):
            b = burgers_rows(l_tile, b_tile, block)
            line = [l_tile[4 * block + a : 4 * block + a + 1] for a in range(3)]
            pulled = [
                stress_ref[a, 0] * b[0] + stress_ref[a, 1] * b[1] + stress_ref[a, 2] * b[2]
                for a in range(3)
            ]
            rows.append(pulled[1] * line[2] - pulled[2] * line[1])
            rows.append(pulled[2] * line[0] - pulled[0] * line[2])
            rows.append(pulled[0] * line[1] - pulled[1] * line[0])
            rows.append(jnp.zeros((1, SEG), F32))
        applied = jnp.concatenate(rows, axis=0)
        left = jnp.where(lane == 0, x_tile, pltpu.roll(x_tile, 1, 1))
        right = jnp.where(lane == SEG - 1, x_tile, pltpu.roll(x_tile, SEG - 1, 1))
        chain = left + right - 2.0 * x_tile
        at = NC * lax.bitwise_and(x_index - s, NX - 1)
        pair = parts_ref[at, side] + parts_ref[at + 1, side]
        drag = jnp.where(row < 4, b_tile[4:5], b_tile[5:6])
        velocity = (COUPLE * pair + applied + TENSION * chain) / drag
        velocity = jnp.where(spare, 0.0, velocity)
        vel_ref[side, s] = velocity
        speed = velocity * velocity
        top = jnp.maximum(top, speed[0:1] + speed[1:2] + speed[2:3])
        top = jnp.maximum(top, speed[4:5] + speed[5:6] + speed[6:7])
    send = top if out_ref.shape[1] == 1 else jnp.where(row == 3, top, vel_ref[core, 0])
    out_ref[...] = jnp.broadcast_to(send[None], out_ref.shape)


def pack_kernel(seg_ref, drag_ref, send_ref, part_ref, raw_ref, out_ref):
    raw_ref[...] = jnp.zeros((24, SEG), F32)
    for block in range(2):
        for comp in range(3):
            raw_ref[4 * block + comp, :] = seg_ref[comp, block, :]
            raw_ref[8 + 4 * block + comp, :] = seg_ref[3 + comp, block, :]
        raw_ref[11 + 4 * block, :] = seg_ref[6, block, :]
        raw_ref[16 + 2 * block, :] = seg_ref[7, block, :]
        raw_ref[17 + 2 * block, :] = seg_ref[8, block, :]
        raw_ref[20 + block, :] = drag_ref[block, :]
    raw_ref[3, :] = send_ref[0, :].astype(F32)
    raw_ref[7, :] = part_ref[0, :].astype(F32)
    for at in range(5):
        rows = raw_ref[4 * at : 4 * at + 4, :]
        for peer in range(NZ):
            out_ref[peer, at] = rows


def last_kernel(codes_ref, top_ref, x_ref, vel_ref, pos_out, vel_out):
    core = codes_ref[6, 0]
    top = jnp.max(jnp.max(top_ref[...], axis=0), axis=1, keepdims=True)
    step = STEP_LENGTH / (jnp.sqrt(top) + EPSILON)
    velocity = vel_ref[core, 0]
    moved = x_ref[core, 0] + step * velocity
    for block in range(2):
        for comp in range(3):
            pos_out[comp, block, :] = moved[4 * block + comp]
            vel_out[comp, block, :] = velocity[4 * block + comp]


SMEM = pl.BlockSpec(memory_space=pltpu.SMEM)
VMEM = pl.BlockSpec(memory_space=pltpu.VMEM)


def shape(*dims, dtype=F32):
    return jax.ShapeDtypeStruct(dims, dtype)


def call(kernel, name, operands, outs, smem_in=0, smem_out=0, scratch=(), mib=4):
    return pl.pallas_call(
        kernel,
        name=name,
        in_specs=[SMEM] * smem_in + [VMEM] * (len(operands) - smem_in),
        out_specs=[VMEM] * (len(outs) - smem_out) + [SMEM] * smem_out,
        out_shape=outs,
        scratch_shapes=scratch,
        compiler_params=pltpu.CompilerParams(vmem_limit_bytes=mib << 20),
    )(*operands)


def pass_x(value, shift):
    return lax.ppermute(value, "x", [(i, (i + shift) % NX) for i in range(NX)])


def exchange(value, axes):
    return lax.all_to_all(value, axes, 0, 0, tiled=True)


def local(segments, stress, drag_coef, send_ids, partner_ids):
    core = lax.axis_index("c")
    y_index = lax.axis_index("y")
    x_index = lax.axis_index("x")
    chip_index = y_index * NZ + lax.axis_index("z")
    raw, to_z = call(
        pack_kernel,
        "pack",
        (
            segments.transpose(1, 0, 2),
            drag_coef,
            send_ids.reshape(1, SEG),
            partner_ids.reshape(1, SEG),
        ),
        [shape(24, SEG), shape(NZ, 5, 4, SEG)],
        mib=56,
    )
    along_z = exchange(to_z, "z")
    group = [raw] + [pass_x(raw, shift) for shift in range(1, NX)]
    near = lax.all_gather(jnp.stack(group), "c", axis=0)
    chip = near[:, 0]

    lane = lax.broadcasted_iota(jnp.int32, (NC, SEG), 1)
    side = lax.broadcasted_iota(jnp.int32, (NC, SEG), 0)
    even = lax.bitwise_and(lane, SEG - 2)
    sent = chip[:, 3].astype(jnp.int32)
    other = chip[:, 7].astype(jnp.int32)
    out = jnp.where(sent >= 0, even + other + 256 * (2 * side + sent), -1)
    first = lane[0:1]
    where = jnp.where(first == 0, core, jnp.where(first == 1, y_index, x_index))
    zero = jnp.zeros((1, SEG), jnp.int32)
    known = jnp.concatenate([out, zero, zero, where, zero], axis=0)
    pick = (lane == 2 * chip_index + side).astype(F32)

    everyone = exchange(
        jnp.broadcast_to(along_z.reshape(1, NZ * 5, 4, SEG), (NY, NZ * 5, 4, SEG)), "y"
    ).reshape(NDEV, 5, 4, SEG)
    lists = everyone[:, 0:2, 3].reshape(2 * NDEV, SEG)
    incoming = lax.dot_general(
        pick, lists, (((1,), (1,)), ((), ())), precision=lax.Precision.HIGHEST
    ).astype(jnp.int32)
    partner = jnp.concatenate([incoming[:, 1:], incoming[:, :1]], axis=1)
    into = jnp.where(incoming >= 0, even + incoming + 256 * (2 * side + partner), -1)
    codes = jnp.concatenate([into, known], axis=0)

    force, items, count = call(
        first_kernel,
        "first_pairs",
        (codes, everyone, near),
        [
            shape(NC, 8, SEG),
            shape(1, LIST, dtype=jnp.int32),
            shape(1, 1, dtype=jnp.int32),
        ],
        smem_in=1,
        smem_out=2,
        scratch=SCRATCH,
        mib=16,
    )
    def finish(force, position, peers, name):
        return call(
            finish_kernel,
            name,
            (codes, stress, exchange(jnp.broadcast_to(force[None], (8, *force.shape)), ("x", "c")), near, position),
            [shape(NC, NX, 8, SEG), shape(*peers, SEG)],
            smem_in=2,
        )

    near_vel, to_z = finish(force, near, (NZ, 8), "finish")
    along_z = exchange(to_z, "z").reshape(1, NZ * 8, SEG)
    vel_all = exchange(jnp.broadcast_to(along_z, (NY, NZ * 8, SEG)), "y").reshape(NDEV, 8, SEG)

    force, position = call(
        second_kernel,
        "second_pairs",
        (codes, items, count, everyone, near, vel_all, near_vel),
        [shape(NC, 8, SEG), shape(NC, NX, 8, SEG)],
        smem_in=3,
        scratch=SCRATCH,
        mib=16,
    )
    near_vel, to_all = finish(force, position, (NDEV, 1), "finish_last")
    tops = exchange(to_all, ("y", "z"))
    positions, velocity = call(
        last_kernel,
        "last",
        (codes, tops, position, near_vel),
        [shape(3, 2, SEG), shape(3, 2, SEG)],
        smem_in=1,
    )
    return positions.transpose(1, 0, 2), velocity.transpose(1, 0, 2)


def solution(mesh):
    split = Mesh(
        mesh.devices.reshape(NY, NZ, NC, mesh.shape["sub"]), ("y", "z", "c", "x")
    )
    return jax.shard_map(
        local,
        mesh=split,
        in_specs=(
            P(DOM_SUB, None, None),
            P(),
            P(DOM_SUB, None),
            P(DOM_SUB, None, None),
            P(DOM_SUB, None, None),
        ),
        out_specs=(P(DOM_SUB, None, None), P(DOM_SUB, None, None)),
        check_vma=False,
    )
```

```python
import functools

import jax
import jax.numpy as jnp
from jax import lax
from jax.experimental import pallas as pl
from jax.experimental.pallas import tpu as pltpu
from jax.sharding import Mesh
from jax.sharding import PartitionSpec as P

NY, NZ, NC = 4, 16, 2
DOM = ("y", "z", "c")
DOM_SUB = ("y", "z", "c", "x")

COUPLE = 0.0625
CORE_SQUARE = 0.5
TENSION = 0.25
STEP_LENGTH = 1.0
EPSILON = 1e-06

SEG = 128
NDEV = NY * NZ
NX = 4
BATCH = 32
LIST = 320
DUMMY = 2 * (NDEV + NX)
F32 = jnp.float32
BF16 = jnp.bfloat16


def sublane(shape=(8, SEG)):
    return lax.broadcasted_iota(jnp.int32, shape, len(shape) - 2)


def up(value, count):
    return jnp.concatenate([value[count:], value[:count]], axis=0)


def split2(value):
    high = value.astype(BF16).astype(F32)
    return high, value - high


def split3(value):
    high, rest = split2(value)
    mid, low = split2(rest)
    return high, mid, low


def source_operands(x_tile, l_tile, b_tile):
    row = sublane()
    x_tile = jnp.where(lax.bitwise_and(row, 3) < 3, x_tile, 0.0)
    square = x_tile * x_tile
    norm0 = square[0:1] + square[1:2] + square[2:3] + CORE_SQUARE
    norm1 = square[4:5] + square[5:6] + square[6:7] + CORE_SQUARE
    full = jnp.where(row == 3, norm0, jnp.where(row == 7, norm1, x_tile))
    high, mid, low = split3(full)
    dist = [high, mid, high, mid, low, high, jnp.ones_like(high)]
    burgers = [burgers_rows(l_tile, b_tile, block) for block in range(2)]
    prod = [jnp.where(row < 4, burgers[0][a], burgers[1][a]) * l_tile for a in range(3)]
    parts = [split2(p) for p in prod]
    highs = [p[0] for p in parts]
    mids = [p[1] for p in parts]
    weight = highs + highs + mids
    first = (jnp.where(row == 3, 1.0, high), jnp.where(row == 3, 0.0, mid))
    second = (jnp.where(row == 3, 1.0, up(high, 4)), jnp.where(row == 3, 0.0, up(mid, 4)))
    return dist + weight, first, second


def burgers_rows(l_tile, b_tile, block):
    return [
        l_tile[4 * block + 3 : 4 * block + 4],
        b_tile[2 * block : 2 * block + 1],
        b_tile[2 * block + 1 : 2 * block + 2],
    ]


def store_rows(ref, index, tiles):
    for at in range(0, len(tiles), 2):
        pair = jnp.concatenate([tiles[at], tiles[at + 1]], axis=0).astype(BF16)
        ref[index, 8 * at : 8 * at + 16, :] = pair


def target_rows(x_tile, l_tile, b_tile, block):
    row = sublane()

    def both(tile):
        other = up(tile, 4)
        own, far = (tile, other) if block == 0 else (other, tile)
        return jnp.where(lax.bitwise_and(row, 3) == 3, 0.0, jnp.where(row < 4, own, far))

    x_both = both(x_tile)
    high, mid, low = split3(x_both)
    square = x_both * x_both
    norm = square[0:1] + square[1:2] + square[2:3]
    norm_h, norm_m, norm_l = split3(norm)
    unit = jnp.where(lax.bitwise_and(row, 3) == 3, 1.0, 0.0)
    norms = jnp.where(
        row == 0, norm_h, jnp.where(row == 1, norm_m, jnp.where(row == 2, norm_l, 0.0))
    )
    zero = jnp.zeros_like(high)
    dist = [
        -2.0 * high + unit,
        -2.0 * high + unit,
        -2.0 * mid,
        -2.0 * mid,
        -2.0 * high + unit,
        -2.0 * low,
        norms,
    ]
    l_both = both(l_tile)
    prod = [b * l_both for b in burgers_rows(l_tile, b_tile, block)]
    parts = [split2(p) for p in prod]
    highs = [p[0] for p in parts]
    mids = [p[1] for p in parts]
    weight = highs + mids + highs
    return jnp.concatenate(dist + [zero] * 9, axis=0), jnp.concatenate([zero] * 7 + weight, axis=0)


def build_list(codes_ref, list_ref, count_ref):
    core = codes_ref[6, 0]

    def add(k, count):
        for line in range(2 * NC):
            code = codes_ref[line, 2 * k + core if line >= NC else 2 * k]
            list_ref[0, count] = code
            count = count + (code >= 0).astype(jnp.int32)
        return count

    count = lax.fori_loop(0, NDEV, add, jnp.int32(0), unroll=8)
    for block in range(2):
        for j in range(2 * NX):
            list_ref[0, count + 2 * NX * block + j] = 256 * (2 * core + block) + 2 * NDEV + j
    count = count + 4 * NX
    for j in range(BATCH):
        list_ref[0, count + j] = DUMMY
    whole = lax.div(count + (BATCH // 2 - 1), BATCH)
    count_ref[0, 0] = whole
    count_ref[0, 1] = (count > whole * BATCH).astype(jnp.int32)


def pair_body(list_ref, count_ref, get_source, get_target, force_ref, source_s, moment_s, target_s):
    def prepare(k):
        tiles, first, second = source_operands(*get_source(k))
        store_rows(source_s, k, tiles)
        moment_s[2 * k] = jnp.concatenate(first, axis=0).astype(BF16)
        moment_s[2 * k + 1] = jnp.concatenate(second, axis=0).astype(BF16)

    def prepare_loop(k, carry):
        prepare(k)
        return carry

    lax.fori_loop(0, NDEV, prepare_loop, 0, unroll=4)
    for k in range(NDEV, NDEV + NX + 1):
        prepare(k)

    lane = lax.broadcasted_iota(jnp.int32, (SEG, SEG), 1)
    place = lax.bitwise_and(lane, 7)
    for side in range(NC):
        x_tile, l_tile, b_tile = get_target(side)
        for block in range(2):
            dist, weight = target_rows(x_tile, l_tile, b_tile, block)
            dist = dist.T
            weight = weight.T
            for j in range(2):
                mine = (place >= 4 * j) & (place < 4 * j + 3)
                keep = mine | (place == 4 * j + 3) | (lane >= 48)
                at = 2 * (2 * side + block) + j
                target_s[at, 0:SEG] = jnp.where(keep, dist, 0.0).astype(BF16)
                target_s[at, SEG : 2 * SEG] = jnp.where(mine, weight, 0.0).astype(BF16)

    def items(start, size, total):
        lows, highs, moments = [], [], []
        for b in range(size):
            code = list_ref[0, start + b]
            n = lax.shift_right_logical(code, 8)
            m = lax.bitwise_and(code, 255)
            at = 2 * n + lax.bitwise_and(m, 1)
            both = jnp.dot(
                target_s[at], source_s[lax.shift_right_logical(m, 1)], preferred_element_type=F32
            )
            inverse = lax.rsqrt(both[0:SEG])
            w = both[SEG : 2 * SEG] * (inverse * inverse * inverse)
            high = w.astype(BF16)
            highs.append(high)
            lows.append((w - high.astype(F32)).astype(BF16))
            moment = moment_s[m]
            zero = jnp.zeros_like(moment)
            moments.append(
                jnp.concatenate([jnp.where(n == t, moment, zero) for t in range(4)], axis=0)
            )
        lhs = jnp.concatenate(moments + moments, axis=1)
        rhs = jnp.concatenate(highs + lows, axis=1)
        return total + lax.dot_general(
            rhs, lhs, (((1,), (1,)), ((), ())), preferred_element_type=F32
        )

    whole = count_ref[0, 0]
    total = lax.fori_loop(
        0,
        whole,
        lambda step, total: items(step * BATCH, BATCH, total),
        jnp.zeros((SEG, 64), F32),
    )
    total = lax.fori_loop(
        0,
        count_ref[0, 1],
        lambda step, total: items(whole * BATCH, BATCH // 2, total),
        total,
    )
    total = jnp.concatenate([total, jnp.zeros((SEG, SEG - 64), F32)], axis=1).T
    for side in range(NC):
        x_tile = get_target(side)[0]
        rows = []
        for block in range(2):
            at = 16 * (2 * side + block)
            x_block = x_tile[4 * block : 4 * block + 3]
            rows.append(
                x_block * total[at + 3 : at + 4] - (total[at : at + 3] + total[at + 8 : at + 11])
            )
            rows.append(jnp.zeros((1, SEG), F32))
        force_ref[side] = jnp.concatenate(rows, axis=0)


SCRATCH = [
    pltpu.VMEM((NDEV + NX + 1, SEG, SEG), BF16),
    pltpu.VMEM((2 * (NDEV + NX + 1), 16, SEG), BF16),
    pltpu.VMEM((8, 2 * SEG, SEG), BF16),
]


def tiles_of(tile):
    return tile[0:8], tile[8:16], tile[16:24]


def tiles_of_rows(rows):
    return (
        jnp.concatenate([rows[0], rows[1]], axis=0),
        jnp.concatenate([rows[2], rows[3]], axis=0),
        rows[4],
    )


def no_source():
    zero = jnp.zeros((8, SEG), F32)
    return zero, zero, zero


def first_kernel(codes_ref, all_ref, near_ref, force_ref, list_ref, count_ref, *scratch):
    build_list(codes_ref, list_ref, count_ref)
    core = codes_ref[6, 0]

    def get_source(k):
        if isinstance(k, int):
            return no_source() if k == NDEV + NX else tiles_of(near_ref.at[core, k - NDEV])
        return tiles_of_rows(all_ref.at[k])

    def get_target(side):
        return tiles_of(near_ref.at[side, 0])

    pair_body(list_ref, count_ref, get_source, get_target, force_ref, *scratch)


def second_kernel(
    codes_ref,
    list_ref,
    count_ref,
    all_ref,
    near_ref,
    vel_ref,
    near_vel_ref,
    force_ref,
    position_ref,
    *scratch,
):
    core = codes_ref[6, 0]
    top = vel_ref[0]
    for k in range(1, NDEV):
        top = jnp.maximum(top, vel_ref[k])
    top = jnp.max(top[3:4], axis=1, keepdims=True)
    step = STEP_LENGTH / (jnp.sqrt(top) + EPSILON)
    for side in range(NC):
        for s in range(NX):
            position_ref[side, s] = near_ref[side, s, 0:8] + step * near_vel_ref[side, s]

    def get_source(k):
        if isinstance(k, int):
            if k == NDEV + NX:
                return no_source()
            tile = near_ref.at[core, k - NDEV]
            return position_ref[core, k - NDEV], tile[8:16], tile[16:24]
        x_tile, l_tile, b_tile = tiles_of_rows(all_ref.at[k])
        return x_tile + step * vel_ref[k], l_tile, b_tile

    def get_target(side):
        return position_ref[side, 0], near_ref[side, 0, 8:16], near_ref[side, 0, 16:24]

    pair_body(list_ref, count_ref, get_source, get_target, force_ref, *scratch)


def finish_kernel(codes_ref, stress_ref, parts_ref, near_ref, x_ref, vel_ref, out_ref):
    core, x_index = codes_ref[6, 0], codes_ref[6, 2]
    row = sublane()
    lane = lax.broadcasted_iota(jnp.int32, (8, SEG), 1)
    spare = lax.bitwise_and(row, 3) == 3
    top = jnp.zeros((1, SEG), F32)
    for side, s in [(side, s) for side in range(NC) for s in range(NX)]:
        x_tile = x_ref[side, s, 0:8]
        l_tile = near_ref[side, s, 8:16]
        b_tile = near_ref[side, s, 16:24]
        rows = []
        for block in range(2):
            b = burgers_rows(l_tile, b_tile, block)
            line = [l_tile[4 * block + a : 4 * block + a + 1] for a in range(3)]
            pulled = [
                stress_ref[a, 0] * b[0] + stress_ref[a, 1] * b[1] + stress_ref[a, 2] * b[2]
                for a in range(3)
            ]
            rows.append(pulled[1] * line[2] - pulled[2] * line[1])
            rows.append(pulled[2] * line[0] - pulled[0] * line[2])
            rows.append(pulled[0] * line[1] - pulled[1] * line[0])
            rows.append(jnp.zeros((1, SEG), F32))
        applied = jnp.concatenate(rows, axis=0)
        left = jnp.where(lane == 0, x_tile, pltpu.roll(x_tile, 1, 1))
        right = jnp.where(lane == SEG - 1, x_tile, pltpu.roll(x_tile, SEG - 1, 1))
        chain = left + right - 2.0 * x_tile
        at = NC * lax.bitwise_and(x_index - s, NX - 1)
        pair = parts_ref[at, side] + parts_ref[at + 1, side]
        drag = jnp.where(row < 4, b_tile[4:5], b_tile[5:6])
        velocity = (COUPLE * pair + applied + TENSION * chain) / drag
        velocity = jnp.where(spare, 0.0, velocity)
        vel_ref[side, s] = velocity
        speed = velocity * velocity
        top = jnp.maximum(top, speed[0:1] + speed[1:2] + speed[2:3])
        top = jnp.maximum(top, speed[4:5] + speed[5:6] + speed[6:7])
    send = top if out_ref.shape[1] == 1 else jnp.where(row == 3, top, vel_ref[core, 0])
    out_ref[...] = jnp.broadcast_to(send[None], out_ref.shape)


def pack_kernel(seg_ref, drag_ref, send_ref, part_ref, raw_ref, out_ref):
    raw_ref[...] = jnp.zeros((24, SEG), F32)
    for block in range(2):
        for comp in range(3):
            raw_ref[4 * block + comp, :] = seg_ref[comp, block, :]
            raw_ref[8 + 4 * block + comp, :] = seg_ref[3 + comp, block, :]
        raw_ref[11 + 4 * block, :] = seg_ref[6, block, :]
        raw_ref[16 + 2 * block, :] = seg_ref[7, block, :]
        raw_ref[17 + 2 * block, :] = seg_ref[8, block, :]
        raw_ref[20 + block, :] = drag_ref[block, :]
    raw_ref[3, :] = send_ref[0, :].astype(F32)
    raw_ref[7, :] = part_ref[0, :].astype(F32)
    for at in range(5):
        rows = raw_ref[4 * at : 4 * at + 4, :]
        for peer in range(NZ):
            out_ref[peer, at] = rows


def last_kernel(codes_ref, top_ref, x_ref, vel_ref, pos_out, vel_out):
    core = codes_ref[6, 0]
    top = jnp.max(jnp.max(top_ref[...], axis=0), axis=1, keepdims=True)
    step = STEP_LENGTH / (jnp.sqrt(top) + EPSILON)
    velocity = vel_ref[core, 0]
    moved = x_ref[core, 0] + step * velocity
    for block in range(2):
        for comp in range(3):
            pos_out[comp, block, :] = moved[4 * block + comp]
            vel_out[comp, block, :] = velocity[4 * block + comp]


SMEM = pl.BlockSpec(memory_space=pltpu.SMEM)
VMEM = pl.BlockSpec(memory_space=pltpu.VMEM)


def shape(*dims, dtype=F32):
    return jax.ShapeDtypeStruct(dims, dtype)


def call(kernel, name, operands, outs, smem_in=0, smem_out=0, scratch=(), mib=4):
    return pl.pallas_call(
        kernel,
        name=name,
        in_specs=[SMEM] * smem_in + [VMEM] * (len(operands) - smem_in),
        out_specs=[VMEM] * (len(outs) - smem_out) + [SMEM] * smem_out,
        out_shape=outs,
        scratch_shapes=scratch,
        compiler_params=pltpu.CompilerParams(vmem_limit_bytes=mib << 20),
    )(*operands)


def pass_x(value, shift):
    return lax.ppermute(value, "x", [(i, (i + shift) % NX) for i in range(NX)])


def exchange(value, axes):
    return lax.all_to_all(value, axes, 0, 0, tiled=True)


def local(segments, stress, drag_coef, send_ids, partner_ids):
    core = lax.axis_index("c")
    y_index = lax.axis_index("y")
    x_index = lax.axis_index("x")
    chip_index = y_index * NZ + lax.axis_index("z")
    raw, to_z = call(
        pack_kernel,
        "pack",
        (
            segments.transpose(1, 0, 2),
            drag_coef,
            send_ids.reshape(1, SEG),
            partner_ids.reshape(1, SEG),
        ),
        [shape(24, SEG), shape(NZ, 5, 4, SEG)],
        mib=56,
    )
    along_z = exchange(to_z, "z")
    late, along_z = lax.optimization_barrier((raw, along_z))
    group = [raw, pass_x(raw, 1), pass_x(raw, 2), pass_x(late, 3)]
    near = lax.all_gather(jnp.stack(group), "c", axis=0)
    chip = near[:, 0]

    lane = lax.broadcasted_iota(jnp.int32, (NC, SEG), 1)
    side = lax.broadcasted_iota(jnp.int32, (NC, SEG), 0)
    even = lax.bitwise_and(lane, SEG - 2)
    sent = chip[:, 3].astype(jnp.int32)
    other = chip[:, 7].astype(jnp.int32)
    out = jnp.where(sent >= 0, even + other + 256 * (2 * side + sent), -1)
    first = lane[0:1]
    where = jnp.where(first == 0, core, jnp.where(first == 1, y_index, x_index))
    zero = jnp.zeros((1, SEG), jnp.int32)
    known = jnp.concatenate([out, zero, zero, where, zero], axis=0)
    pick = (lane == 2 * chip_index + side).astype(F32)

    everyone = exchange(
        jnp.broadcast_to(along_z.reshape(1, NZ * 5, 4, SEG), (NY, NZ * 5, 4, SEG)), "y"
    ).reshape(NDEV, 5, 4, SEG)
    lists = everyone[:, 0:2, 3].reshape(2 * NDEV, SEG)
    incoming = lax.dot_general(
        pick, lists, (((1,), (1,)), ((), ())), precision=lax.Precision.HIGHEST
    ).astype(jnp.int32)
    partner = jnp.concatenate([incoming[:, 1:], incoming[:, :1]], axis=1)
    into = jnp.where(incoming >= 0, even + incoming + 256 * (2 * side + partner), -1)
    codes = jnp.concatenate([into, known], axis=0)

    force, items, count = call(
        first_kernel,
        "first_pairs",
        (codes, everyone, near),
        [
            shape(NC, 8, SEG),
            shape(1, LIST, dtype=jnp.int32),
            shape(1, 2, dtype=jnp.int32),
        ],
        smem_in=1,
        smem_out=2,
        scratch=SCRATCH,
        mib=16,
    )
    def finish(force, position, peers, name):
        return call(
            finish_kernel,
            name,
            (codes, stress, exchange(jnp.broadcast_to(force[None], (8, *force.shape)), ("x", "c")), near, position),
            [shape(NC, NX, 8, SEG), shape(*peers, SEG)],
            smem_in=2,
        )

    near_vel, to_all = finish(force, near, (NDEV, 8), "finish")
    vel_all = exchange(to_all, ("y", "z"))

    force, position = call(
        second_kernel,
        "second_pairs",
        (codes, items, count, everyone, near, vel_all, near_vel),
        [shape(NC, 8, SEG), shape(NC, NX, 8, SEG)],
        smem_in=3,
        scratch=SCRATCH,
        mib=16,
    )
    near_vel, to_all = finish(force, position, (NDEV, 1), "finish_last")
    tops = exchange(to_all, ("y", "z"))
    positions, velocity = call(
        last_kernel,
        "last",
        (codes, tops, position, near_vel),
        [shape(3, 2, SEG), shape(3, 2, SEG)],
        smem_in=1,
    )
    return positions.transpose(1, 0, 2), velocity.transpose(1, 0, 2)


def solution(mesh):
    split = Mesh(
        mesh.devices.reshape(NY, NZ, NC, mesh.shape["sub"]), ("y", "z", "c", "x")
    )
    return jax.shard_map(
        local,
        mesh=split,
        in_specs=(
            P(DOM_SUB, None, None),
            P(),
            P(DOM_SUB, None),
            P(DOM_SUB, None, None),
            P(DOM_SUB, None, None),
        ),
        out_specs=(P(DOM_SUB, None, None), P(DOM_SUB, None, None)),
        check_vma=False,
    )
```

```python
import functools

import jax
import jax.numpy as jnp
from jax import lax
from jax.experimental import pallas as pl
from jax.experimental.pallas import tpu as pltpu
from jax.sharding import Mesh
from jax.sharding import PartitionSpec as P

NY, NZ, NC = 4, 16, 2
DOM = ("y", "z", "c")
DOM_SUB = ("y", "z", "c", "x")

COUPLE = 0.0625
CORE_SQUARE = 0.5
TENSION = 0.25
STEP_LENGTH = 1.0
EPSILON = 1e-06

SEG = 128
NDEV = NY * NZ
NX = 4
BATCH = 32
LIST = 320
F32 = jnp.float32
BF16 = jnp.bfloat16


def sublane(shape=(8, SEG)):
    return lax.broadcasted_iota(jnp.int32, shape, len(shape) - 2)


def up(value, count):
    return jnp.concatenate([value[count:], value[:count]], axis=0)


def split2(value):
    high = value.astype(BF16).astype(F32)
    return high, value - high


def split3(value):
    high, rest = split2(value)
    mid, low = split2(rest)
    return high, mid, low


def source_operands(x_tile, l_tile, b_tile):
    row = sublane()
    x_tile = jnp.where(lax.bitwise_and(row, 3) < 3, x_tile, 0.0)
    square = x_tile * x_tile
    norm0 = square[0:1] + square[1:2] + square[2:3] + CORE_SQUARE
    norm1 = square[4:5] + square[5:6] + square[6:7] + CORE_SQUARE
    full = jnp.where(row == 3, norm0, jnp.where(row == 7, norm1, x_tile))
    high, mid, low = split3(full)
    dist = [high, mid, high, mid, low, high, jnp.ones_like(high)]
    burgers = [burgers_rows(l_tile, b_tile, block) for block in range(2)]
    prod = [jnp.where(row < 4, burgers[0][a], burgers[1][a]) * l_tile for a in range(3)]
    parts = [split2(p) for p in prod]
    highs = [p[0] for p in parts]
    mids = [p[1] for p in parts]
    weight = highs + highs + mids
    first = (jnp.where(row == 3, 1.0, high), jnp.where(row == 3, 0.0, mid))
    second = (jnp.where(row == 3, 1.0, up(high, 4)), jnp.where(row == 3, 0.0, up(mid, 4)))
    return dist + weight, first, second


def burgers_rows(l_tile, b_tile, block):
    return [
        l_tile[4 * block + 3 : 4 * block + 4],
        b_tile[2 * block : 2 * block + 1],
        b_tile[2 * block + 1 : 2 * block + 2],
    ]


def store_rows(ref, index, tiles):
    for at in range(0, len(tiles), 2):
        pair = jnp.concatenate([tiles[at], tiles[at + 1]], axis=0).astype(BF16)
        ref[index, 8 * at : 8 * at + 16, :] = pair


def target_rows(x_tile, l_tile, b_tile, block):
    row = sublane()

    def both(tile):
        other = up(tile, 4)
        own, far = (tile, other) if block == 0 else (other, tile)
        return jnp.where(lax.bitwise_and(row, 3) == 3, 0.0, jnp.where(row < 4, own, far))

    x_both = both(x_tile)
    high, mid, low = split3(x_both)
    square = x_both * x_both
    norm = square[0:1] + square[1:2] + square[2:3]
    norm_h, norm_m, norm_l = split3(norm)
    unit = jnp.where(lax.bitwise_and(row, 3) == 3, 1.0, 0.0)
    norms = jnp.where(
        row == 0, norm_h, jnp.where(row == 1, norm_m, jnp.where(row == 2, norm_l, 0.0))
    )
    zero = jnp.zeros_like(high)
    dist = [
        -2.0 * high + unit,
        -2.0 * high + unit,
        -2.0 * mid,
        -2.0 * mid,
        -2.0 * high + unit,
        -2.0 * low,
        norms,
    ]
    l_both = both(l_tile)
    prod = [b * l_both for b in burgers_rows(l_tile, b_tile, block)]
    parts = [split2(p) for p in prod]
    highs = [p[0] for p in parts]
    mids = [p[1] for p in parts]
    weight = highs + mids + highs
    return jnp.concatenate(dist + [zero] * 9, axis=0), jnp.concatenate([zero] * 7 + weight, axis=0)


def add_code(list_ref, count, code, keep):
    list_ref[0, count] = code
    return count + keep.astype(jnp.int32)


def add_group(list_ref, count, core, lines):
    for block in range(2):
        for j in range(2 * NX):
            list_ref[0, count + 2 * NX * block + j] = 256 * (2 * core + block) + 2 * lines + j
    count = count + 4 * NX
    for j in range(BATCH):
        list_ref[0, count + j] = 2 * (lines + NX)
    return count


def batches(count):
    whole = lax.div(count + (BATCH // 2 - 1), BATCH)
    return whole, (count > whole * BATCH).astype(jnp.int32)


def build_list(codes_ref, list_ref):
    core, y_index = codes_ref[6, 0], codes_ref[6, 1]

    def add_in(k, count):
        for side in range(NC):
            code = codes_ref[side, 2 * k]
            count = add_code(list_ref, count, code, code >= 0)
        return count

    def add_out(at, count):
        k = lax.bitwise_and(at + NZ * (y_index + 1), NDEV - 1)
        for side in range(NC):
            code = codes_ref[NC + side, 2 * k + core]
            count = add_code(list_ref, count, code, code >= 0)
        return count

    count = lax.fori_loop(0, NDEV, add_in, jnp.int32(0), unroll=8)
    first = lax.fori_loop(0, NDEV - NZ, add_out, count, unroll=8)
    count = lax.fori_loop(NDEV - NZ, NDEV, add_out, first, unroll=8)
    return first, add_group(list_ref, count, core, NDEV)


def build_near_list(codes_ref, list_ref):
    core, y_index = codes_ref[6, 0], codes_ref[6, 1]

    def add_out(z, count):
        for side in range(NC):
            code = codes_ref[NC + side, 2 * (NZ * y_index + z) + core]
            count = add_code(list_ref, count, code - 2 * NZ * y_index, code >= 0)
        return count

    count = lax.fori_loop(0, NZ, add_out, jnp.int32(0), unroll=8)
    return add_group(list_ref, count, core, NZ)


def pair_body(
    list_ref, whole, tail, limit, lines, get_source, get_target, force_ref, scratch, more=None
):
    source_s, moment_s, target_s = scratch

    def prepare(k):
        tiles, first, second = source_operands(*get_source(k))
        store_rows(source_s, k, tiles)
        moment_s[2 * k] = jnp.concatenate(first, axis=0).astype(BF16)
        moment_s[2 * k + 1] = jnp.concatenate(second, axis=0).astype(BF16)

    def prepare_loop(k, carry):
        prepare(k)
        return carry

    lax.fori_loop(0, lines, prepare_loop, 0, unroll=4)
    for k in range(lines, lines + NX + 1):
        prepare(k)

    lane = lax.broadcasted_iota(jnp.int32, (SEG, SEG), 1)
    place = lax.bitwise_and(lane, 7)
    for side in range(NC):
        x_tile, l_tile, b_tile = get_target(side)
        for block in range(2):
            dist, weight = target_rows(x_tile, l_tile, b_tile, block)
            dist = dist.T
            weight = weight.T
            for j in range(2):
                mine = (place >= 4 * j) & (place < 4 * j + 3)
                keep = mine | (place == 4 * j + 3) | (lane >= 48)
                at = 2 * (2 * side + block) + j
                target_s[at, 0:SEG] = jnp.where(keep, dist, 0.0).astype(BF16)
                target_s[at, SEG : 2 * SEG] = jnp.where(mine, weight, 0.0).astype(BF16)

    def items(start, size, total):
        lows, highs, moments = [], [], []
        for b in range(size):
            code = list_ref[0, start + b]
            if limit is not None:
                code = jnp.where(start + b < limit, code, 2 * (lines + NX))
            n = lax.shift_right_logical(code, 8)
            m = lax.bitwise_and(code, 255)
            at = 2 * n + lax.bitwise_and(m, 1)
            both = jnp.dot(
                target_s[at], source_s[lax.shift_right_logical(m, 1)], preferred_element_type=F32
            )
            inverse = lax.rsqrt(both[0:SEG])
            w = both[SEG : 2 * SEG] * (inverse * inverse * inverse)
            high = w.astype(BF16)
            highs.append(high)
            lows.append((w - high.astype(F32)).astype(BF16))
            moment = moment_s[m]
            zero = jnp.zeros_like(moment)
            moments.append(
                jnp.concatenate([jnp.where(n == t, moment, zero) for t in range(4)], axis=0)
            )
        sums = lax.dot_general(
            jnp.concatenate(
                [jnp.concatenate(highs, axis=1), jnp.concatenate(lows, axis=1)], axis=0
            ),
            jnp.concatenate(moments, axis=1),
            (((1,), (1,)), ((), ())),
            preferred_element_type=F32,
        )
        return total + sums[0:SEG] + sums[SEG : 2 * SEG]

    total = lax.fori_loop(
        0,
        whole,
        lambda step, total: items(step * BATCH, BATCH, total),
        jnp.zeros((SEG, 64), F32),
    )
    total = lax.fori_loop(
        0, tail, lambda step, total: items(whole * BATCH, BATCH // 2, total), total
    )
    total = jnp.concatenate([total, jnp.zeros((SEG, SEG - 64), F32)], axis=1).T
    for side in range(NC):
        x_tile = get_target(side)[0]
        rows = []
        for block in range(2):
            at = 16 * (2 * side + block)
            x_block = x_tile[4 * block : 4 * block + 3]
            rows.append(
                x_block * total[at + 3 : at + 4] - (total[at : at + 3] + total[at + 8 : at + 11])
            )
            rows.append(jnp.zeros((1, SEG), F32))
        force = jnp.concatenate(rows, axis=0)
        force_ref[side] = force if more is None else force + more[side]


def scratch_of(lines):
    return [
        pltpu.VMEM((lines + NX + 1, SEG, SEG), BF16),
        pltpu.VMEM((2 * (lines + NX + 1), 16, SEG), BF16),
        pltpu.VMEM((8, 2 * SEG, SEG), BF16),
    ]


def tiles_of(tile):
    return tile[0:8], tile[8:16], tile[16:24]


def tiles_of_rows(rows):
    return (
        jnp.concatenate([rows[0], rows[1]], axis=0),
        jnp.concatenate([rows[2], rows[3]], axis=0),
        rows[4],
    )


def no_source():
    zero = jnp.zeros((8, SEG), F32)
    return zero, zero, zero


def near_kernel(codes_ref, line_ref, near_ref, force_ref, list_s, *scratch):
    count = build_near_list(codes_ref, list_s)
    core = codes_ref[6, 0]

    def get_source(k):
        if isinstance(k, int):
            return no_source() if k == NZ + NX else tiles_of(near_ref.at[core, k - NZ])
        return tiles_of_rows(line_ref.at[k])

    def get_target(side):
        return tiles_of(near_ref.at[side, 0])

    pair_body(list_s, *batches(count), None, NZ, get_source, get_target, force_ref, scratch)


def first_kernel(codes_ref, all_ref, near_ref, more_ref, force_ref, list_ref, count_ref, *scratch):
    first, count = build_list(codes_ref, list_ref)
    whole, tail = batches(count)
    count_ref[0, 0] = whole
    count_ref[0, 1] = tail

    def get_source(k):
        return no_source() if isinstance(k, int) else tiles_of_rows(all_ref.at[k])

    def get_target(side):
        return tiles_of(near_ref.at[side, 0])

    pair_body(
        list_ref,
        *batches(first),
        first,
        NDEV,
        get_source,
        get_target,
        force_ref,
        scratch,
        more_ref,
    )


def second_kernel(
    codes_ref,
    list_ref,
    count_ref,
    all_ref,
    near_ref,
    vel_ref,
    near_vel_ref,
    force_ref,
    position_ref,
    *scratch,
):
    core = codes_ref[6, 0]
    top = vel_ref[0]
    for k in range(1, NDEV):
        top = jnp.maximum(top, vel_ref[k])
    top = jnp.max(top[3:4], axis=1, keepdims=True)
    step = STEP_LENGTH / (jnp.sqrt(top) + EPSILON)
    for side in range(NC):
        for s in range(NX):
            position_ref[side, s] = near_ref[side, s, 0:8] + step * near_vel_ref[side, s]

    def get_source(k):
        if isinstance(k, int):
            if k == NDEV + NX:
                return no_source()
            tile = near_ref.at[core, k - NDEV]
            return position_ref[core, k - NDEV], tile[8:16], tile[16:24]
        x_tile, l_tile, b_tile = tiles_of_rows(all_ref.at[k])
        return x_tile + step * vel_ref[k], l_tile, b_tile

    def get_target(side):
        return position_ref[side, 0], near_ref[side, 0, 8:16], near_ref[side, 0, 16:24]

    pair_body(
        list_ref,
        count_ref[0, 0],
        count_ref[0, 1],
        None,
        NDEV,
        get_source,
        get_target,
        force_ref,
        scratch,
    )


def finish_kernel(codes_ref, stress_ref, parts_ref, near_ref, x_ref, vel_ref, out_ref):
    core, x_index = codes_ref[6, 0], codes_ref[6, 2]
    row = sublane()
    lane = lax.broadcasted_iota(jnp.int32, (8, SEG), 1)
    spare = lax.bitwise_and(row, 3) == 3
    top = jnp.zeros((1, SEG), F32)
    for side, s in [(side, s) for side in range(NC) for s in range(NX)]:
        x_tile = x_ref[side, s, 0:8]
        l_tile = near_ref[side, s, 8:16]
        b_tile = near_ref[side, s, 16:24]
        rows = []
        for block in range(2):
            b = burgers_rows(l_tile, b_tile, block)
            line = [l_tile[4 * block + a : 4 * block + a + 1] for a in range(3)]
            pulled = [
                stress_ref[a, 0] * b[0] + stress_ref[a, 1] * b[1] + stress_ref[a, 2] * b[2]
                for a in range(3)
            ]
            rows.append(pulled[1] * line[2] - pulled[2] * line[1])
            rows.append(pulled[2] * line[0] - pulled[0] * line[2])
            rows.append(pulled[0] * line[1] - pulled[1] * line[0])
            rows.append(jnp.zeros((1, SEG), F32))
        applied = jnp.concatenate(rows, axis=0)
        left = jnp.where(lane == 0, x_tile, pltpu.roll(x_tile, 1, 1))
        right = jnp.where(lane == SEG - 1, x_tile, pltpu.roll(x_tile, SEG - 1, 1))
        chain = left + right - 2.0 * x_tile
        at = NC * lax.bitwise_and(x_index - s, NX - 1)
        pair = parts_ref[at, side] + parts_ref[at + 1, side]
        drag = jnp.where(row < 4, b_tile[4:5], b_tile[5:6])
        velocity = (COUPLE * pair + applied + TENSION * chain) / drag
        velocity = jnp.where(spare, 0.0, velocity)
        vel_ref[side, s] = velocity
        speed = velocity * velocity
        top = jnp.maximum(top, speed[0:1] + speed[1:2] + speed[2:3])
        top = jnp.maximum(top, speed[4:5] + speed[5:6] + speed[6:7])
    send = top if out_ref.shape[1] == 1 else jnp.where(row == 3, top, vel_ref[core, 0])
    out_ref[...] = jnp.broadcast_to(send[None], out_ref.shape)


def pack_kernel(seg_ref, drag_ref, send_ref, part_ref, raw_ref, out_ref):
    raw_ref[...] = jnp.zeros((24, SEG), F32)
    for block in range(2):
        for comp in range(3):
            raw_ref[4 * block + comp, :] = seg_ref[comp, block, :]
            raw_ref[8 + 4 * block + comp, :] = seg_ref[3 + comp, block, :]
        raw_ref[11 + 4 * block, :] = seg_ref[6, block, :]
        raw_ref[16 + 2 * block, :] = seg_ref[7, block, :]
        raw_ref[17 + 2 * block, :] = seg_ref[8, block, :]
        raw_ref[20 + block, :] = drag_ref[block, :]
    raw_ref[3, :] = send_ref[0, :].astype(F32)
    raw_ref[7, :] = part_ref[0, :].astype(F32)
    for at in range(5):
        rows = raw_ref[4 * at : 4 * at + 4, :]
        for peer in range(NZ):
            out_ref[peer, at] = rows


def last_kernel(codes_ref, top_ref, x_ref, vel_ref, pos_out, vel_out):
    core = codes_ref[6, 0]
    top = jnp.max(jnp.max(top_ref[...], axis=0), axis=1, keepdims=True)
    step = STEP_LENGTH / (jnp.sqrt(top) + EPSILON)
    velocity = vel_ref[core, 0]
    moved = x_ref[core, 0] + step * velocity
    for block in range(2):
        for comp in range(3):
            pos_out[comp, block, :] = moved[4 * block + comp]
            vel_out[comp, block, :] = velocity[4 * block + comp]


SMEM = pl.BlockSpec(memory_space=pltpu.SMEM)
VMEM = pl.BlockSpec(memory_space=pltpu.VMEM)


def shape(*dims, dtype=F32):
    return jax.ShapeDtypeStruct(dims, dtype)


def call(kernel, name, operands, outs, smem_in=0, smem_out=0, scratch=(), mib=4, cost=None):
    return pl.pallas_call(
        kernel,
        name=name,
        in_specs=[SMEM] * smem_in + [VMEM] * (len(operands) - smem_in),
        out_specs=[VMEM] * (len(outs) - smem_out) + [SMEM] * smem_out,
        out_shape=outs,
        scratch_shapes=scratch,
        compiler_params=pltpu.CompilerParams(vmem_limit_bytes=mib << 20),
        cost_estimate=cost,
    )(*operands)


def pass_x(value, shift):
    return lax.ppermute(value, "x", [(i, (i + shift) % NX) for i in range(NX)])


def exchange(value, axes):
    return lax.all_to_all(value, axes, 0, 0, tiled=True)


def local(segments, stress, drag_coef, send_ids, partner_ids):
    core = lax.axis_index("c")
    y_index = lax.axis_index("y")
    x_index = lax.axis_index("x")
    chip_index = y_index * NZ + lax.axis_index("z")
    raw, to_z = call(
        pack_kernel,
        "pack",
        (
            segments.transpose(1, 0, 2),
            drag_coef,
            send_ids.reshape(1, SEG),
            partner_ids.reshape(1, SEG),
        ),
        [shape(24, SEG), shape(NZ, 5, 4, SEG)],
        mib=56,
    )
    along_z = exchange(to_z, "z")
    group = [raw] + [pass_x(raw, shift) for shift in range(1, NX)]
    near = lax.all_gather(jnp.stack(group), "c", axis=0)
    chip = near[:, 0]

    lane = lax.broadcasted_iota(jnp.int32, (NC, SEG), 1)
    side = lax.broadcasted_iota(jnp.int32, (NC, SEG), 0)
    even = lax.bitwise_and(lane, SEG - 2)
    sent = chip[:, 3].astype(jnp.int32)
    other = chip[:, 7].astype(jnp.int32)
    out = jnp.where(sent >= 0, even + other + 256 * (2 * side + sent), -1)
    first = lane[0:1]
    where = jnp.where(first == 0, core, jnp.where(first == 1, y_index, x_index))
    zero = jnp.zeros((1, SEG), jnp.int32)
    known = jnp.concatenate([out, zero, zero, where, zero], axis=0)
    nothing = jnp.zeros((NC, SEG), jnp.int32)
    pick = (lane == 2 * chip_index + side).astype(F32)

    everyone = exchange(
        jnp.broadcast_to(along_z.reshape(1, NZ * 5, 4, SEG), (NY, NZ * 5, 4, SEG)), "y"
    ).reshape(NDEV, 5, 4, SEG)
    (near_force,) = call(
        near_kernel,
        "near_pairs",
        (jnp.concatenate([nothing, known], axis=0), along_z, near),
        [shape(NC, 8, SEG)],
        smem_in=1,
        scratch=[pltpu.SMEM((1, 128), jnp.int32)] + scratch_of(NZ),
        mib=8,
        cost=pl.CostEstimate(flops=1 << 30, bytes_accessed=1 << 24, transcendentals=1 << 20),
    )
    everyone, near_force = lax.optimization_barrier((everyone, near_force))
    lists = everyone[:, 0:2, 3].reshape(2 * NDEV, SEG)
    incoming = lax.dot_general(
        pick, lists, (((1,), (1,)), ((), ())), precision=lax.Precision.HIGHEST
    ).astype(jnp.int32)
    partner = jnp.concatenate([incoming[:, 1:], incoming[:, :1]], axis=1)
    into = jnp.where(incoming >= 0, even + incoming + 256 * (2 * side + partner), -1)
    codes = jnp.concatenate([into, known], axis=0)

    force, items, count = call(
        first_kernel,
        "first_pairs",
        (codes, everyone, near, near_force),
        [
            shape(NC, 8, SEG),
            shape(1, LIST, dtype=jnp.int32),
            shape(1, 2, dtype=jnp.int32),
        ],
        smem_in=1,
        smem_out=2,
        scratch=scratch_of(NDEV),
        mib=16,
    )
    def finish(force, position, peers, name):
        return call(
            finish_kernel,
            name,
            (codes, stress, exchange(jnp.broadcast_to(force[None], (8, *force.shape)), ("x", "c")), near, position),
            [shape(NC, NX, 8, SEG), shape(*peers, SEG)],
            smem_in=2,
        )

    near_vel, to_z = finish(force, near, (NZ, 8), "finish")
    along_z = exchange(to_z, "z").reshape(1, NZ * 8, SEG)
    vel_all = exchange(jnp.broadcast_to(along_z, (NY, NZ * 8, SEG)), "y").reshape(NDEV, 8, SEG)

    force, position = call(
        second_kernel,
        "second_pairs",
        (codes, items, count, everyone, near, vel_all, near_vel),
        [shape(NC, 8, SEG), shape(NC, NX, 8, SEG)],
        smem_in=3,
        scratch=scratch_of(NDEV),
        mib=16,
    )
    near_vel, to_all = finish(force, position, (NDEV, 1), "finish_last")
    tops = exchange(to_all, ("y", "z"))
    positions, velocity = call(
        last_kernel,
        "last",
        (codes, tops, position, near_vel),
        [shape(3, 2, SEG), shape(3, 2, SEG)],
        smem_in=1,
    )
    return positions.transpose(1, 0, 2), velocity.transpose(1, 0, 2)


def solution(mesh):
    split = Mesh(
        mesh.devices.reshape(NY, NZ, NC, mesh.shape["sub"]), ("y", "z", "c", "x")
    )
    return jax.shard_map(
        local,
        mesh=split,
        in_specs=(
            P(DOM_SUB, None, None),
            P(),
            P(DOM_SUB, None),
            P(DOM_SUB, None, None),
            P(DOM_SUB, None, None),
        ),
        out_specs=(P(DOM_SUB, None, None), P(DOM_SUB, None, None)),
        check_vma=False,
    )
```

```python
import functools

import jax
import jax.numpy as jnp
from jax import lax
from jax.experimental import pallas as pl
from jax.experimental.pallas import tpu as pltpu
from jax.sharding import Mesh
from jax.sharding import PartitionSpec as P

NY, NZ, NC = 4, 16, 2
DOM = ("y", "z", "c")
DOM_SUB = ("y", "z", "c", "x")

COUPLE = 0.0625
CORE_SQUARE = 0.5
TENSION = 0.25
STEP_LENGTH = 1.0
EPSILON = 1e-06

SEG = 128
NDEV = NY * NZ
NX = 4
BATCH = 32
LIST = 320
F32 = jnp.float32
BF16 = jnp.bfloat16


def sublane(shape=(8, SEG)):
    return lax.broadcasted_iota(jnp.int32, shape, len(shape) - 2)


def up(value, count):
    return jnp.concatenate([value[count:], value[:count]], axis=0)


def split2(value):
    high = value.astype(BF16).astype(F32)
    return high, value - high


def split3(value):
    high, rest = split2(value)
    mid, low = split2(rest)
    return high, mid, low


def source_operands(x_tile, l_tile, b_tile):
    row = sublane()
    x_tile = jnp.where(lax.bitwise_and(row, 3) < 3, x_tile, 0.0)
    square = x_tile * x_tile
    norm0 = square[0:1] + square[1:2] + square[2:3] + CORE_SQUARE
    norm1 = square[4:5] + square[5:6] + square[6:7] + CORE_SQUARE
    full = jnp.where(row == 3, norm0, jnp.where(row == 7, norm1, x_tile))
    high, mid, low = split3(full)
    dist = [high, mid, high, mid, low, high, jnp.ones_like(high)]
    burgers = [burgers_rows(l_tile, b_tile, block) for block in range(2)]
    prod = [jnp.where(row < 4, burgers[0][a], burgers[1][a]) * l_tile for a in range(3)]
    parts = [split2(p) for p in prod]
    highs = [p[0] for p in parts]
    mids = [p[1] for p in parts]
    weight = highs + highs + mids
    first = (jnp.where(row == 3, 1.0, high), jnp.where(row == 3, 0.0, mid))
    second = (jnp.where(row == 3, 1.0, up(high, 4)), jnp.where(row == 3, 0.0, up(mid, 4)))
    return dist + weight, first, second


def burgers_rows(l_tile, b_tile, block):
    return [
        l_tile[4 * block + 3 : 4 * block + 4],
        b_tile[2 * block : 2 * block + 1],
        b_tile[2 * block + 1 : 2 * block + 2],
    ]


def store_rows(ref, index, tiles):
    for at in range(0, len(tiles), 2):
        pair = jnp.concatenate([tiles[at], tiles[at + 1]], axis=0).astype(BF16)
        ref[index, 8 * at : 8 * at + 16, :] = pair


def target_rows(x_tile, l_tile, b_tile, block):
    row = sublane()

    def both(tile):
        other = up(tile, 4)
        own, far = (tile, other) if block == 0 else (other, tile)
        return jnp.where(lax.bitwise_and(row, 3) == 3, 0.0, jnp.where(row < 4, own, far))

    x_both = both(x_tile)
    high, mid, low = split3(x_both)
    square = x_both * x_both
    norm = square[0:1] + square[1:2] + square[2:3]
    norm_h, norm_m, norm_l = split3(norm)
    unit = jnp.where(lax.bitwise_and(row, 3) == 3, 1.0, 0.0)
    norms = jnp.where(
        row == 0, norm_h, jnp.where(row == 1, norm_m, jnp.where(row == 2, norm_l, 0.0))
    )
    zero = jnp.zeros_like(high)
    dist = [
        -2.0 * high + unit,
        -2.0 * high + unit,
        -2.0 * mid,
        -2.0 * mid,
        -2.0 * high + unit,
        -2.0 * low,
        norms,
    ]
    l_both = both(l_tile)
    prod = [b * l_both for b in burgers_rows(l_tile, b_tile, block)]
    parts = [split2(p) for p in prod]
    highs = [p[0] for p in parts]
    mids = [p[1] for p in parts]
    weight = highs + mids + highs
    return jnp.concatenate(dist + [zero] * 9, axis=0), jnp.concatenate([zero] * 7 + weight, axis=0)


def add_code(list_ref, count, code, keep):
    list_ref[0, count] = code
    return count + keep.astype(jnp.int32)


def add_group(list_ref, count, core, lines):
    for block in range(2):
        for j in range(2 * NX):
            list_ref[0, count + 2 * NX * block + j] = 256 * (2 * core + block) + 2 * lines + j
    count = count + 4 * NX
    for j in range(BATCH):
        list_ref[0, count + j] = 2 * (lines + NX)
    return count


def batches(count):
    whole = lax.div(count + (BATCH // 2 - 1), BATCH)
    return whole, (count > whole * BATCH).astype(jnp.int32)


def build_list(codes_ref, list_ref):
    core, y_index = codes_ref[6, 0], codes_ref[6, 1]

    def add_in(at, count):
        k = lax.bitwise_and(at + NZ * (y_index + 1), NDEV - 1)
        for side in range(NC):
            code = codes_ref[side, 2 * k]
            count = add_code(list_ref, count, code, code >= 0)
        return count

    def add_out(at, count):
        k = lax.bitwise_and(at + NZ * (y_index + 1), NDEV - 1)
        for side in range(NC):
            code = codes_ref[NC + side, 2 * k + core]
            count = add_code(list_ref, count, code, code >= 0)
        return count

    far = NDEV - NZ
    count = lax.fori_loop(0, far, add_in, jnp.int32(0), unroll=8)
    first = lax.fori_loop(0, far, add_out, count, unroll=8)
    count = lax.fori_loop(far, NDEV, add_in, first, unroll=8)
    count = lax.fori_loop(far, NDEV, add_out, count, unroll=8)
    return first, add_group(list_ref, count, core, NDEV)


def build_near_list(codes_ref, into_ref, list_ref):
    core, y_index, chip = codes_ref[6, 0], codes_ref[6, 1], codes_ref[6, 3]

    def add_both(z, count):
        for side in range(NC):
            code = into_ref[z, 2 * chip + side]
            count = add_code(list_ref, count, code, code >= 0)
            code = codes_ref[NC + side, 2 * (NZ * y_index + z) + core]
            count = add_code(list_ref, count, code - 2 * NZ * y_index, code >= 0)
        return count

    count = lax.fori_loop(0, NZ, add_both, jnp.int32(0), unroll=8)
    return add_group(list_ref, count, core, NZ)


def pair_body(
    list_ref, whole, tail, limit, lines, get_source, get_target, force_ref, scratch, more=None
):
    source_s, moment_s, target_s = scratch

    def prepare(k):
        tiles, first, second = source_operands(*get_source(k))
        store_rows(source_s, k, tiles)
        moment_s[2 * k] = jnp.concatenate(first, axis=0).astype(BF16)
        moment_s[2 * k + 1] = jnp.concatenate(second, axis=0).astype(BF16)

    def prepare_loop(k, carry):
        prepare(k)
        return carry

    lax.fori_loop(0, lines, prepare_loop, 0, unroll=4)
    for k in range(lines, lines + NX + 1):
        prepare(k)

    lane = lax.broadcasted_iota(jnp.int32, (SEG, SEG), 1)
    place = lax.bitwise_and(lane, 7)
    for side in range(NC):
        x_tile, l_tile, b_tile = get_target(side)
        for block in range(2):
            dist, weight = target_rows(x_tile, l_tile, b_tile, block)
            dist = dist.T
            weight = weight.T
            for j in range(2):
                mine = (place >= 4 * j) & (place < 4 * j + 3)
                keep = mine | (place == 4 * j + 3) | (lane >= 48)
                at = 2 * (2 * side + block) + j
                target_s[at, 0:SEG] = jnp.where(keep, dist, 0.0).astype(BF16)
                target_s[at, SEG : 2 * SEG] = jnp.where(mine, weight, 0.0).astype(BF16)

    def items(start, size, total):
        lows, highs, moments = [], [], []
        for b in range(size):
            code = list_ref[0, start + b]
            if limit is not None:
                code = jnp.where(start + b < limit, code, 2 * (lines + NX))
            n = lax.shift_right_logical(code, 8)
            m = lax.bitwise_and(code, 255)
            at = 2 * n + lax.bitwise_and(m, 1)
            both = jnp.dot(
                target_s[at], source_s[lax.shift_right_logical(m, 1)], preferred_element_type=F32
            )
            inverse = lax.rsqrt(both[0:SEG])
            w = both[SEG : 2 * SEG] * (inverse * inverse * inverse)
            high = w.astype(BF16)
            highs.append(high)
            lows.append((w - high.astype(F32)).astype(BF16))
            moment = moment_s[m]
            zero = jnp.zeros_like(moment)
            moments.append(
                jnp.concatenate([jnp.where(n == t, moment, zero) for t in range(4)], axis=0)
            )
        sums = lax.dot_general(
            jnp.concatenate(
                [jnp.concatenate(highs, axis=1), jnp.concatenate(lows, axis=1)], axis=0
            ),
            jnp.concatenate(moments, axis=1),
            (((1,), (1,)), ((), ())),
            preferred_element_type=F32,
        )
        return total + sums[0:SEG] + sums[SEG : 2 * SEG]

    total = lax.fori_loop(
        0,
        whole,
        lambda step, total: items(step * BATCH, BATCH, total),
        jnp.zeros((SEG, 64), F32),
    )
    total = lax.fori_loop(
        0, tail, lambda step, total: items(whole * BATCH, BATCH // 2, total), total
    )
    total = jnp.concatenate([total, jnp.zeros((SEG, SEG - 64), F32)], axis=1).T
    for side in range(NC):
        x_tile = get_target(side)[0]
        rows = []
        for block in range(2):
            at = 16 * (2 * side + block)
            x_block = x_tile[4 * block : 4 * block + 3]
            rows.append(
                x_block * total[at + 3 : at + 4] - (total[at : at + 3] + total[at + 8 : at + 11])
            )
            rows.append(jnp.zeros((1, SEG), F32))
        force = jnp.concatenate(rows, axis=0)
        force_ref[side] = force if more is None else force + more[side]


def scratch_of(lines):
    return [
        pltpu.VMEM((lines + NX + 1, SEG, SEG), BF16),
        pltpu.VMEM((2 * (lines + NX + 1), 16, SEG), BF16),
        pltpu.VMEM((8, 2 * SEG, SEG), BF16),
    ]


def tiles_of(tile):
    return tile[0:8], tile[8:16], tile[16:24]


def tiles_of_rows(rows):
    return (
        jnp.concatenate([rows[0], rows[1]], axis=0),
        jnp.concatenate([rows[2], rows[3]], axis=0),
        rows[4],
    )


def no_source():
    zero = jnp.zeros((8, SEG), F32)
    return zero, zero, zero


def near_kernel(codes_ref, into_ref, line_ref, near_ref, force_ref, list_s, *scratch):
    count = build_near_list(codes_ref, into_ref, list_s)
    core = codes_ref[6, 0]

    def get_source(k):
        if isinstance(k, int):
            return no_source() if k == NZ + NX else tiles_of(near_ref.at[core, k - NZ])
        return tiles_of_rows(line_ref.at[k])

    def get_target(side):
        return tiles_of(near_ref.at[side, 0])

    pair_body(list_s, *batches(count), None, NZ, get_source, get_target, force_ref, scratch)


def first_kernel(codes_ref, all_ref, near_ref, more_ref, force_ref, list_ref, count_ref, *scratch):
    first, count = build_list(codes_ref, list_ref)
    whole, tail = batches(count)
    count_ref[0, 0] = whole
    count_ref[0, 1] = tail

    def get_source(k):
        return no_source() if isinstance(k, int) else tiles_of_rows(all_ref.at[k])

    def get_target(side):
        return tiles_of(near_ref.at[side, 0])

    pair_body(
        list_ref,
        *batches(first),
        first,
        NDEV,
        get_source,
        get_target,
        force_ref,
        scratch,
        more_ref,
    )


def second_kernel(
    codes_ref,
    list_ref,
    count_ref,
    all_ref,
    near_ref,
    vel_ref,
    near_vel_ref,
    force_ref,
    position_ref,
    *scratch,
):
    core = codes_ref[6, 0]
    top = vel_ref[0]
    for k in range(1, NDEV):
        top = jnp.maximum(top, vel_ref[k])
    top = jnp.max(top[3:4], axis=1, keepdims=True)
    step = STEP_LENGTH / (jnp.sqrt(top) + EPSILON)
    for side in range(NC):
        for s in range(NX):
            position_ref[side, s] = near_ref[side, s, 0:8] + step * near_vel_ref[side, s]

    def get_source(k):
        if isinstance(k, int):
            if k == NDEV + NX:
                return no_source()
            tile = near_ref.at[core, k - NDEV]
            return position_ref[core, k - NDEV], tile[8:16], tile[16:24]
        x_tile, l_tile, b_tile = tiles_of_rows(all_ref.at[k])
        return x_tile + step * vel_ref[k], l_tile, b_tile

    def get_target(side):
        return position_ref[side, 0], near_ref[side, 0, 8:16], near_ref[side, 0, 16:24]

    pair_body(
        list_ref,
        count_ref[0, 0],
        count_ref[0, 1],
        None,
        NDEV,
        get_source,
        get_target,
        force_ref,
        scratch,
    )


def finish_kernel(codes_ref, stress_ref, parts_ref, near_ref, x_ref, vel_ref, out_ref):
    core, x_index = codes_ref[6, 0], codes_ref[6, 2]
    row = sublane()
    lane = lax.broadcasted_iota(jnp.int32, (8, SEG), 1)
    spare = lax.bitwise_and(row, 3) == 3
    top = jnp.zeros((1, SEG), F32)
    for side, s in [(side, s) for side in range(NC) for s in range(NX)]:
        x_tile = x_ref[side, s, 0:8]
        l_tile = near_ref[side, s, 8:16]
        b_tile = near_ref[side, s, 16:24]
        rows = []
        for block in range(2):
            b = burgers_rows(l_tile, b_tile, block)
            line = [l_tile[4 * block + a : 4 * block + a + 1] for a in range(3)]
            pulled = [
                stress_ref[a, 0] * b[0] + stress_ref[a, 1] * b[1] + stress_ref[a, 2] * b[2]
                for a in range(3)
            ]
            rows.append(pulled[1] * line[2] - pulled[2] * line[1])
            rows.append(pulled[2] * line[0] - pulled[0] * line[2])
            rows.append(pulled[0] * line[1] - pulled[1] * line[0])
            rows.append(jnp.zeros((1, SEG), F32))
        applied = jnp.concatenate(rows, axis=0)
        left = jnp.where(lane == 0, x_tile, pltpu.roll(x_tile, 1, 1))
        right = jnp.where(lane == SEG - 1, x_tile, pltpu.roll(x_tile, SEG - 1, 1))
        chain = left + right - 2.0 * x_tile
        at = NC * lax.bitwise_and(x_index - s, NX - 1)
        pair = parts_ref[at, side] + parts_ref[at + 1, side]
        drag = jnp.where(row < 4, b_tile[4:5], b_tile[5:6])
        velocity = (COUPLE * pair + applied + TENSION * chain) / drag
        velocity = jnp.where(spare, 0.0, velocity)
        vel_ref[side, s] = velocity
        speed = velocity * velocity
        top = jnp.maximum(top, speed[0:1] + speed[1:2] + speed[2:3])
        top = jnp.maximum(top, speed[4:5] + speed[5:6] + speed[6:7])
    send = top if out_ref.shape[1] == 1 else jnp.where(row == 3, top, vel_ref[core, 0])
    out_ref[...] = jnp.broadcast_to(send[None], out_ref.shape)


def pack_kernel(seg_ref, drag_ref, send_ref, part_ref, raw_ref, out_ref):
    raw_ref[...] = jnp.zeros((24, SEG), F32)
    for block in range(2):
        for comp in range(3):
            raw_ref[4 * block + comp, :] = seg_ref[comp, block, :]
            raw_ref[8 + 4 * block + comp, :] = seg_ref[3 + comp, block, :]
        raw_ref[11 + 4 * block, :] = seg_ref[6, block, :]
        raw_ref[16 + 2 * block, :] = seg_ref[7, block, :]
        raw_ref[17 + 2 * block, :] = seg_ref[8, block, :]
        raw_ref[20 + block, :] = drag_ref[block, :]
    raw_ref[3, :] = send_ref[0, :].astype(F32)
    raw_ref[7, :] = part_ref[0, :].astype(F32)
    for at in range(5):
        rows = raw_ref[4 * at : 4 * at + 4, :]
        for peer in range(NZ):
            out_ref[peer, at] = rows


def last_kernel(codes_ref, top_ref, x_ref, vel_ref, pos_out, vel_out):
    core = codes_ref[6, 0]
    top = jnp.max(jnp.max(top_ref[...], axis=0), axis=1, keepdims=True)
    step = STEP_LENGTH / (jnp.sqrt(top) + EPSILON)
    velocity = vel_ref[core, 0]
    moved = x_ref[core, 0] + step * velocity
    for block in range(2):
        for comp in range(3):
            pos_out[comp, block, :] = moved[4 * block + comp]
            vel_out[comp, block, :] = velocity[4 * block + comp]


SMEM = pl.BlockSpec(memory_space=pltpu.SMEM)
VMEM = pl.BlockSpec(memory_space=pltpu.VMEM)


def shape(*dims, dtype=F32):
    return jax.ShapeDtypeStruct(dims, dtype)


def call(kernel, name, operands, outs, smem_in=0, smem_out=0, scratch=(), mib=4, cost=None):
    return pl.pallas_call(
        kernel,
        name=name,
        in_specs=[SMEM] * smem_in + [VMEM] * (len(operands) - smem_in),
        out_specs=[VMEM] * (len(outs) - smem_out) + [SMEM] * smem_out,
        out_shape=outs,
        scratch_shapes=scratch,
        compiler_params=pltpu.CompilerParams(vmem_limit_bytes=mib << 20),
        cost_estimate=cost,
    )(*operands)


def pass_x(value, shift):
    return lax.ppermute(value, "x", [(i, (i + shift) % NX) for i in range(NX)])


def exchange(value, axes):
    return lax.all_to_all(value, axes, 0, 0, tiled=True)


def local(segments, stress, drag_coef, send_ids, partner_ids):
    core = lax.axis_index("c")
    y_index = lax.axis_index("y")
    x_index = lax.axis_index("x")
    chip_index = y_index * NZ + lax.axis_index("z")
    raw, to_z = call(
        pack_kernel,
        "pack",
        (
            segments.transpose(1, 0, 2),
            drag_coef,
            send_ids.reshape(1, SEG),
            partner_ids.reshape(1, SEG),
        ),
        [shape(24, SEG), shape(NZ, 5, 4, SEG)],
        mib=56,
    )
    along_z = exchange(to_z, "z")
    group = [raw] + [pass_x(raw, shift) for shift in range(1, NX)]
    near = lax.all_gather(jnp.stack(group), "c", axis=0)
    chip = near[:, 0]

    lane = lax.broadcasted_iota(jnp.int32, (NC, SEG), 1)
    side = lax.broadcasted_iota(jnp.int32, (NC, SEG), 0)
    even = lax.bitwise_and(lane, SEG - 2)
    sent = chip[:, 3].astype(jnp.int32)
    other = chip[:, 7].astype(jnp.int32)
    out = jnp.where(sent >= 0, even + other + 256 * (2 * side + sent), -1)
    first = lane[0:1]
    where = jnp.where(first == 0, core, jnp.where(first == 1, y_index, x_index))
    where = jnp.where(first == 3, chip_index, where)
    zero = jnp.zeros((1, SEG), jnp.int32)
    known = jnp.concatenate([out, zero, zero, where, zero], axis=0)
    nothing = jnp.zeros((NC, SEG), jnp.int32)
    pick = (lane == 2 * chip_index + side).astype(F32)

    near_sent = along_z[:, 0, 3].astype(jnp.int32)
    near_part = along_z[:, 1, 3].astype(jnp.int32)
    z_row = lax.broadcasted_iota(jnp.int32, (NZ, SEG), 0)
    target = lax.bitwise_and(lax.broadcasted_iota(jnp.int32, (NZ, SEG), 1), 1)
    near_into = jnp.where(
        near_sent >= 0, 2 * z_row + near_sent + 256 * (2 * target + near_part), -1
    )
    along_z, near_into = lax.optimization_barrier((along_z, near_into))
    everyone = exchange(
        jnp.broadcast_to(along_z.reshape(1, NZ * 5, 4, SEG), (NY, NZ * 5, 4, SEG)), "y"
    ).reshape(NDEV, 5, 4, SEG)
    (near_force,) = call(
        near_kernel,
        "near_pairs",
        (jnp.concatenate([nothing, known], axis=0), near_into, along_z, near),
        [shape(NC, 8, SEG)],
        smem_in=2,
        scratch=[pltpu.SMEM((1, 128), jnp.int32)] + scratch_of(NZ),
        mib=8,
        cost=pl.CostEstimate(flops=1 << 30, bytes_accessed=1 << 24, transcendentals=1 << 20),
    )
    everyone, near_force = lax.optimization_barrier((everyone, near_force))
    lists = everyone[:, 0:2, 3].reshape(2 * NDEV, SEG)
    incoming = lax.dot_general(
        pick, lists, (((1,), (1,)), ((), ())), precision=lax.Precision.HIGHEST
    ).astype(jnp.int32)
    partner = jnp.concatenate([incoming[:, 1:], incoming[:, :1]], axis=1)
    into = jnp.where(incoming >= 0, even + incoming + 256 * (2 * side + partner), -1)
    codes = jnp.concatenate([into, known], axis=0)

    force, items, count = call(
        first_kernel,
        "first_pairs",
        (codes, everyone, near, near_force),
        [
            shape(NC, 8, SEG),
            shape(1, LIST, dtype=jnp.int32),
            shape(1, 2, dtype=jnp.int32),
        ],
        smem_in=1,
        smem_out=2,
        scratch=scratch_of(NDEV),
        mib=16,
    )
    def finish(force, position, peers, name):
        return call(
            finish_kernel,
            name,
            (codes, stress, exchange(jnp.broadcast_to(force[None], (8, *force.shape)), ("x", "c")), near, position),
            [shape(NC, NX, 8, SEG), shape(*peers, SEG)],
            smem_in=2,
        )

    near_vel, to_z = finish(force, near, (NZ, 8), "finish")
    along_z = exchange(to_z, "z").reshape(1, NZ * 8, SEG)
    vel_all = exchange(jnp.broadcast_to(along_z, (NY, NZ * 8, SEG)), "y").reshape(NDEV, 8, SEG)

    force, position = call(
        second_kernel,
        "second_pairs",
        (codes, items, count, everyone, near, vel_all, near_vel),
        [shape(NC, 8, SEG), shape(NC, NX, 8, SEG)],
        smem_in=3,
        scratch=scratch_of(NDEV),
        mib=16,
    )
    near_vel, to_all = finish(force, position, (NDEV, 1), "finish_last")
    tops = exchange(to_all, ("y", "z"))
    positions, velocity = call(
        last_kernel,
        "last",
        (codes, tops, position, near_vel),
        [shape(3, 2, SEG), shape(3, 2, SEG)],
        smem_in=1,
    )
    return positions.transpose(1, 0, 2), velocity.transpose(1, 0, 2)


def solution(mesh):
    split = Mesh(
        mesh.devices.reshape(NY, NZ, NC, mesh.shape["sub"]), ("y", "z", "c", "x")
    )
    return jax.shard_map(
        local,
        mesh=split,
        in_specs=(
            P(DOM_SUB, None, None),
            P(),
            P(DOM_SUB, None),
            P(DOM_SUB, None, None),
            P(DOM_SUB, None, None),
        ),
        out_specs=(P(DOM_SUB, None, None), P(DOM_SUB, None, None)),
        check_vma=False,
    )
```

```python
import functools

import jax
import jax.numpy as jnp
from jax import lax
from jax.experimental import pallas as pl
from jax.experimental.pallas import tpu as pltpu
from jax.sharding import Mesh
from jax.sharding import PartitionSpec as P

NY, NZ, NC = 4, 16, 2
DOM = ("y", "z", "c")
DOM_SUB = ("y", "z", "c", "x")

COUPLE = 0.0625
CORE_SQUARE = 0.5
TENSION = 0.25
STEP_LENGTH = 1.0
EPSILON = 1e-06

SEG = 128
NDEV = NY * NZ
NX = 4
BATCH = 32
LIST = 320
F32 = jnp.float32
BF16 = jnp.bfloat16


def sublane(shape=(8, SEG)):
    return lax.broadcasted_iota(jnp.int32, shape, len(shape) - 2)


def up(value, count):
    return jnp.concatenate([value[count:], value[:count]], axis=0)


def split2(value):
    high = value.astype(BF16).astype(F32)
    return high, value - high


def split3(value):
    high, rest = split2(value)
    mid, low = split2(rest)
    return high, mid, low


def source_operands(x_tile, l_tile, b_tile):
    row = sublane()
    x_tile = jnp.where(lax.bitwise_and(row, 3) < 3, x_tile, 0.0)
    square = x_tile * x_tile
    norm0 = square[0:1] + square[1:2] + square[2:3] + CORE_SQUARE
    norm1 = square[4:5] + square[5:6] + square[6:7] + CORE_SQUARE
    full = jnp.where(row == 3, norm0, jnp.where(row == 7, norm1, x_tile))
    high, mid, low = split3(full)
    dist = [high, mid, high, mid, low, high, jnp.ones_like(high)]
    burgers = [burgers_rows(l_tile, b_tile, block) for block in range(2)]
    prod = [jnp.where(row < 4, burgers[0][a], burgers[1][a]) * l_tile for a in range(3)]
    parts = [split2(p) for p in prod]
    highs = [p[0] for p in parts]
    mids = [p[1] for p in parts]
    weight = highs + highs + mids
    first = (jnp.where(row == 3, 1.0, high), jnp.where(row == 3, 0.0, mid))
    second = (jnp.where(row == 3, 1.0, up(high, 4)), jnp.where(row == 3, 0.0, up(mid, 4)))
    return dist + weight, first, second


def burgers_rows(l_tile, b_tile, block):
    return [
        l_tile[4 * block + 3 : 4 * block + 4],
        b_tile[2 * block : 2 * block + 1],
        b_tile[2 * block + 1 : 2 * block + 2],
    ]


def store_rows(ref, index, tiles):
    for at in range(0, len(tiles), 2):
        pair = jnp.concatenate([tiles[at], tiles[at + 1]], axis=0).astype(BF16)
        ref[index, 8 * at : 8 * at + 16, :] = pair


def target_rows(x_tile, l_tile, b_tile, block):
    row = sublane()

    def both(tile):
        other = up(tile, 4)
        own, far = (tile, other) if block == 0 else (other, tile)
        return jnp.where(lax.bitwise_and(row, 3) == 3, 0.0, jnp.where(row < 4, own, far))

    x_both = both(x_tile)
    high, mid, low = split3(x_both)
    square = x_both * x_both
    norm = square[0:1] + square[1:2] + square[2:3]
    norm_h, norm_m, norm_l = split3(norm)
    unit = jnp.where(lax.bitwise_and(row, 3) == 3, 1.0, 0.0)
    norms = jnp.where(
        row == 0, norm_h, jnp.where(row == 1, norm_m, jnp.where(row == 2, norm_l, 0.0))
    )
    zero = jnp.zeros_like(high)
    dist = [
        -2.0 * high + unit,
        -2.0 * high + unit,
        -2.0 * mid,
        -2.0 * mid,
        -2.0 * high + unit,
        -2.0 * low,
        norms,
    ]
    l_both = both(l_tile)
    prod = [b * l_both for b in burgers_rows(l_tile, b_tile, block)]
    parts = [split2(p) for p in prod]
    highs = [p[0] for p in parts]
    mids = [p[1] for p in parts]
    weight = highs + mids + highs
    return jnp.concatenate(dist + [zero] * 9, axis=0), jnp.concatenate([zero] * 7 + weight, axis=0)


def add_code(list_ref, count, code, keep):
    list_ref[0, count] = code
    return count + keep.astype(jnp.int32)


def add_group(list_ref, count, core, lines):
    for block in range(2):
        for j in range(2 * NX):
            list_ref[0, count + 2 * NX * block + j] = 256 * (2 * core + block) + 2 * lines + j
    count = count + 4 * NX
    for j in range(BATCH):
        list_ref[0, count + j] = 2 * (lines + NX)
    return count


def batches(count):
    whole = lax.div(count + (BATCH // 2 - 1), BATCH)
    return whole, (count > whole * BATCH).astype(jnp.int32)


def build_list(codes_ref, list_ref):
    core, y_index = codes_ref[6, 0], codes_ref[6, 1]

    def add_in(at, count):
        k = lax.bitwise_and(at + NZ * (y_index + 1), NDEV - 1)
        for side in range(NC):
            code = codes_ref[side, 2 * k]
            count = add_code(list_ref, count, code, code >= 0)
        return count

    def add_out(at, count):
        k = lax.bitwise_and(at + NZ * (y_index + 1), NDEV - 1)
        for side in range(NC):
            code = codes_ref[NC + side, 2 * k + core]
            count = add_code(list_ref, count, code, code >= 0)
        return count

    far = NDEV - NZ
    count = lax.fori_loop(0, far, add_in, jnp.int32(0), unroll=8)
    first = lax.fori_loop(0, far, add_out, count, unroll=8)
    count = lax.fori_loop(far, NDEV, add_in, first, unroll=8)
    count = lax.fori_loop(far, NDEV, add_out, count, unroll=8)
    return first, add_group(list_ref, count, core, NDEV)


def build_near_list(codes_ref, into_ref, list_ref):
    core, y_index, chip = codes_ref[6, 0], codes_ref[6, 1], codes_ref[6, 3]

    def add_both(z, count):
        for side in range(NC):
            code = into_ref[z, 2 * chip + side]
            count = add_code(list_ref, count, code, code >= 0)
            code = codes_ref[NC + side, 2 * (NZ * y_index + z) + core]
            count = add_code(list_ref, count, code - 2 * NZ * y_index, code >= 0)
        return count

    count = lax.fori_loop(0, NZ, add_both, jnp.int32(0), unroll=8)
    return add_group(list_ref, count, core, NZ)


def pair_body(
    list_ref, whole, tail, limit, lines, get_source, get_target, force_ref, scratch, more=None, far=None
):
    source_s, moment_s, target_s = scratch

    def prepare(k):
        tiles, first, second = source_operands(*get_source(k))
        store_rows(source_s, k, tiles)
        moment_s[2 * k] = jnp.concatenate(first, axis=0).astype(BF16)
        moment_s[2 * k + 1] = jnp.concatenate(second, axis=0).astype(BF16)

    def prepare_loop(at, carry):
        prepare(at if far is None else lax.bitwise_and(at + far, NDEV - 1))
        return carry

    lax.fori_loop(0, lines if far is None else NDEV - NZ, prepare_loop, 0, unroll=4)
    for k in range(lines, lines + NX + 1):
        prepare(k)

    lane = lax.broadcasted_iota(jnp.int32, (SEG, SEG), 1)
    place = lax.bitwise_and(lane, 7)
    for side in range(NC):
        x_tile, l_tile, b_tile = get_target(side)
        for block in range(2):
            dist, weight = target_rows(x_tile, l_tile, b_tile, block)
            dist = dist.T
            weight = weight.T
            for j in range(2):
                mine = (place >= 4 * j) & (place < 4 * j + 3)
                keep = mine | (place == 4 * j + 3) | (lane >= 48)
                at = 2 * (2 * side + block) + j
                target_s[at, 0:SEG] = jnp.where(keep, dist, 0.0).astype(BF16)
                target_s[at, SEG : 2 * SEG] = jnp.where(mine, weight, 0.0).astype(BF16)

    def items(start, size, total):
        lows, highs, moments = [], [], []
        for b in range(size):
            code = list_ref[0, start + b]
            if limit is not None:
                code = jnp.where(start + b < limit, code, 2 * (lines + NX))
            n = lax.shift_right_logical(code, 8)
            m = lax.bitwise_and(code, 255)
            at = 2 * n + lax.bitwise_and(m, 1)
            both = jnp.dot(
                target_s[at], source_s[lax.shift_right_logical(m, 1)], preferred_element_type=F32
            )
            inverse = lax.rsqrt(both[0:SEG])
            w = both[SEG : 2 * SEG] * (inverse * inverse * inverse)
            high = w.astype(BF16)
            highs.append(high)
            lows.append((w - high.astype(F32)).astype(BF16))
            moment = moment_s[m]
            zero = jnp.zeros_like(moment)
            moments.append(
                jnp.concatenate([jnp.where(n == t, moment, zero) for t in range(4)], axis=0)
            )
        sums = lax.dot_general(
            jnp.concatenate(
                [jnp.concatenate(highs, axis=1), jnp.concatenate(lows, axis=1)], axis=0
            ),
            jnp.concatenate(moments, axis=1),
            (((1,), (1,)), ((), ())),
            preferred_element_type=F32,
        )
        return total + sums[0:SEG] + sums[SEG : 2 * SEG]

    total = lax.fori_loop(
        0,
        whole,
        lambda step, total: items(step * BATCH, BATCH, total),
        jnp.zeros((SEG, 64), F32),
    )
    total = lax.fori_loop(
        0, tail, lambda step, total: items(whole * BATCH, BATCH // 2, total), total
    )
    total = jnp.concatenate([total, jnp.zeros((SEG, SEG - 64), F32)], axis=1).T
    for side in range(NC):
        x_tile = get_target(side)[0]
        rows = []
        for block in range(2):
            at = 16 * (2 * side + block)
            x_block = x_tile[4 * block : 4 * block + 3]
            rows.append(
                x_block * total[at + 3 : at + 4] - (total[at : at + 3] + total[at + 8 : at + 11])
            )
            rows.append(jnp.zeros((1, SEG), F32))
        force = jnp.concatenate(rows, axis=0)
        force_ref[side] = force if more is None else force + more[side]


def scratch_of(lines):
    return [
        pltpu.VMEM((lines + NX + 1, SEG, SEG), BF16),
        pltpu.VMEM((2 * (lines + NX + 1), 16, SEG), BF16),
        pltpu.VMEM((8, 2 * SEG, SEG), BF16),
    ]


def tiles_of(tile):
    return tile[0:8], tile[8:16], tile[16:24]


def tiles_of_rows(rows):
    return (
        jnp.concatenate([rows[0], rows[1]], axis=0),
        jnp.concatenate([rows[2], rows[3]], axis=0),
        rows[4],
    )


def no_source():
    zero = jnp.zeros((8, SEG), F32)
    return zero, zero, zero


def near_kernel(codes_ref, into_ref, line_ref, near_ref, force_ref, list_s, *scratch):
    count = build_near_list(codes_ref, into_ref, list_s)
    core = codes_ref[6, 0]

    def get_source(k):
        if isinstance(k, int):
            return no_source() if k == NZ + NX else tiles_of(near_ref.at[core, k - NZ])
        return tiles_of_rows(line_ref.at[k])

    def get_target(side):
        return tiles_of(near_ref.at[side, 0])

    pair_body(list_s, *batches(count), None, NZ, get_source, get_target, force_ref, scratch)


def first_kernel(codes_ref, all_ref, near_ref, more_ref, force_ref, list_ref, count_ref, *scratch):
    first, count = build_list(codes_ref, list_ref)
    whole, tail = batches(count)
    count_ref[0, 0] = whole
    count_ref[0, 1] = tail

    def get_source(k):
        return no_source() if isinstance(k, int) else tiles_of_rows(all_ref.at[k])

    def get_target(side):
        return tiles_of(near_ref.at[side, 0])

    pair_body(
        list_ref,
        *batches(first),
        first,
        NDEV,
        get_source,
        get_target,
        force_ref,
        scratch,
        more_ref,
        NZ * (codes_ref[6, 1] + 1),
    )


def second_kernel(
    codes_ref,
    list_ref,
    count_ref,
    all_ref,
    near_ref,
    vel_ref,
    near_vel_ref,
    force_ref,
    position_ref,
    *scratch,
):
    core = codes_ref[6, 0]
    top = vel_ref[0]
    for k in range(1, NDEV):
        top = jnp.maximum(top, vel_ref[k])
    top = jnp.max(top[3:4], axis=1, keepdims=True)
    step = STEP_LENGTH / (jnp.sqrt(top) + EPSILON)
    for side in range(NC):
        for s in range(NX):
            position_ref[side, s] = near_ref[side, s, 0:8] + step * near_vel_ref[side, s]

    def get_source(k):
        if isinstance(k, int):
            if k == NDEV + NX:
                return no_source()
            tile = near_ref.at[core, k - NDEV]
            return position_ref[core, k - NDEV], tile[8:16], tile[16:24]
        x_tile, l_tile, b_tile = tiles_of_rows(all_ref.at[k])
        return x_tile + step * vel_ref[k], l_tile, b_tile

    def get_target(side):
        return position_ref[side, 0], near_ref[side, 0, 8:16], near_ref[side, 0, 16:24]

    pair_body(
        list_ref,
        count_ref[0, 0],
        count_ref[0, 1],
        None,
        NDEV,
        get_source,
        get_target,
        force_ref,
        scratch,
    )


def finish_kernel(codes_ref, stress_ref, parts_ref, near_ref, x_ref, vel_ref, out_ref):
    core, x_index = codes_ref[6, 0], codes_ref[6, 2]
    row = sublane()
    lane = lax.broadcasted_iota(jnp.int32, (8, SEG), 1)
    spare = lax.bitwise_and(row, 3) == 3
    top = jnp.zeros((1, SEG), F32)
    for side, s in [(side, s) for side in range(NC) for s in range(NX)]:
        x_tile = x_ref[side, s, 0:8]
        l_tile = near_ref[side, s, 8:16]
        b_tile = near_ref[side, s, 16:24]
        rows = []
        for block in range(2):
            b = burgers_rows(l_tile, b_tile, block)
            line = [l_tile[4 * block + a : 4 * block + a + 1] for a in range(3)]
            pulled = [
                stress_ref[a, 0] * b[0] + stress_ref[a, 1] * b[1] + stress_ref[a, 2] * b[2]
                for a in range(3)
            ]
            rows.append(pulled[1] * line[2] - pulled[2] * line[1])
            rows.append(pulled[2] * line[0] - pulled[0] * line[2])
            rows.append(pulled[0] * line[1] - pulled[1] * line[0])
            rows.append(jnp.zeros((1, SEG), F32))
        applied = jnp.concatenate(rows, axis=0)
        left = jnp.where(lane == 0, x_tile, pltpu.roll(x_tile, 1, 1))
        right = jnp.where(lane == SEG - 1, x_tile, pltpu.roll(x_tile, SEG - 1, 1))
        chain = left + right - 2.0 * x_tile
        at = NC * lax.bitwise_and(x_index - s, NX - 1)
        pair = parts_ref[at, side] + parts_ref[at + 1, side]
        drag = jnp.where(row < 4, b_tile[4:5], b_tile[5:6])
        velocity = (COUPLE * pair + applied + TENSION * chain) / drag
        velocity = jnp.where(spare, 0.0, velocity)
        vel_ref[side, s] = velocity
        speed = velocity * velocity
        top = jnp.maximum(top, speed[0:1] + speed[1:2] + speed[2:3])
        top = jnp.maximum(top, speed[4:5] + speed[5:6] + speed[6:7])
    send = top if out_ref.shape[1] == 1 else jnp.where(row == 3, top, vel_ref[core, 0])
    out_ref[...] = jnp.broadcast_to(send[None], out_ref.shape)


def pack_kernel(seg_ref, drag_ref, send_ref, part_ref, raw_ref, out_ref):
    raw_ref[...] = jnp.zeros((24, SEG), F32)
    for block in range(2):
        for comp in range(3):
            raw_ref[4 * block + comp, :] = seg_ref[comp, block, :]
            raw_ref[8 + 4 * block + comp, :] = seg_ref[3 + comp, block, :]
        raw_ref[11 + 4 * block, :] = seg_ref[6, block, :]
        raw_ref[16 + 2 * block, :] = seg_ref[7, block, :]
        raw_ref[17 + 2 * block, :] = seg_ref[8, block, :]
        raw_ref[20 + block, :] = drag_ref[block, :]
    raw_ref[3, :] = send_ref[0, :].astype(F32)
    raw_ref[7, :] = part_ref[0, :].astype(F32)
    for at in range(5):
        rows = raw_ref[4 * at : 4 * at + 4, :]
        for peer in range(NZ):
            out_ref[peer, at] = rows


def fan_kernel(in_ref, out_ref, sems):
    copies = [
        pltpu.make_async_copy(in_ref, out_ref.at[peer], sems.at[peer]) for peer in range(NY)
    ]
    for copy in copies:
        copy.start()
    for copy in copies:
        copy.wait()


def last_kernel(codes_ref, top_ref, x_ref, vel_ref, pos_out, vel_out):
    core = codes_ref[6, 0]
    top = jnp.max(jnp.max(top_ref[...], axis=0), axis=1, keepdims=True)
    step = STEP_LENGTH / (jnp.sqrt(top) + EPSILON)
    velocity = vel_ref[core, 0]
    moved = x_ref[core, 0] + step * velocity
    for block in range(2):
        for comp in range(3):
            pos_out[comp, block, :] = moved[4 * block + comp]
            vel_out[comp, block, :] = velocity[4 * block + comp]


SMEM = pl.BlockSpec(memory_space=pltpu.SMEM)
VMEM = pl.BlockSpec(memory_space=pltpu.VMEM)


def shape(*dims, dtype=F32):
    return jax.ShapeDtypeStruct(dims, dtype)


def call(kernel, name, operands, outs, smem_in=0, smem_out=0, scratch=(), mib=4, cost=None):
    return pl.pallas_call(
        kernel,
        name=name,
        in_specs=[SMEM] * smem_in + [VMEM] * (len(operands) - smem_in),
        out_specs=[VMEM] * (len(outs) - smem_out) + [SMEM] * smem_out,
        out_shape=outs,
        scratch_shapes=scratch,
        compiler_params=pltpu.CompilerParams(vmem_limit_bytes=mib << 20),
        cost_estimate=cost,
    )(*operands)


def pass_x(value, shift):
    return lax.ppermute(value, "x", [(i, (i + shift) % NX) for i in range(NX)])


def exchange(value, axes):
    return lax.all_to_all(value, axes, 0, 0, tiled=True)


def local(segments, stress, drag_coef, send_ids, partner_ids):
    core = lax.axis_index("c")
    y_index = lax.axis_index("y")
    x_index = lax.axis_index("x")
    chip_index = y_index * NZ + lax.axis_index("z")
    raw, to_z = call(
        pack_kernel,
        "pack",
        (
            segments.transpose(1, 0, 2),
            drag_coef,
            send_ids.reshape(1, SEG),
            partner_ids.reshape(1, SEG),
        ),
        [shape(24, SEG), shape(NZ, 5, 4, SEG)],
        mib=56,
    )
    along_z = exchange(to_z, "z")
    group = [raw] + [pass_x(raw, shift) for shift in range(1, NX)]
    near = lax.all_gather(jnp.stack(group), "c", axis=0)
    chip = near[:, 0]

    lane = lax.broadcasted_iota(jnp.int32, (NC, SEG), 1)
    side = lax.broadcasted_iota(jnp.int32, (NC, SEG), 0)
    even = lax.bitwise_and(lane, SEG - 2)
    sent = chip[:, 3].astype(jnp.int32)
    other = chip[:, 7].astype(jnp.int32)
    out = jnp.where(sent >= 0, even + other + 256 * (2 * side + sent), -1)
    first = lane[0:1]
    where = jnp.where(first == 0, core, jnp.where(first == 1, y_index, x_index))
    where = jnp.where(first == 3, chip_index, where)
    zero = jnp.zeros((1, SEG), jnp.int32)
    known = jnp.concatenate([out, zero, zero, where, zero], axis=0)
    nothing = jnp.zeros((NC, SEG), jnp.int32)
    pick = (lane == 2 * chip_index + side).astype(F32)

    near_sent = along_z[:, 0, 3].astype(jnp.int32)
    near_part = along_z[:, 1, 3].astype(jnp.int32)
    z_row = lax.broadcasted_iota(jnp.int32, (NZ, SEG), 0)
    target = lax.bitwise_and(lax.broadcasted_iota(jnp.int32, (NZ, SEG), 1), 1)
    near_into = jnp.where(
        near_sent >= 0, 2 * z_row + near_sent + 256 * (2 * target + near_part), -1
    )
    along_z, near_into = lax.optimization_barrier((along_z, near_into))
    to_y = pl.pallas_call(
        fan_kernel,
        name="fan",
        in_specs=[VMEM],
        out_specs=pl.BlockSpec(memory_space=pl.ANY),
        out_shape=shape(NY, NZ * 5, 4, SEG),
        scratch_shapes=[pltpu.SemaphoreType.DMA((NY,))],
        compiler_params=pltpu.CompilerParams(vmem_limit_bytes=4 << 20),
    )(along_z.reshape(NZ * 5, 4, SEG))
    everyone = exchange(to_y, "y").reshape(NDEV, 5, 4, SEG)
    (near_force,) = call(
        near_kernel,
        "near_pairs",
        (jnp.concatenate([nothing, known], axis=0), near_into, along_z, near),
        [shape(NC, 8, SEG)],
        smem_in=2,
        scratch=[pltpu.SMEM((1, 128), jnp.int32)] + scratch_of(NZ),
        mib=8,
        cost=pl.CostEstimate(flops=1 << 30, bytes_accessed=1 << 24, transcendentals=1 << 20),
    )
    everyone, near_force = lax.optimization_barrier((everyone, near_force))
    lists = everyone[:, 0:2, 3].reshape(2 * NDEV, SEG)
    incoming = lax.dot_general(
        pick, lists, (((1,), (1,)), ((), ())), precision=lax.Precision.HIGHEST
    ).astype(jnp.int32)
    partner = jnp.concatenate([incoming[:, 1:], incoming[:, :1]], axis=1)
    into = jnp.where(incoming >= 0, even + incoming + 256 * (2 * side + partner), -1)
    codes = jnp.concatenate([into, known], axis=0)

    force, items, count = call(
        first_kernel,
        "first_pairs",
        (codes, everyone, near, near_force),
        [
            shape(NC, 8, SEG),
            shape(1, LIST, dtype=jnp.int32),
            shape(1, 2, dtype=jnp.int32),
        ],
        smem_in=1,
        smem_out=2,
        scratch=scratch_of(NDEV),
        mib=16,
    )
    def finish(force, position, peers, name):
        return call(
            finish_kernel,
            name,
            (codes, stress, exchange(jnp.broadcast_to(force[None], (8, *force.shape)), ("x", "c")), near, position),
            [shape(NC, NX, 8, SEG), shape(*peers, SEG)],
            smem_in=2,
        )

    near_vel, to_z = finish(force, near, (NZ, 8), "finish")
    along_z = exchange(to_z, "z").reshape(1, NZ * 8, SEG)
    vel_all = exchange(jnp.broadcast_to(along_z, (NY, NZ * 8, SEG)), "y").reshape(NDEV, 8, SEG)

    force, position = call(
        second_kernel,
        "second_pairs",
        (codes, items, count, everyone, near, vel_all, near_vel),
        [shape(NC, 8, SEG), shape(NC, NX, 8, SEG)],
        smem_in=3,
        scratch=scratch_of(NDEV),
        mib=16,
    )
    near_vel, to_all = finish(force, position, (NDEV, 1), "finish_last")
    tops = exchange(to_all, ("y", "z"))
    positions, velocity = call(
        last_kernel,
        "last",
        (codes, tops, position, near_vel),
        [shape(3, 2, SEG), shape(3, 2, SEG)],
        smem_in=1,
    )
    return positions.transpose(1, 0, 2), velocity.transpose(1, 0, 2)


def solution(mesh):
    split = Mesh(
        mesh.devices.reshape(NY, NZ, NC, mesh.shape["sub"]), ("y", "z", "c", "x")
    )
    return jax.shard_map(
        local,
        mesh=split,
        in_specs=(
            P(DOM_SUB, None, None),
            P(),
            P(DOM_SUB, None),
            P(DOM_SUB, None, None),
            P(DOM_SUB, None, None),
        ),
        out_specs=(P(DOM_SUB, None, None), P(DOM_SUB, None, None)),
        check_vma=False,
    )
```
